32 devices in a mesh: mx: 8 (over z, core), my: 4 (over y, x).
Axes of the slice: x: 2, y: 2, z: 4, core: 2. Of those that a mesh axis runs over, the one named last changes fastest.
Arguments:
- features: bfloat16 [1024, 32, 512], P(('mx', 'my')), may hold values from -6 to 6
- coords: int32 [3, 1024], P(None, ('mx', 'my')), may hold values from 0 to 31, as said below
- counts: int32 [32], P(('mx', 'my')), may hold values from 16 to 32, as said below
- neighbours: int32 [6, 1024], P(None, ('mx', 'my')), may hold values from -1 to 1023, as said below
- fine_weights: bfloat16 [3, 32, 224], replicated, may hold values from -0.375 to 0.375
- down_weight: bfloat16 [2048, 256], replicated, may hold values from -0.25 to 0.25
- up_weight: bfloat16 [256, 2048], replicated, may hold values from -0.375 to 0.375
- norm_gain: float32 [256], replicated, may hold values from 0.1 to 1.9
- norm_bias: float32 [256], replicated, may hold values from -3 to 3
- coarse_weight: bfloat16 [6912, 256], P(None, 'my'), may hold values from -0.078125 to 0.078125
Outputs:
- fine_out: bfloat16 [1024, 32, 512], P(('mx', 'my'))
- coarse_out: bfloat16 [16, 8, 2, 256], P('mx', 'my')
The draws below stay inside these ranges and needn't reach their ends.
Inputs may be any that keep to these rules, and one draw needn't show every extreme that they name: The live slots of a device are its first counts entries; some device is full in every draw. `coords`: the live blocks of the device with mx index i and my index j lie at z in [i * 4, (i + 1) * 4), y in [j * 4, (j + 1) * 4), x in [0, 4), distinct, in Morton order of their coordinates inside that region; slots that are not live hold 0. `neighbours`: A live block's entry is the slot of the live block one step away in that direction, or -1 if there is none; the relation is symmetric; slots that are not live hold -1.
All inputs are finite; a program needn't handle non-finite values.
Results may differ from the reference program's by a relative error of at most 0.0095.
Values may be sent and summed in bfloat16 or wider, within the bound.
A program may use at most 128 MiB of HBM per device.

```python
import jax
import jax.numpy as jnp
from jax import lax

C = 32
CC = 256
GROUPS = 32
SIDE = 8
RZ = 4
RY = 4
RX = 4
BLK_DEV = 32
SLOTS = 1024
N_MX = 8
N_MY = 4


def morton_code(local_z, local_y, local_x):
    morton = jnp.zeros_like(local_x)
    for bit_pos in range(8):
        morton = morton | (local_x >> bit_pos & 1) << 3 * bit_pos
        morton = morton | (local_y >> bit_pos & 1) << 3 * bit_pos + 1
        morton = morton | (local_z >> bit_pos & 1) << 3 * bit_pos + 2
    return morton


def geometry(key):
    device_total = N_MX * N_MY
    region = RZ * RY * RX
    folded = jax.random.fold_in(key, 11)
    count_key, full_key, choose_key = jax.random.split(folded, 3)
    counts = jax.random.randint(count_key, (device_total,), BLK_DEV // 2, BLK_DEV + 1, dtype=jnp.int32)
    fullest = jax.random.randint(full_key, (), 0, device_total, dtype=jnp.int32)
    device_ids = jnp.arange(device_total, dtype=jnp.int32)
    counts = jnp.where(device_ids == fullest, BLK_DEV, counts).astype(jnp.int32)
    cell_ids = jnp.arange(region, dtype=jnp.int32)
    local_z = cell_ids // (RY * RX)
    local_y = cell_ids // RX % RY
    local_x = cell_ids % RX
    morton = morton_code(local_z, local_y, local_x)

    def per_device(device_key, live_count):
        ranking = jax.random.permutation(device_key, region).astype(jnp.int32)
        chosen = ranking < live_count
        scores = jnp.where(chosen, morton, morton + (1 << 25))
        return jnp.argsort(scores)[:BLK_DEV].astype(jnp.int32)
    orderings = jax.vmap(per_device)(jax.random.split(choose_key, device_total), counts)
    is_live = jnp.arange(BLK_DEV, dtype=jnp.int32)[None, :] < counts[:, None]
    block_z = (device_ids // N_MY)[:, None] * RZ + local_z[orderings]
    block_y = (device_ids % N_MY)[:, None] * RY + local_y[orderings]
    block_x = local_x[orderings]
    block_z = jnp.where(is_live, block_z, 0).reshape(-1)
    block_y = jnp.where(is_live, block_y, 0).reshape(-1)
    block_x = jnp.where(is_live, block_x, 0).reshape(-1)
    is_live = is_live.reshape(-1)
    extent_z = RZ * N_MX
    extent_y = RY * N_MY
    grid_cells = extent_z * extent_y * RX
    linear = (block_z * extent_y + block_y) * RX + block_x
    slot_ids = jnp.arange(device_total * BLK_DEV, dtype=jnp.int32)
    lookup = jnp.full((grid_cells,), -1, jnp.int32).at[jnp.where(is_live, linear, grid_cells)].set(slot_ids, mode='drop')
    steps_list = ((0, 0, 1), (0, 0, -1), (0, 1, 0), (0, -1, 0), (1, 0, 0), (-1, 0, 0))
    link_rows = []
    for step_z, step_y, step_x in steps_list:
        near_z = block_z + step_z
        near_y = block_y + step_y
        near_x = block_x + step_x
        inside = (near_z >= 0) & (near_z < extent_z) & (near_y >= 0) & (near_y < extent_y) & (near_x >= 0) & (near_x < RX) & is_live
        near_linear = (near_z * extent_y + near_y) * RX + near_x
        link_rows.append(jnp.where(inside, lookup[jnp.clip(near_linear, 0, grid_cells - 1)], -1))
    neighbours = jnp.stack(link_rows).astype(jnp.int32)
    coords = jnp.stack([block_z, block_y, block_x]).astype(jnp.int32)
    return (counts, coords, neighbours)


def draw_counts(key, part):
    return geometry(key)[0]


def draw_coords(key, part):
    return geometry(key)[1]


def draw_neighbours(key, part):
    return geometry(key)[2]


def block_levels(rng, shape, cuts, low, top_value):
    def one(position, blocks):
        draws = jax.random.uniform(jax.random.fold_in(jax.random.fold_in(rng, 6), position), (blocks,), jnp.float32, low / len(cuts), top_value / len(cuts))
        return jnp.repeat(jnp.exp(draws), shape[position] // blocks).reshape((-1,) + (1,) * (len(shape) - position - 1))

    level = one(*cuts[0])
    for cut in cuts[1:]:
        level = level * one(*cut)
    return level


def normal_values(own_key, shape, width, most, cuts=(), kind=jnp.bfloat16):
    array = width * jax.random.normal(own_key, shape, jnp.float32)
    if cuts:
        array = array * block_levels(own_key, shape, cuts, -0.22, 0.18)
    return jnp.clip(array, -most, most).astype(kind)


def setup_inputs(seed: int = 0) -> dict:
    splits = jax.random.split(jax.random.key(seed), 11)
    return {
        "features": normal_values(splits[0], (SLOTS, C, SIDE * SIDE * SIDE), 1.0, 6.0, ((0, 32),)),
        "coords": draw_coords(jax.random.fold_in(splits[10], 71), 0),
        "counts": draw_counts(jax.random.fold_in(splits[10], 71), 0),
        "neighbours": draw_neighbours(jax.random.fold_in(splits[10], 71), 0),
        "fine_weights": normal_values(splits[4], (3, C, 7 * C), (7 * C) ** -0.5, 0.375),
        "down_weight": normal_values(splits[5], (64 * C, CC), (16 * C) ** -0.5, 0.25),
        "up_weight": normal_values(splits[6], (CC, 64 * C), CC ** -0.5, 0.375),
        "norm_gain": jnp.clip(1.0 + 0.18 * jax.random.normal(splits[7], (CC,), jnp.float32), 0.1, 1.9),
        "norm_bias": normal_values(splits[8], (CC,), 0.5, 3.0, (), jnp.float32),
        "coarse_weight": normal_values(splits[9], (27 * CC, CC), (27 * CC) ** -0.5, 0.078125, ((1, 4),)),
    }


def displaced_taps(signal, near_blocks, block_side):
    volume = block_side * block_side * block_side
    voxel_ids = jnp.arange(volume, dtype=jnp.int32)
    along_x = voxel_ids % block_side
    along_y = voxel_ids // block_side % block_side
    along_z = voxel_ids // (block_side * block_side)
    last_layer = block_side - 1
    square = block_side * block_side
    plans = ((along_x < last_layer, -1, last_layer), (along_x > 0, 1, -last_layer), (along_y < last_layer, -block_side, block_side * last_layer), (along_y > 0, block_side, -block_side * last_layer), (along_z < last_layer, -square, square * last_layer), (along_z > 0, square, -square * last_layer))
    tap_list = [signal]
    for (inside, own_shift, near_shift), block in zip(plans, near_blocks):
        tap_list.append(jnp.where(inside, jnp.roll(signal, own_shift, axis=2), jnp.roll(block, near_shift, axis=2)))
    tap_stack = jnp.stack(tap_list, axis=1)
    return tap_stack.reshape(signal.shape[0], 7 * signal.shape[1], volume)

def coarse_patches(padded, depth, height, breadth):
    channel_count = padded.shape[3]
    pieces = []
    for step_z in range(3):
        for step_y in range(3):
            for step_x in range(3):
                pieces.append(padded[step_z:step_z + depth, step_y:step_y + height, step_x:step_x + breadth])
    return jnp.stack(pieces, axis=3).reshape(depth * height * breadth, 27 * channel_count)

def residual_step(base, neighbours, kernel_weight):
    signal = jax.nn.silu(base.astype(jnp.float32)).astype(jnp.bfloat16)
    device_total = N_MX * N_MY
    slot_total, chans, volume = base.shape
    block_count = slot_total // device_total

    def per_device(device_id):
        first_row = device_id * block_count
        own_rows = lax.dynamic_slice_in_dim(signal, first_row, block_count, 0)
        kept_rows = lax.dynamic_slice_in_dim(base, first_row, block_count, 0)
        link_rows = lax.dynamic_slice_in_dim(neighbours, first_row, block_count, 1)
        near_blocks = []
        for direction in range(6):
            present = link_rows[direction] >= 0
            picked = signal[jnp.clip(link_rows[direction], 0, slot_total - 1)]
            near_blocks.append(jnp.where(present[:, None, None], picked, jnp.zeros_like(picked)))
        tap_stack = displaced_taps(own_rows, near_blocks, SIDE)
        convolution_result = jnp.einsum('pn,enh->eph', kernel_weight.astype(jnp.float32), tap_stack.astype(jnp.float32))
        return (kept_rows.astype(jnp.float32) + convolution_result).astype(jnp.bfloat16)
    result = lax.map(per_device, jnp.arange(device_total, dtype=jnp.int32))
    return result.reshape(slot_total, chans, volume)

def reference(features, coords, counts, neighbours, fine_weights, down_weight, up_weight, norm_gain, norm_bias, coarse_weight):
    device_total = N_MX * N_MY
    slot_total, chans, volume = features.shape
    block_count = slot_total // device_total
    slot_ids = jnp.arange(slot_total, dtype=jnp.int32)
    is_live = slot_ids % block_count < counts[slot_ids // block_count]
    first_level = residual_step(features, neighbours, fine_weights[0])
    half_side = SIDE // 2
    pooled = lax.optimization_barrier(jnp.mean(first_level.reshape(slot_total, chans, 2, half_side, 2, half_side, 2, half_side), axis=(3, 5, 7), dtype=jnp.float32))
    pooled = pooled.transpose(0, 2, 3, 4, 1).reshape(slot_total, 8 * chans).astype(jnp.bfloat16)
    grid_z = RZ // 2 * N_MX
    grid_y = RY // 2 * N_MY
    grid_x = RX // 2
    cell_count = grid_z * grid_y * grid_x
    block_z = coords[0]
    block_y = coords[1]
    block_x = coords[2]
    cell_ids = (block_z // 2 * grid_y + block_y // 2) * grid_x + block_x // 2
    octant_pos = block_z % 2 * 4 + block_y % 2 * 2 + block_x % 2
    target = jnp.where(is_live, cell_ids * 8 + octant_pos, cell_count * 8).astype(jnp.int32)
    gathered = jnp.zeros((cell_count * 8, 8 * chans), jnp.bfloat16).at[target].set(pooled, mode='drop')
    coarse_in = jnp.dot(gathered.reshape(cell_count, 64 * chans), down_weight, preferred_element_type=jnp.float32)
    coarse_width = coarse_in.shape[1]
    grouped = coarse_in.reshape(cell_count, GROUPS, coarse_width // GROUPS)
    group_mean = lax.optimization_barrier(jnp.mean(grouped, axis=(0, 2)))
    centred = grouped - group_mean[None, :, None]
    variance = lax.optimization_barrier(jnp.mean(centred * centred, axis=(0, 2)))
    normed = (centred / jnp.sqrt(variance + 1e-05)[None, :, None]).reshape(cell_count, coarse_width) * norm_gain + norm_bias
    activated = jax.nn.silu(normed).astype(jnp.bfloat16).reshape(grid_z, grid_y, grid_x, coarse_width)
    padded = jnp.pad(activated, ((1, 1), (1, 1), (1, 1), (0, 0)))
    convolution_result = jnp.dot(coarse_patches(padded, grid_z, grid_y, grid_x), coarse_weight, preferred_element_type=jnp.float32)
    coarse_out = (convolution_result + coarse_in).astype(jnp.bfloat16)
    lifted = jnp.dot(coarse_out, up_weight, preferred_element_type=jnp.float32).reshape(cell_count * 8, 8 * chans)
    per_block = lifted[jnp.clip(target, 0, cell_count * 8 - 1)]
    per_block = jnp.where(is_live[:, None], per_block, jnp.zeros_like(per_block))

    def join_device(device_id):
        first_row = device_id * block_count
        level_row_list = lax.dynamic_slice_in_dim(first_level, first_row, block_count, 0)
        lift_rows = lax.dynamic_slice_in_dim(per_block, first_row, block_count, 0)
        spread_up = lift_rows.reshape(block_count, 2, 2, 2, chans).transpose(0, 4, 1, 2, 3)
        spread_up = jnp.broadcast_to(spread_up[:, :, :, None, :, None, :, None], (block_count, chans, 2, half_side, 2, half_side, 2, half_side))
        return (level_row_list.astype(jnp.float32) + spread_up.reshape(block_count, chans, volume)).astype(jnp.bfloat16)
    merged_features = lax.map(join_device, jnp.arange(device_total, dtype=jnp.int32)).reshape(slot_total, chans, volume)
    second_level = residual_step(merged_features, neighbours, fine_weights[1])
    final_level = residual_step(second_level, neighbours, fine_weights[2])
    fine_out = jnp.where(is_live[:, None, None], final_level, jnp.zeros_like(final_level))
    return (fine_out, coarse_out.reshape(grid_z, grid_y, grid_x, coarse_width))
```

```python
import functools

import jax
import jax.numpy as jnp
import numpy as np
from jax import lax
from jax.experimental import pallas as pl
from jax.experimental.pallas import tpu as pltpu
from jax.sharding import PartitionSpec as P

GROUPS = 32
SIDE = 8
RZ = 4
RY = 4
RX = 4
HALF = SIDE // 2
CUBES = HALF**3
PLANE = HALF**2
FACE = 16
norm_eps = 1e-05
MESH = pl.DeviceIdType.MESH
BF = jnp.bfloat16
F32 = jnp.float32
I32 = jnp.int32
VM = pl.BlockSpec(memory_space=pltpu.VMEM)
SM = pl.BlockSpec(memory_space=pltpu.SMEM)
NN = (((1,), (0,)), ((), ()))
NT = (((1,), (1,)), ((), ()))
TN = (((0,), (0,)), ((), ()))


def constants(chans):
    lane = np.arange(4 * chans)
    masks = np.stack([lane < 2 * chans, lane // chans % 2 == 0])
    masks = np.broadcast_to(masks[:, None, :], (2, 32, 4 * chans))
    sel = np.zeros((256, 256))
    for w in range(8):
        vy, vz, vx = w >> 2, w >> 1 & 1, w & 1
        for i in range(32):
            z, y, x = i // 16 * 2 + vz, i // 4 % 4 * 2 + vy, i % 4 * 2 + vx
            sel[w * 32 + i, (z * SIDE + y) * SIDE + x] = 1
    swap = np.zeros((256, 256))
    for i in range(16):
        for s in range(16):
            swap[i * 16 + s, s * 16 + i] = 1
    wide = np.arange(8 * chans)
    same = wide[:, None] % chans == wide[None, :] % chans
    as_bf = lambda a: jnp.asarray(np.asarray(a, np.float32), BF)
    return as_bf(masks), as_bf(sel), as_bf(swap), as_bf(same)


def dot(a, b, dims=NN):
    return lax.dot_general(a, b, dims, preferred_element_type=F32)


def silu(x):
    h = 0.5 * x
    return h * jnp.tanh(h) + h


def swap_blocks(parts, low64, low32):
    left, right = [p[0] for p in parts], [p[1] for p in parts]
    m = [(left[i], left[i + 4]) for i in range(4)] + [(right[i], right[i + 4]) for i in range(4)]
    for bit, low, up, down in ((2, low64, 64, 64), (1, low32, 32, 96)):
        n = list(m)
        for j in range(8):
            if j & bit:
                continue
            a, b = m[j], m[j | bit]
            n[j] = tuple(jnp.where(low, a[t], pltpu.roll(b[t], up, 1)) for t in range(2))
            n[j | bit] = tuple(jnp.where(low, pltpu.roll(a[t], down, 1), b[t]) for t in range(2))
        m = n
    return m


def level_kernel(
    slots, chans, cells,
    counts, coords, neighbours,
    feat, fine_w, gain, bias, sel, swap, same, masks,
    down_h, up_h, weight_h,
    fine, coarse_out,
    down, up, weight,
    blocks, base, sig, sig2, acc, wts, gx, gyp, gym, gz, faces, halo, term,
    coarse, stats, window, everyone, pad, part, result,
    load, fsend, frecv, ssend, srecv, wsend, wrecv, rsend, rrecv,
):
    n_mx, n_my = lax.axis_size("mx"), lax.axis_size("my")
    mx, my = lax.axis_index("mx"), lax.axis_index("my")
    n = n_mx * n_my
    me = mx * n_my + my
    width = 8 * chans
    side = width // 2
    wide_c = gain.shape[1]

    loads = [
        pltpu.make_async_copy(a, b, load.at[i])
        for i, (a, b) in enumerate(((down_h, down), (weight_h, weight), (up_h, up)))
    ]
    for c in loads:
        c.start()

    barrier = pltpu.get_barrier_semaphore()

    def where_is(d):
        t = lax.rem(me + d, n)
        return (t // n_my, lax.rem(t, n_my))

    def greet(d, c):
        pl.semaphore_signal(barrier, inc=1, device_id=where_is(d), device_id_type=MESH)
        return c

    lax.fori_loop(1, n, greet, 0)

    def rows(ref, q):
        return ref[q * slots : (q + 1) * slots, :]

    def left(ref, q):
        return ref[q * slots : (q + 1) * slots, :side]

    def right(ref, q):
        return ref[q * slots : (q + 1) * slots, side:]

    low64, low32 = masks[0] > 0.5, masks[1] > 0.5
    zero = jnp.zeros((slots, side), BF)

    for g in range(slots // 8):
        for h in range(2):
            x = feat[8 * g : 8 * g + 8, :, 256 * h : 256 * h + 256].reshape(8 * chans, 256)
            r = dot(sel[...], x, NT).astype(BF)
            m = [(r[32 * w : 32 * w + 32, :side], r[32 * w : 32 * w + 32, side:]) for w in range(8)]
            m = swap_blocks(m, low64, low32)
            for s in range(8):
                at = (8 * g + s) * CUBES + 32 * h
                blocks[at : at + 32, :side] = m[s][0]
                blocks[at : at + 32, side:] = m[s][1]
    for z in range(HALF):
        for g in range(slots // 16):
            x = jnp.concatenate(
                [blocks[(16 * g + s) * CUBES + 16 * z : (16 * g + s) * CUBES + 16 * z + 16, :]
                 for s in range(16)], axis=0)
            r = dot(swap[...], x)
            rb = r.astype(BF)
            rs = silu(r).astype(BF)
            for i in range(16):
                at = (16 * z + i) * slots + 16 * g
                base[at : at + 16, :] = rb[16 * i : 16 * i + 16]
                sig[at : at + 16, :] = rs[16 * i : 16 * i + 16]

    def one_hot(row, count):
        return (lax.broadcasted_iota(I32, (count, slots), 0) == row).astype(F32).astype(BF)

    eye = (
        lax.broadcasted_iota(I32, (slots, slots), 0) == lax.broadcasted_iota(I32, (slots, slots), 1)
    ).astype(F32).astype(BF)

    def turned(table):
        return dot(eye, table, NT).astype(BF)

    pz = coords[0:1, :] - mx * RZ
    py = coords[1:2, :] - my * RY
    px = coords[2:3, :]
    live = lax.broadcasted_iota(I32, (1, slots), 1) < counts[0]

    def link(d):
        g = neighbours[d : d + 1, :]
        here = g - me * slots
        inside = (here >= 0) & (here < slots)
        far = slots + (pz if d < 4 else py) * RX + px
        return jnp.where(g < 0, -1, jnp.where(inside, here, far))

    halo_rows = slots + FACE
    g_x = turned(jnp.concatenate([one_hot(link(d), slots) for d in (0, 1)], axis=0))
    g_yp = turned(one_hot(link(2), halo_rows))
    g_ym = turned(one_hot(link(3), halo_rows))
    g_z = turned(jnp.concatenate([one_hot(link(d), halo_rows) for d in (4, 5)], axis=0))
    edge = (
        jnp.where(live & (py == 0), pz * RX + px, -1),
        jnp.where(live & (py == RY - 1), pz * RX + px, -1),
        jnp.where(live & (pz == 0), py * RX + px, -1),
        jnp.where(live & (pz == RZ - 1), py * RX + px, -1),
    )
    g_edge = [one_hot(e, FACE) for e in edge]
    cell = (pz // 2 * 2 + px // 2) * 2 + py // 2
    place = pz % 2 * 4 + py % 2 * 2 + px % 2
    g_cell = one_hot(jnp.where(live, place * cells + cell, -1), 8 * cells)
    g_lift = turned(g_cell)
    alive = dot(
        jnp.where(live, eye.astype(F32), 0.0).astype(BF), jnp.ones((slots, width), BF)
    ) > 0.5

    peers = (
        (my > 0, mx, my - 1),
        (my < n_my - 1, mx, my + 1),
        (mx > 0, mx - 1, my),
        (mx < n_mx - 1, mx + 1, my),
    )

    def face_copy(r, f):
        _, a, b = peers[f]
        return pltpu.make_async_remote_copy(
            src_ref=faces.at[r, f], dst_ref=halo.at[r, f], send_sem=fsend.at[r, f],
            recv_sem=frecv.at[r, f], device_id=(a, b), device_id_type=MESH,
        )

    low64_face = low64[:FACE]

    def send_face(r, src, f):
        for k in range(PLANE // 2):
            a, x = k // 2, k % 2 * 2
            if f < 2:
                part_of = left if f == 0 else right
                q = a * PLANE + (0 if f == 0 else HALF - 1) * HALF + x
                pair = jnp.concatenate([part_of(src, q), part_of(src, q + 1)], axis=1)
                v = dot(g_edge[f], pair).astype(BF)
                faces[r, f, 2 * k] = v[:, :side]
                faces[r, f, 2 * k + 1] = v[:, side:]
            else:
                q = (0 if f == 2 else HALF - 1) * PLANE + a * HALF + x
                va = dot(g_edge[f], rows(src, q)).astype(BF)
                vb = dot(g_edge[f], rows(src, q + 1)).astype(BF)
                for t in range(2):
                    own = va[:, t * side : (t + 1) * side]
                    other = pltpu.roll(vb[:, t * side : (t + 1) * side], 64, 1)
                    if f == 2:
                        faces[r, f, 2 * k + t] = jnp.where(low64_face, own, other)
                    else:
                        faces[r, f, 2 * k + t] = jnp.where(low64_face, other, own)

        @pl.when(peers[f][0])
        def _():
            face_copy(r, f).start()

        @pl.when(jnp.logical_not(peers[f ^ 1][0]))
        def _():
            halo[r, f] = jnp.zeros_like(halo[r, f])

    def take_face(r, f):
        @pl.when(peers[f][0])
        def _():
            face_copy(r, f).wait_send()

        @pl.when(peers[f ^ 1][0])
        def _():
            face_copy(r, f).wait_recv()

    def z_halo(r, f, y, x):
        k = 2 * (y * 2 + x // 2)
        v = [halo[r, f, k + t] for t in range(2)]
        if x % 2:
            v = [pltpu.roll(a, 64, 1) for a in v]
        none = jnp.zeros_like(v[0])
        if f == 2:
            v = [jnp.where(low64_face, a, none) for a in v]
        else:
            v = [jnp.where(low64_face, none, a) for a in v]
        return jnp.concatenate(v, axis=1)

    def both(low, a, b):
        return jnp.concatenate([jnp.where(low, a[t], b[t]) for t in range(2)], axis=1)

    def halves(ref, q):
        return left(ref, q), right(ref, q)

    block = 8

    def near(r, src):
        for zy in range(PLANE):
            first, last = halves(src, zy * HALF), halves(src, zy * HALF + HALF - 1)
            pair = jnp.concatenate(
                [both(low32, first, (zero, zero)), both(low32, (zero, zero), last)], axis=0
            )
            gx[zy * slots : (zy + 1) * slots, :] = dot(g_x, pair).astype(BF)
        for b in range(CUBES // block):
            taps = []
            for q in range(b * block, (b + 1) * block):
                edge_of = halves(gx, q // HALF)
                after = halves(src, q + 1) if q % HALF < HALF - 1 else edge_of
                before = halves(src, q - 1) if q % HALF > 0 else edge_of
                taps.append(both(low32, after, before))
            span = slice(b * block * slots, (b + 1) * block * slots)
            acc[span, :] = base[span, :].astype(F32) + (
                dot(src[span, :], wts[r, 0]) + dot(jnp.concatenate(taps, axis=0), wts[r, 1])
            )

    def far(r, src, finish):
        for f in range(4):
            take_face(r, f)
        for k in range(PLANE // 2):
            z, x = k // 2, k % 2 * 2
            for f, part_of, table, out in ((0, left, g_yp, gyp), (1, right, g_ym, gym)):
                q = z * PLANE + (0 if f == 0 else HALF - 1) * HALF + x
                own = jnp.concatenate([part_of(src, q), part_of(src, q + 1)], axis=1)
                got = jnp.concatenate([halo[r, f, 2 * k], halo[r, f, 2 * k + 1]], axis=1)
                v = dot(table, jnp.concatenate([own, got], axis=0)).astype(BF)
                out[2 * k * slots : (2 * k + 1) * slots, :] = v[:, :side]
                out[(2 * k + 1) * slots : (2 * k + 2) * slots, :] = v[:, side:]
        for y in range(HALF):
            for x in range(HALF):
                i = y * HALF + x
                first, last = halves(src, i), halves(src, (HALF - 1) * PLANE + i)
                stack = jnp.concatenate(
                    [both(low64, first, (zero, zero)), z_halo(r, 2, y, x),
                     both(low64, (zero, zero), last), z_halo(r, 3, y, x)], axis=0,
                )
                gz[i * slots : (i + 1) * slots, :] = dot(g_z, stack).astype(BF)
        for b in range(CUBES // block):
            y_taps, z_taps = [], []
            for q in range(b * block, (b + 1) * block):
                z, y, x = q // PLANE, q // HALF % HALF, q % HALF
                zx = z * HALF + x
                span = slice(zx * slots, (zx + 1) * slots)
                after = left(src, q + HALF) if y < HALF - 1 else gyp[span, :]
                before = right(src, q - HALF) if y > 0 else gym[span, :]
                y_taps.append(jnp.concatenate([after, before], axis=1))
                edge_of = halves(gz, y * HALF + x)
                after = halves(src, q + PLANE) if z < HALF - 1 else edge_of
                before = halves(src, q - PLANE) if z > 0 else edge_of
                z_taps.append(both(low64, after, before))
            span = slice(b * block * slots, (b + 1) * block * slots)
            finish(span, acc[span, :] + (
                dot(jnp.concatenate(y_taps, axis=0), wts[r, 2])
                + dot(jnp.concatenate(z_taps, axis=0), wts[r, 3])
            ))

    lane_block = lax.broadcasted_iota(I32, (slots, width), 1) // chans
    block_f = lane_block.astype(F32).astype(BF)
    spread = (
        lax.broadcasted_iota(I32, (chans, width), 0)
        == lax.broadcasted_iota(I32, (chans, width), 1) % chans
    ).astype(F32).astype(BF)
    none = jnp.zeros((chans, width), BF)
    is_block = [block_f == float(w) for w in range(8)]

    def fill(r):
        t = dot(fine_w[r], spread, TN).astype(BF)
        t = [t[i * chans : (i + 1) * chans] for i in range(7)]
        for w in range(8):
            span = slice(w * chans, (w + 1) * chans)
            vy, vz, vx = w >> 2, w >> 1 & 1, w & 1
            v = jnp.where(is_block[w], t[0], none)
            v = jnp.where(is_block[w ^ 1], t[1] if vx else t[2], v)
            v = jnp.where(is_block[w ^ 4], t[3] if vy else t[4], v)
            v = jnp.where(is_block[w ^ 2], t[5] if vz else t[6], v)
            wts[r, 0, span, :] = v
            wts[r, 1, span, :] = jnp.where(is_block[w ^ 1], t[2] if vx else t[1], none)
            wts[r, 2, span, :] = jnp.where(is_block[w ^ 4], t[4] if vy else t[3], none)
            wts[r, 3, span, :] = jnp.where(is_block[w ^ 2], t[6] if vz else t[5], none)

    pl.semaphore_wait(barrier, n - 1)
    for f in range(4):
        send_face(0, sig, f)
    for r in range(3):
        fill(r)
    near(0, sig)

    def first_done(span, value):
        base[span, :] = value.astype(BF)

    far(0, sig, first_done)

    sums = []
    for o in range(8):
        total = None
        for i in range(8):
            z, y, x = (o >> 2) * 2 + (i >> 2), (o >> 1 & 1) * 2 + (i >> 1 & 1), (o & 1) * 2 + (i & 1)
            v = rows(base, (z * HALF + y) * HALF + x).astype(F32)
            total = v if i == 0 else total + v
        hi = total.astype(BF)
        sums += [hi, (total - hi.astype(F32)).astype(BF)]
    sums = dot(jnp.concatenate(sums, axis=0), same[...])
    pooled = jnp.zeros((slots, width), F32)
    for o in range(8):
        v = sums[2 * o * slots : (2 * o + 1) * slots] + sums[(2 * o + 1) * slots : (2 * o + 2) * slots]
        pooled = jnp.where(lane_block == o, v, pooled)
    pooled = (pooled * (1.0 / HALF**3)).astype(BF)
    flat = dot(g_cell, pooled).astype(BF)
    loads[0].wait()
    ci = jnp.zeros((cells, wide_c), F32)
    for p in range(8):
        ci = ci + jnp.dot(
            flat[p * cells : (p + 1) * cells],
            down[p * width : (p + 1) * width, :],
            preferred_element_type=F32,
        )
    layer = cells // 2
    coarse[0] = ci[:layer]
    coarse[1] = ci[layer:]
    stats[0:1, :] = jnp.sum(ci, axis=0, keepdims=True)
    stats[1:2, :] = jnp.sum(ci * ci, axis=0, keepdims=True)

    def stat_copy(d):
        return pltpu.make_async_remote_copy(
            src_ref=stats, dst_ref=everyone.at[me], send_sem=ssend.at[d], recv_sem=srecv.at[d],
            device_id=where_is(d), device_id_type=MESH,
        )

    def stat_go(d, c):
        stat_copy(d).start()
        return c

    def stat_wait(d, c):
        stat_copy(d).wait()
        return c

    def win_copy(kind, d):
        t = lax.rem(my + d, n_my)
        if kind == 0:
            src, dst, a = coarse, window.at[my, pl.ds(1, 2)], mx
        elif kind == 1:
            src, dst, a = coarse.at[pl.ds(0, 1)], window.at[my, pl.ds(3, 1)], mx - 1
        else:
            src, dst, a = coarse.at[pl.ds(1, 1)], window.at[my, pl.ds(0, 1)], mx + 1
        return pltpu.make_async_remote_copy(
            src_ref=src, dst_ref=dst, send_sem=wsend.at[kind, d], recv_sem=wrecv.at[kind, d],
            device_id=(a, t), device_id_type=MESH,
        )

    lax.fori_loop(1, n, stat_go, 0)
    low, high = mx > 0, mx < n_mx - 1
    for d in range(n_my):
        if d:
            win_copy(0, d).start()

        @pl.when(low)
        def _():
            win_copy(1, d).start()

        @pl.when(high)
        def _():
            win_copy(2, d).start()
    window[my, 1:3] = coarse[...]
    everyone[me] = stats[...]

    @pl.when(jnp.logical_not(low))
    def _():
        for j in range(n_my):
            window[j, 0] = jnp.zeros_like(window[j, 0])

    @pl.when(jnp.logical_not(high))
    def _():
        for j in range(n_my):
            window[j, 3] = jnp.zeros_like(window[j, 3])

    pad[...] = jnp.zeros_like(pad)
    group = wide_c // GROUPS
    pooling = (
        lax.broadcasted_iota(jnp.int32, (wide_c, wide_c), 0) // group
        == lax.broadcasted_iota(jnp.int32, (wide_c, wide_c), 1) // group
    ).astype(F32)
    for c in loads[1:]:
        c.wait()
    for d in range(n_my):
        if d:
            win_copy(0, d).wait()

        @pl.when(low)
        def _():
            win_copy(1, d).wait_send()
            win_copy(2, d).wait_recv()

        @pl.when(high)
        def _():
            win_copy(2, d).wait_send()
            win_copy(1, d).wait_recv()
    lax.fori_loop(1, n, stat_wait, 0)

    total = float(cells * group) * n
    sums = jnp.sum(everyone[...], axis=0)
    sums = jnp.concatenate([sums, jnp.zeros((6, wide_c), F32)], axis=0)
    sums = jnp.dot(sums, pooling, precision=lax.Precision.HIGHEST, preferred_element_type=F32) / total
    mean = sums[0:1]
    std = jnp.sqrt(sums[1:2] - mean * mean + norm_eps)
    g = gain[...]
    b = bias[...]
    for zw in range(4):
        for j in range(n_my):
            value = silu((window[j, zw] - mean) / std * g + b)
            if zw == 0:
                value = jnp.where(low, value, 0.0)
            if zw == 3:
                value = jnp.where(high, value, 0.0)
            for x in range(2):
                pad[1 + x, zw, 1 + 2 * j : 3 + 2 * j, :] = value[2 * x : 2 * x + 2]
    tall = 2 * n_my
    sums = jnp.zeros((4 * tall, part.shape[2]), F32)
    t = 0
    for dz in range(3):
        for dy in range(3):
            for dx in range(3):
                lhs = jnp.concatenate(
                    [pad[x + dx, z + dz, dy : dy + tall, :] for z in range(2) for x in range(2)],
                    axis=0,
                ).astype(BF)
                sums = sums + lax.dot_general(
                    lhs, weight[:, t * wide_c : (t + 1) * wide_c], (((1,), (1,)), ((), ())),
                    preferred_element_type=F32,
                )
                t += 1
    for j in range(n_my):
        for zx in range(4):
            part[j, 2 * zx : 2 * zx + 2, :] = sums[zx * tall + 2 * j : zx * tall + 2 * j + 2, :]
    copies = []
    for d in range(1, n_my):
        to = lax.rem(my + d, n_my)
        copies.append(
            pltpu.make_async_remote_copy(
                src_ref=part.at[to], dst_ref=result.at[my], send_sem=rsend.at[d],
                recv_sem=rrecv.at[d], device_id=(mx, to), device_id_type=MESH,
            )
        )
    for c in copies:
        c.start()
    result[my] = part[my]
    for c in copies:
        c.wait()

    whole = jnp.concatenate([result[j] for j in range(n_my)], axis=1)
    co = (whole + jnp.concatenate([coarse[0], coarse[1]], axis=0)).astype(BF)
    cof = co.astype(F32)
    for z in range(2):
        for y in range(2):
            q = z * 4 + y
            pair = jnp.concatenate([cof[q : q + 1], cof[q + 2 : q + 3]], axis=0)
            coarse_out[z, y] = pair.astype(BF)
    wide = jnp.dot(co, up[...], preferred_element_type=F32)
    lifted = jnp.concatenate([wide[:, p * width : (p + 1) * width] for p in range(8)], axis=0)
    hi = lifted.astype(BF)
    lo = (lifted - hi.astype(F32)).astype(BF)
    picked = [dot(g_lift, v).astype(BF) for v in (hi, lo)]
    spots = [jnp.where(is_block[o], v, jnp.zeros_like(v)) for o in range(8) for v in picked]
    sums = dot(jnp.concatenate(spots, axis=0), same[...])
    for o in range(8):
        v = sums[2 * o * slots : (2 * o + 1) * slots] + sums[(2 * o + 1) * slots : (2 * o + 2) * slots]
        term[o * slots : (o + 1) * slots, :] = v

    for q in range(CUBES):
        z, y, x = q // PLANE, q // HALF % HALF, q % HALF
        o = z // 2 * 4 + y // 2 * 2 + x // 2
        span = slice(q * slots, (q + 1) * slots)
        f = (base[span, :].astype(F32) + term[o * slots : (o + 1) * slots, :]).astype(BF)
        base[span, :] = f
        sig[span, :] = silu(f.astype(F32)).astype(BF)
    for f in range(4):
        send_face(1, sig, f)

    def second_done(span, value):
        f = value.astype(BF)
        base[span, :] = f
        sig2[span, :] = silu(f.astype(F32)).astype(BF)

    near(1, sig)
    far(1, sig, second_done)
    for f in range(4):
        send_face(2, sig2, f)

    def last_done(span, value):
        for i in range(block):
            at = slice(i * slots, (i + 1) * slots)
            fine[span.start + at.start : span.start + at.stop, :] = jnp.where(
                alive, value[at], 0.0
            ).astype(BF)

    near(2, sig2)
    far(2, sig2, last_done)


def unfold_kernel(slots, chans, rows, coarse, sel, swap, masks, fine, coarse_out, blocks):
    width = 8 * chans
    side = width // 2
    low64, low32 = masks[0] > 0.5, masks[1] > 0.5
    for z in range(HALF):
        for g in range(slots // 16):
            x = jnp.concatenate(
                [rows[(16 * z + i) * slots + 16 * g : (16 * z + i) * slots + 16 * g + 16, :]
                 for i in range(16)], axis=0)
            r = dot(swap[...], x).astype(BF)
            for s in range(16):
                at = (16 * g + s) * CUBES + 16 * z
                blocks[at : at + 16, :] = r[16 * s : 16 * s + 16]
    for g in range(slots // 8):
        for h in range(2):
            m = []
            for s in range(8):
                at = (8 * g + s) * CUBES + 32 * h
                m.append((blocks[at : at + 32, :side], blocks[at : at + 32, side:]))
            m = swap_blocks(m, low64, low32)
            x = jnp.concatenate([jnp.concatenate(p, axis=1) for p in m], axis=0)
            r = dot(x.T, sel[...]).astype(BF)
            fine[8 * g : 8 * g + 8, :, 256 * h : 256 * h + 256] = r.reshape(8, chans, 256)
    coarse_out[...] = coarse[...]


def local(
    features, coords, counts, neighbours, fine_weights, down_weight, up_weight, norm_gain,
    norm_bias, coarse_weight,
):
    slots, chans, _ = features.shape
    n_mx, n_my = lax.axis_size("mx"), lax.axis_size("my")
    cells = (RZ // 2) * (RY // 2) * (RX // 2)
    width = down_weight.shape[1]
    lanes = 8 * chans
    masks, sel, swap, same = constants(chans)
    n = n_mx * n_my
    sds = jax.ShapeDtypeStruct
    weight_t = coarse_weight.T
    held = [pltpu.VMEM(a.shape, a.dtype) for a in (down_weight, up_weight, weight_t)]
    dma = pltpu.SemaphoreType.DMA
    total = slots * CUBES
    plane = slots * PLANE
    scratch = held + [
        pltpu.VMEM((total, lanes), BF),
        pltpu.VMEM((total, lanes), BF),
        pltpu.VMEM((total, lanes), BF),
        pltpu.VMEM((total, lanes), BF),
        pltpu.VMEM((total, lanes), F32),
        pltpu.VMEM((3, 4, lanes, lanes), BF),
        pltpu.VMEM((plane, lanes), BF),
        pltpu.VMEM((plane, lanes // 2), BF),
        pltpu.VMEM((plane, lanes // 2), BF),
        pltpu.VMEM((plane, lanes), BF),
        pltpu.VMEM((3, 4, PLANE, FACE, lanes // 2), BF),
        pltpu.VMEM((3, 4, PLANE, FACE, lanes // 2), BF),
        pltpu.VMEM((8 * slots, lanes), F32),
        pltpu.VMEM((2, cells // 2, width), F32),
        pltpu.VMEM((2, width), F32),
        pltpu.VMEM((n_my, 4, cells // 2, width), F32),
        pltpu.VMEM((n, 2, width), F32),
        pltpu.VMEM((4, 4, -(-(2 * n_my + 2) // 8) * 8, width), F32),
        pltpu.VMEM((n_my, cells, coarse_weight.shape[1]), F32),
        pltpu.VMEM((n_my, cells, coarse_weight.shape[1]), F32),
        dma((3,)), dma((3, 4)), dma((3, 4)), dma((n,)), dma((n,)),
        dma((3, n_my)), dma((3, n_my)), dma((n_my,)), dma((n_my,)),
    ]
    small = (RZ // 2, RY // 2, RX // 2, width)
    rows, coarse = pl.pallas_call(
        functools.partial(level_kernel, slots, chans, cells),
        out_shape=(sds((total, lanes), BF), sds(small, BF)),
        in_specs=[SM] + [VM] * 10 + [pl.BlockSpec(memory_space=pl.ANY)] * 3,
        out_specs=(VM, VM),
        scratch_shapes=scratch,
        compiler_params=pltpu.CompilerParams(collective_id=0, has_side_effects=True),
    )(
        counts, coords, neighbours, features, fine_weights, norm_gain[None, :],
        norm_bias[None, :], sel, swap, same, masks, down_weight, up_weight, weight_t,
    )
    return pl.pallas_call(
        functools.partial(unfold_kernel, slots, chans),
        out_shape=(sds(features.shape, BF), sds(small, BF)),
        in_specs=[VM] * 5,
        out_specs=(VM, VM),
        scratch_shapes=[pltpu.VMEM((total, lanes), BF)],
    )(rows, coarse, sel, swap, masks)


def solution(mesh):
    in_specs = (
        P(("mx", "my"), None, None),
        P(None, ("mx", "my")),
        P(("mx", "my")),
        P(None, ("mx", "my")),
        P(),
        P(),
        P(),
        P(),
        P(),
        P(None, "my"),
    )
    out_specs = (P(("mx", "my"), None, None), P("mx", "my", None, None))
    return jax.shard_map(local, mesh=mesh, in_specs=in_specs, out_specs=out_specs, check_vma=False)
```

```python
import functools

import jax
import jax.numpy as jnp
import numpy as np
from jax import lax
from jax.experimental import pallas as pl
from jax.experimental.pallas import tpu as pltpu
from jax.sharding import PartitionSpec as P

GROUPS = 32
SIDE = 8
RZ = 4
RY = 4
RX = 4
HALF = SIDE // 2
CUBES = HALF**3
PLANE = HALF**2
FACE = 16
norm_eps = 1e-05
MESH = pl.DeviceIdType.MESH
BF = jnp.bfloat16
F32 = jnp.float32
I32 = jnp.int32
VM = pl.BlockSpec(memory_space=pltpu.VMEM)
HBM = pl.BlockSpec(memory_space=pl.ANY)
NN = (((1,), (0,)), ((), ()))
NT = (((1,), (1,)), ((), ()))
TN = (((0,), (0,)), ((), ()))


def constants(chans):
    lane = np.arange(4 * chans)
    masks = np.stack([lane < 2 * chans, lane // chans % 2 == 0])
    masks = np.broadcast_to(masks[:, None, :], (2, 32, 4 * chans))
    sel = np.zeros((256, 256))
    for w in range(8):
        vy, vz, vx = w >> 2, w >> 1 & 1, w & 1
        for i in range(32):
            z, y, x = i // 16 * 2 + vz, i // 4 % 4 * 2 + vy, i % 4 * 2 + vx
            sel[w * 32 + i, (z * SIDE + y) * SIDE + x] = 1
    swap = np.zeros((256, 256))
    for i in range(16):
        for s in range(16):
            swap[i * 16 + s, s * 16 + i] = 1
    wide = np.arange(8 * chans)
    same = wide[:, None] % chans == wide[None, :] % chans
    as_bf = lambda a: jnp.asarray(np.asarray(a, np.float32), BF)
    return as_bf(masks), as_bf(sel), as_bf(swap), as_bf(same)


def dot(a, b, dims=NN):
    return lax.dot_general(a, b, dims, preferred_element_type=F32)


def silu(x):
    h = 0.5 * x
    return h * jnp.tanh(h) + h


def swap_blocks(parts, low64, low32):
    left, right = [p[0] for p in parts], [p[1] for p in parts]
    m = [(left[i], left[i + 4]) for i in range(4)] + [(right[i], right[i + 4]) for i in range(4)]
    for bit, low, up, down in ((2, low64, 64, 64), (1, low32, 32, 96)):
        n = list(m)
        for j in range(8):
            if j & bit:
                continue
            a, b = m[j], m[j | bit]
            n[j] = tuple(jnp.where(low, a[t], pltpu.roll(b[t], up, 1)) for t in range(2))
            n[j | bit] = tuple(jnp.where(low, pltpu.roll(a[t], down, 1), b[t]) for t in range(2))
        m = n
    return m


def level_kernel(
    slots, chans, cells,
    counts_h, coords_h, neighbours_h, feat_h, fine_w_h, gain_h, bias_h, sel_h, swap_h, same_h,
    masks_h, down_h, up_h, weight_h,
    fine, coarse_out,
    counts, coords, neighbours, feat, fine_w, gain, bias, sel, swap, same, masks, down, up, weight,
    blocks, base, sig, sig2, acc, wts, gx, gyp, gym, gz, faces, halo, term,
    coarse, stats, window, everyone, pad, part, result,
    load, fsend, frecv, ssend, srecv, wsend, wrecv, rsend, rrecv, ready, store,
):
    n_mx, n_my = lax.axis_size("mx"), lax.axis_size("my")
    mx, my = lax.axis_index("mx"), lax.axis_index("my")
    n = n_mx * n_my
    me = mx * n_my + my
    width = 8 * chans
    side = width // 2
    wide_c = gain.shape[1]

    order = (
        ("feat", feat_h, feat), ("sel", sel_h, sel), ("masks", masks_h, masks),
        ("swap", swap_h, swap), ("fine_w", fine_w_h, fine_w), ("counts", counts_h, counts),
        ("coords", coords_h, coords), ("neighbours", neighbours_h, neighbours),
        ("same", same_h, same), ("down", down_h, down), ("gain", gain_h, gain),
        ("bias", bias_h, bias), ("weight", weight_h, weight), ("up", up_h, up),
    )
    loads = {
        name: pltpu.make_async_copy(a, b, load.at[i]) for i, (name, a, b) in enumerate(order)
    }
    for name, _, _ in order:
        loads[name].start()

    barrier = pltpu.get_barrier_semaphore()
    low, high = mx > 0, mx < n_mx - 1

    def greet(a, b):
        pl.semaphore_signal(barrier, inc=1, device_id=(a, b), device_id_type=MESH)

    @pl.when(low)
    def _():
        greet(mx - 1, my)

    @pl.when(high)
    def _():
        greet(mx + 1, my)

    for d in range(1, n_my):
        greet(mx, lax.rem(my + d, n_my))

    def entered():
        pl.semaphore_wait(barrier, n_my - 1 + low.astype(I32) + high.astype(I32))

    rounds = max(n_mx - 1, 0).bit_length()

    def tell(k):
        @pl.when(mx + 2**k < n_mx)
        def _():
            pl.semaphore_signal(
                ready.at[k, 0], inc=1, device_id=(mx + 2**k, my), device_id_type=MESH
            )

        @pl.when(mx - 2**k >= 0)
        def _():
            pl.semaphore_signal(
                ready.at[k, 1], inc=1, device_id=(mx - 2**k, my), device_id_type=MESH
            )

    def hear(k):
        @pl.when(mx - 2**k >= 0)
        def _():
            pl.semaphore_wait(ready.at[k, 0], 1)

        @pl.when(mx + 2**k < n_mx)
        def _():
            pl.semaphore_wait(ready.at[k, 1], 1)

    def where_is(d):
        t = lax.rem(me + d, n)
        return (t // n_my, lax.rem(t, n_my))

    for name in ("feat", "sel", "masks"):
        loads[name].wait()

    def rows(ref, q):
        return ref[q * slots : (q + 1) * slots, :]

    def left(ref, q):
        return ref[q * slots : (q + 1) * slots, :side]

    def right(ref, q):
        return ref[q * slots : (q + 1) * slots, side:]

    low64, low32 = masks[0] > 0.5, masks[1] > 0.5
    zero = jnp.zeros((slots, side), BF)

    for g in range(slots // 8):
        for h in range(2):
            x = feat[8 * g : 8 * g + 8, :, 256 * h : 256 * h + 256].reshape(8 * chans, 256)
            r = dot(sel[...], x, NT).astype(BF)
            m = [(r[32 * w : 32 * w + 32, :side], r[32 * w : 32 * w + 32, side:]) for w in range(8)]
            m = swap_blocks(m, low64, low32)
            for s in range(8):
                at = (8 * g + s) * CUBES + 32 * h
                blocks[at : at + 32, :side] = m[s][0]
                blocks[at : at + 32, side:] = m[s][1]
    loads["swap"].wait()
    for z in range(HALF):
        for g in range(slots // 16):
            x = jnp.concatenate(
                [blocks[(16 * g + s) * CUBES + 16 * z : (16 * g + s) * CUBES + 16 * z + 16, :]
                 for s in range(16)], axis=0)
            r = dot(swap[...], x)
            rb = r.astype(BF)
            rs = silu(r).astype(BF)
            for i in range(16):
                at = (16 * z + i) * slots + 16 * g
                base[at : at + 16, :] = rb[16 * i : 16 * i + 16]
                sig[at : at + 16, :] = rs[16 * i : 16 * i + 16]

    for name in ("counts", "coords", "neighbours"):
        loads[name].wait()
    def one_hot(row, count):
        return (lax.broadcasted_iota(I32, (count, slots), 0) == row).astype(F32).astype(BF)

    eye = (
        lax.broadcasted_iota(I32, (slots, slots), 0) == lax.broadcasted_iota(I32, (slots, slots), 1)
    ).astype(F32).astype(BF)

    def turned(table):
        return dot(eye, table, NT).astype(BF)

    pz = coords[0:1, :] - mx * RZ
    py = coords[1:2, :] - my * RY
    px = coords[2:3, :]
    live = lax.broadcasted_iota(I32, (1, slots), 1) < counts[...]

    def link(d):
        g = neighbours[d : d + 1, :]
        here = g - me * slots
        inside = (here >= 0) & (here < slots)
        far = slots + (pz if d < 4 else py) * RX + px
        return jnp.where(g < 0, -1, jnp.where(inside, here, far))

    halo_rows = slots + FACE
    g_x = turned(jnp.concatenate([one_hot(link(d), slots) for d in (0, 1)], axis=0))
    g_yp = turned(one_hot(link(2), halo_rows))
    g_ym = turned(one_hot(link(3), halo_rows))
    g_z = turned(jnp.concatenate([one_hot(link(d), halo_rows) for d in (4, 5)], axis=0))
    edge = (
        jnp.where(live & (py == 0), pz * RX + px, -1),
        jnp.where(live & (py == RY - 1), pz * RX + px, -1),
        jnp.where(live & (pz == 0), py * RX + px, -1),
        jnp.where(live & (pz == RZ - 1), py * RX + px, -1),
    )
    g_edge = [one_hot(e, FACE) for e in edge]
    cell = (pz // 2 * 2 + px // 2) * 2 + py // 2
    place = pz % 2 * 4 + py % 2 * 2 + px % 2
    g_cell = one_hot(jnp.where(live, place * cells + cell, -1), 8 * cells)
    g_lift = turned(g_cell)
    alive = dot(
        jnp.where(live, eye.astype(F32), 0.0).astype(BF), jnp.ones((slots, width), BF)
    ) > 0.5

    peers = (
        (my > 0, mx, my - 1),
        (my < n_my - 1, mx, my + 1),
        (mx > 0, mx - 1, my),
        (mx < n_mx - 1, mx + 1, my),
    )

    def face_copy(r, f):
        _, a, b = peers[f]
        return pltpu.make_async_remote_copy(
            src_ref=faces.at[r, f], dst_ref=halo.at[r, f], send_sem=fsend.at[r, f],
            recv_sem=frecv.at[r, f], device_id=(a, b), device_id_type=MESH,
        )

    low64_face = low64[:FACE]

    def send_face(r, src, f):
        for k in range(PLANE // 2):
            a, x = k // 2, k % 2 * 2
            if f < 2:
                part_of = left if f == 0 else right
                q = a * PLANE + (0 if f == 0 else HALF - 1) * HALF + x
                pair = jnp.concatenate([part_of(src, q), part_of(src, q + 1)], axis=1)
                v = dot(g_edge[f], pair).astype(BF)
                faces[r, f, 2 * k] = v[:, :side]
                faces[r, f, 2 * k + 1] = v[:, side:]
            else:
                q = (0 if f == 2 else HALF - 1) * PLANE + a * HALF + x
                va = dot(g_edge[f], rows(src, q)).astype(BF)
                vb = dot(g_edge[f], rows(src, q + 1)).astype(BF)
                for t in range(2):
                    own = va[:, t * side : (t + 1) * side]
                    other = pltpu.roll(vb[:, t * side : (t + 1) * side], 64, 1)
                    if f == 2:
                        faces[r, f, 2 * k + t] = jnp.where(low64_face, own, other)
                    else:
                        faces[r, f, 2 * k + t] = jnp.where(low64_face, other, own)

        @pl.when(peers[f][0])
        def _():
            face_copy(r, f).start()

        @pl.when(jnp.logical_not(peers[f ^ 1][0]))
        def _():
            halo[r, f] = jnp.zeros_like(halo[r, f])

    def sent_faces(r):
        for f in range(4):
            @pl.when(peers[f][0])
            def _():
                face_copy(r, f).wait_send()

    def take_face(r, f):
        @pl.when(peers[f ^ 1][0])
        def _():
            face_copy(r, f).wait_recv()

    def z_halo(r, f, y, x):
        k = 2 * (y * 2 + x // 2)
        v = [halo[r, f, k + t] for t in range(2)]
        if x % 2:
            v = [pltpu.roll(a, 64, 1) for a in v]
        none = jnp.zeros_like(v[0])
        if f == 2:
            v = [jnp.where(low64_face, a, none) for a in v]
        else:
            v = [jnp.where(low64_face, none, a) for a in v]
        return jnp.concatenate(v, axis=1)

    def both(low, a, b):
        return jnp.concatenate([jnp.where(low, a[t], b[t]) for t in range(2)], axis=1)

    def halves(ref, q):
        return left(ref, q), right(ref, q)

    def run(ref, z, y):
        at = (z * HALF + y) * HALF * slots
        return ref[at : at + HALF * slots, :]

    def spans(runs):
        return [
            slice((z * HALF + y) * HALF * slots, (z * HALF + y + 1) * HALF * slots)
            for z, y in runs
        ]

    def stack(parts):
        return jnp.concatenate(parts, axis=0)

    def x_taps(src, runs):
        taps = []
        for z, y in runs:
            edge_of = halves(gx, z * HALF + y)
            for x in range(HALF):
                q = (z * HALF + y) * HALF + x
                after = halves(src, q + 1) if x < HALF - 1 else edge_of
                before = halves(src, q - 1) if x > 0 else edge_of
                taps.append(both(low32, after, before))
        return stack(taps)

    def y_taps(src, runs):
        taps = []
        for z, y in runs:
            for x in range(HALF):
                q = (z * HALF + y) * HALF + x
                zx = z * HALF + x
                span = slice(zx * slots, (zx + 1) * slots)
                after = left(src, q + HALF) if y < HALF - 1 else gyp[span, :]
                before = right(src, q - HALF) if y > 0 else gym[span, :]
                taps.append(jnp.concatenate([after, before], axis=1))
        return stack(taps)

    def z_taps(src, runs):
        taps = []
        for z, y in runs:
            for x in range(HALF):
                q = (z * HALF + y) * HALF + x
                edge_of = halves(gz, y * HALF + x)
                after = halves(src, q + PLANE) if z < HALF - 1 else edge_of
                before = halves(src, q - PLANE) if z > 0 else edge_of
                taps.append(both(low64, after, before))
        return stack(taps)

    def passes(r, src, runs, kinds):
        taps = {
            0: lambda: stack([run(src, z, y) for z, y in runs]),
            1: lambda: x_taps(src, runs),
            2: lambda: y_taps(src, runs),
            3: lambda: z_taps(src, runs),
        }
        total = None
        for k in kinds:
            v = dot(taps[k](), wts[r, k])
            total = v if total is None else total + v
        return total

    def add_to(ref, runs, value):
        tall = HALF * slots
        return [
            (span, ref[span, :].astype(F32) + value[i * tall : (i + 1) * tall])
            for i, span in enumerate(spans(runs))
        ]

    inner, outer = range(1, HALF - 1), (0, HALF - 1)

    def near(r, src, finish):
        for zy in range(PLANE):
            first, last = halves(src, zy * HALF), halves(src, zy * HALF + HALF - 1)
            pair = jnp.concatenate(
                [both(low32, first, (zero, zero)), both(low32, (zero, zero), last)], axis=0
            )
            gx[zy * slots : (zy + 1) * slots, :] = dot(g_x, pair).astype(BF)
        for y in outer:
            for zs, kinds in ((inner, (0, 1, 3)), (outer, (0, 1))):
                runs = [(z, y) for z in zs]
                for span, v in add_to(base, runs, passes(r, src, runs, kinds)):
                    acc[span, :] = v
        for z in outer:
            runs = [(z, y) for y in inner]
            for span, v in add_to(base, runs, passes(r, src, runs, (0, 1, 2))):
                acc[span, :] = v
        for z in inner:
            runs = [(z, y) for y in inner]
            for span, v in add_to(base, runs, passes(r, src, runs, (0, 1, 2, 3))):
                finish(span, v)

    def far_z(r, src, finish):
        for f in (2, 3):
            take_face(r, f)
        for y in range(HALF):
            for x in range(HALF):
                i = y * HALF + x
                first, last = halves(src, i), halves(src, (HALF - 1) * PLANE + i)
                both_z = jnp.concatenate(
                    [both(low64, first, (zero, zero)), z_halo(r, 2, y, x),
                     both(low64, (zero, zero), last), z_halo(r, 3, y, x)], axis=0,
                )
                gz[i * slots : (i + 1) * slots, :] = dot(g_z, both_z).astype(BF)
        for z in outer:
            runs = [(z, y) for y in inner]
            for span, v in add_to(acc, runs, passes(r, src, runs, (3,))):
                finish(span, v)
        for y in outer:
            runs = [(z, y) for z in outer]
            for span, v in add_to(acc, runs, passes(r, src, runs, (3,))):
                acc[span, :] = v

    def far_y(r, src, finish, f):
        take_face(r, f)
        part_of, table, out = ((left, g_yp, gyp), (right, g_ym, gym))[f]
        for k in range(PLANE // 2):
            z, x = k // 2, k % 2 * 2
            q = z * PLANE + (0 if f == 0 else HALF - 1) * HALF + x
            own = jnp.concatenate([part_of(src, q), part_of(src, q + 1)], axis=1)
            got = jnp.concatenate([halo[r, f, 2 * k], halo[r, f, 2 * k + 1]], axis=1)
            v = dot(table, jnp.concatenate([own, got], axis=0)).astype(BF)
            out[2 * k * slots : (2 * k + 1) * slots, :] = v[:, :side]
            out[(2 * k + 1) * slots : (2 * k + 2) * slots, :] = v[:, side:]
        y = HALF - 1 if f == 0 else 0
        for zs in (range(HALF // 2), range(HALF // 2, HALF)):
            runs = [(z, y) for z in zs]
            for span, v in add_to(acc, runs, passes(r, src, runs, (2,))):
                finish(span, v)

    lane_block = lax.broadcasted_iota(I32, (slots, width), 1) // chans
    block_f = lane_block.astype(F32).astype(BF)
    spread = (
        lax.broadcasted_iota(I32, (chans, width), 0)
        == lax.broadcasted_iota(I32, (chans, width), 1) % chans
    ).astype(F32).astype(BF)
    none = jnp.zeros((chans, width), BF)
    is_block = [block_f == float(w) for w in range(8)]

    def fill(r):
        t = dot(fine_w[r], spread, TN).astype(BF)
        t = [t[i * chans : (i + 1) * chans] for i in range(7)]
        for w in range(8):
            span = slice(w * chans, (w + 1) * chans)
            vy, vz, vx = w >> 2, w >> 1 & 1, w & 1
            v = jnp.where(is_block[w], t[0], none)
            v = jnp.where(is_block[w ^ 1], t[1] if vx else t[2], v)
            v = jnp.where(is_block[w ^ 4], t[3] if vy else t[4], v)
            v = jnp.where(is_block[w ^ 2], t[5] if vz else t[6], v)
            wts[r, 0, span, :] = v
            wts[r, 1, span, :] = jnp.where(is_block[w ^ 1], t[2] if vx else t[1], none)
            wts[r, 2, span, :] = jnp.where(is_block[w ^ 4], t[4] if vy else t[3], none)
            wts[r, 3, span, :] = jnp.where(is_block[w ^ 2], t[6] if vz else t[5], none)

    def first_done(span, value):
        base[span, :] = value.astype(BF)

    loads["fine_w"].wait()
    fill(0)
    near(0, sig, first_done)
    entered()
    for f in (0, 1, 2, 3):
        send_face(0, sig, f)
    for k in range(rounds):
        if k:
            hear(k - 1)
        tell(k)
        if k == 0:
            far_z(0, sig, first_done)
    far_y(0, sig, first_done, 1)
    far_y(0, sig, first_done, 0)
    hear(rounds - 1) if rounds else None

    sums = []
    for o in range(8):
        total = None
        for i in range(8):
            z, y, x = (o >> 2) * 2 + (i >> 2), (o >> 1 & 1) * 2 + (i >> 1 & 1), (o & 1) * 2 + (i & 1)
            v = rows(base, (z * HALF + y) * HALF + x).astype(F32)
            total = v if i == 0 else total + v
        hi = total.astype(BF)
        sums += [hi, (total - hi.astype(F32)).astype(BF)]
    loads["same"].wait()
    sums = dot(jnp.concatenate(sums, axis=0), same[...])
    pooled = jnp.zeros((slots, width), F32)
    for o in range(8):
        v = sums[2 * o * slots : (2 * o + 1) * slots] + sums[(2 * o + 1) * slots : (2 * o + 2) * slots]
        pooled = jnp.where(lane_block == o, v, pooled)
    pooled = (pooled * (1.0 / HALF**3)).astype(BF)
    flat = dot(g_cell, pooled).astype(BF)
    loads["down"].wait()
    ci = jnp.zeros((cells, wide_c), F32)
    for p in range(8):
        ci = ci + jnp.dot(
            flat[p * cells : (p + 1) * cells],
            down[p * width : (p + 1) * width, :],
            preferred_element_type=F32,
        )
    layer = cells // 2
    coarse[0] = ci[:layer]
    coarse[1] = ci[layer:]
    group = wide_c // GROUPS
    lanes = stats.shape[1]

    def split(v):
        a = v.astype(BF)
        rest = v - a.astype(F32)
        b = rest.astype(BF)
        return [a, b, (rest - b.astype(F32)).astype(BF)]

    def in_three(v, table, dims):
        parts = dot(jnp.concatenate([p.astype(F32) for p in split(v)], axis=0).astype(BF), table, dims)
        tall = v.shape[0]
        return parts[:tall] + (parts[tall : 2 * tall] + parts[2 * tall :])

    grouped = (
        lax.broadcasted_iota(I32, (wide_c, lanes), 0) // group
        == lax.broadcasted_iota(I32, (wide_c, lanes), 1)
    ).astype(F32).astype(BF)
    rest = jnp.zeros((6, wide_c), F32)
    local = jnp.concatenate(
        [jnp.sum(ci, axis=0, keepdims=True), jnp.sum(ci * ci, axis=0, keepdims=True), rest], axis=0
    )
    stats[...] = in_three(local, grouped, NN)[0:2]

    def stat_copy(d):
        return pltpu.make_async_remote_copy(
            src_ref=stats, dst_ref=everyone.at[me], send_sem=ssend.at[d], recv_sem=srecv.at[d],
            device_id=where_is(d), device_id_type=MESH,
        )

    def stat_go(d, c):
        stat_copy(d).start()
        return c

    def stat_wait(d, c):
        stat_copy(d).wait()
        return c

    def win_copy(kind, d):
        t = lax.rem(my + d, n_my)
        if kind == 0:
            src, dst, a = coarse, window.at[my, pl.ds(1, 2)], mx
        elif kind == 1:
            src, dst, a = coarse.at[pl.ds(0, 1)], window.at[my, pl.ds(3, 1)], mx - 1
        else:
            src, dst, a = coarse.at[pl.ds(1, 1)], window.at[my, pl.ds(0, 1)], mx + 1
        return pltpu.make_async_remote_copy(
            src_ref=src, dst_ref=dst, send_sem=wsend.at[kind, d], recv_sem=wrecv.at[kind, d],
            device_id=(a, t), device_id_type=MESH,
        )

    lax.fori_loop(1, n, stat_go, 0)
    for d in range(n_my):
        if d:
            win_copy(0, d).start()

        @pl.when(low)
        def _():
            win_copy(1, d).start()

        @pl.when(high)
        def _():
            win_copy(2, d).start()
    window[my, 1:3] = coarse[...]
    everyone[me] = stats[...]

    @pl.when(jnp.logical_not(low))
    def _():
        for j in range(n_my):
            window[j, 0] = jnp.zeros_like(window[j, 0])

    @pl.when(jnp.logical_not(high))
    def _():
        for j in range(n_my):
            window[j, 3] = jnp.zeros_like(window[j, 3])

    pad[...] = jnp.zeros_like(pad)
    sent_faces(0)
    for r in (1, 2):
        fill(r)
    for name in ("gain", "bias", "weight", "up"):
        loads[name].wait()
    for d in range(n_my):
        if d:
            win_copy(0, d).wait()

        @pl.when(low)
        def _():
            win_copy(1, d).wait_send()
            win_copy(2, d).wait_recv()

        @pl.when(high)
        def _():
            win_copy(2, d).wait_send()
            win_copy(1, d).wait_recv()
    lax.fori_loop(1, n, stat_wait, 0)

    total = float(cells * group) * n
    sums = jnp.sum(everyone[...], axis=0) / total
    mean = sums[0:1]
    std = jnp.sqrt(sums[1:2] - mean * mean + norm_eps)
    both_rows = jnp.concatenate([mean, std, jnp.zeros((6, lanes), F32)], axis=0)
    both_rows = in_three(both_rows, grouped, NT)
    mean, std = both_rows[0:1], both_rows[1:2]
    g = gain[...]
    b = bias[...]
    for zw in range(4):
        for j in range(n_my):
            value = silu((window[j, zw] - mean) / std * g + b)
            if zw == 0:
                value = jnp.where(low, value, 0.0)
            if zw == 3:
                value = jnp.where(high, value, 0.0)
            for x in range(2):
                pad[1 + x, zw, 1 + 2 * j : 3 + 2 * j, :] = value[2 * x : 2 * x + 2]
    tall = 2 * n_my
    sums = jnp.zeros((4 * tall, part.shape[2]), F32)
    t = 0
    for dz in range(3):
        for dy in range(3):
            for dx in range(3):
                lhs = jnp.concatenate(
                    [pad[x + dx, z + dz, dy : dy + tall, :] for z in range(2) for x in range(2)],
                    axis=0,
                ).astype(BF)
                sums = sums + lax.dot_general(
                    lhs, weight[:, t * wide_c : (t + 1) * wide_c], (((1,), (1,)), ((), ())),
                    preferred_element_type=F32,
                )
                t += 1
    for j in range(n_my):
        for zx in range(4):
            part[j, 2 * zx : 2 * zx + 2, :] = sums[zx * tall + 2 * j : zx * tall + 2 * j + 2, :]
    copies = []
    for d in range(1, n_my):
        to = lax.rem(my + d, n_my)
        copies.append(
            pltpu.make_async_remote_copy(
                src_ref=part.at[to], dst_ref=result.at[my], send_sem=rsend.at[d],
                recv_sem=rrecv.at[d], device_id=(mx, to), device_id_type=MESH,
            )
        )
    for c in copies:
        c.start()
    result[my] = part[my]
    for c in copies:
        c.wait()

    whole = jnp.concatenate([result[j] for j in range(n_my)], axis=1)
    co = (whole + jnp.concatenate([coarse[0], coarse[1]], axis=0)).astype(BF)
    cof = co.astype(F32)
    for z in range(2):
        for y in range(2):
            q = z * 4 + y
            pair = jnp.concatenate([cof[q : q + 1], cof[q + 2 : q + 3]], axis=0)
            coarse_out[z, y] = pair.astype(BF)
    wide = jnp.dot(co, up[...], preferred_element_type=F32)
    lifted = jnp.concatenate([wide[:, p * width : (p + 1) * width] for p in range(8)], axis=0)
    hi = lifted.astype(BF)
    lo = (lifted - hi.astype(F32)).astype(BF)
    picked = [dot(g_lift, v).astype(BF) for v in (hi, lo)]
    spots = [jnp.where(is_block[o], v, jnp.zeros_like(v)) for o in range(8) for v in picked]
    sums = dot(jnp.concatenate(spots, axis=0), same[...])
    for o in range(8):
        v = sums[2 * o * slots : (2 * o + 1) * slots] + sums[(2 * o + 1) * slots : (2 * o + 2) * slots]
        term[o * slots : (o + 1) * slots, :] = v

    def join(z, y):
        for x in range(HALF):
            q = (z * HALF + y) * HALF + x
            o = z // 2 * 4 + y // 2 * 2 + x // 2
            span = slice(q * slots, (q + 1) * slots)
            f = (base[span, :].astype(F32) + term[o * slots : (o + 1) * slots, :]).astype(BF)
            base[span, :] = f
            sig[span, :] = silu(f.astype(F32)).astype(BF)

    for f, y in ((0, 0), (1, HALF - 1)):
        for z in range(HALF):
            join(z, y)
        send_face(1, sig, f)
    for f, z in ((2, 0), (3, HALF - 1)):
        for y in inner:
            join(z, y)
        send_face(1, sig, f)
    for z in inner:
        for y in inner:
            join(z, y)

    def second_done(span, value):
        f = value.astype(BF)
        base[span, :] = f
        sig2[span, :] = silu(f.astype(F32)).astype(BF)

    near(1, sig, second_done)
    far_z(1, sig, second_done)
    for f in (1, 0):
        far_y(1, sig, second_done, f)
        send_face(2, sig2, f ^ 1)
    for f in (2, 3):
        send_face(2, sig2, f)

    def last_done(span, value):
        for i in range(HALF):
            at = slice(span.start + i * slots, span.start + (i + 1) * slots)
            base[at, :] = jnp.where(alive, value[i * slots : (i + 1) * slots], 0.0).astype(BF)

    near(2, sig2, last_done)
    far_z(2, sig2, last_done)
    sent_faces(1)
    for f in (1, 0):
        far_y(2, sig2, last_done, f)

    stores = []
    for g in range(slots // 16):
        for z in range(HALF):
            x = jnp.concatenate(
                [base[(16 * z + i) * slots + 16 * g : (16 * z + i) * slots + 16 * g + 16, :]
                 for i in range(16)], axis=0)
            r = dot(swap[...], x).astype(BF)
            for s in range(16):
                at = (16 * g + s) * CUBES + 16 * z
                blocks[at : at + 16, :] = r[16 * s : 16 * s + 16]
        piece = pl.ds(16 * g * CUBES, 16 * CUBES)
        stores.append(pltpu.make_async_copy(blocks.at[piece], fine.at[piece], store.at[g]))
        stores[-1].start()
    sent_faces(2)
    for c in stores:
        c.wait()


def unfold_kernel(chans, rows, coarse, sel, masks, fine, coarse_out):
    side = 4 * chans
    low64, low32 = masks[0] > 0.5, masks[1] > 0.5
    for h in range(2):
        m = []
        for s in range(8):
            at = s * CUBES + 32 * h
            m.append((rows[at : at + 32, :side], rows[at : at + 32, side:]))
        m = swap_blocks(m, low64, low32)
        x = jnp.concatenate([jnp.concatenate(p, axis=1) for p in m], axis=0)
        r = dot(x.T, sel[...]).astype(BF)
        fine[:, :, 256 * h : 256 * h + 256] = r.reshape(8, chans, 256)
    coarse_out[...] = coarse[...]


def local(
    features, coords, counts, neighbours, fine_weights, down_weight, up_weight, norm_gain,
    norm_bias, coarse_weight,
):
    slots, chans, _ = features.shape
    n_mx, n_my = lax.axis_size("mx"), lax.axis_size("my")
    cells = (RZ // 2) * (RY // 2) * (RX // 2)
    width = down_weight.shape[1]
    lanes = 8 * chans
    masks, sel, swap, same = constants(chans)
    n = n_mx * n_my
    sds = jax.ShapeDtypeStruct
    weight_t = coarse_weight.T
    ins = (
        counts[None, :], coords, neighbours, features, fine_weights, norm_gain[None, :],
        norm_bias[None, :], sel, swap, same, masks, down_weight, up_weight, weight_t,
    )
    held = [pltpu.VMEM(a.shape, a.dtype) for a in ins]
    dma = pltpu.SemaphoreType.DMA
    total = slots * CUBES
    plane = slots * PLANE
    scratch = held + [
        pltpu.VMEM((total, lanes), BF),
        pltpu.VMEM((total, lanes), BF),
        pltpu.VMEM((total, lanes), BF),
        pltpu.VMEM((total, lanes), BF),
        pltpu.VMEM((total, lanes), F32),
        pltpu.VMEM((3, 4, lanes, lanes), BF),
        pltpu.VMEM((plane, lanes), BF),
        pltpu.VMEM((plane, lanes // 2), BF),
        pltpu.VMEM((plane, lanes // 2), BF),
        pltpu.VMEM((plane, lanes), BF),
        pltpu.VMEM((3, 4, PLANE, FACE, lanes // 2), BF),
        pltpu.VMEM((3, 4, PLANE, FACE, lanes // 2), BF),
        pltpu.VMEM((8 * slots, lanes), F32),
        pltpu.VMEM((2, cells // 2, width), F32),
        pltpu.VMEM((2, 128), F32),
        pltpu.VMEM((n_my, 4, cells // 2, width), F32),
        pltpu.VMEM((n, 2, 128), F32),
        pltpu.VMEM((4, 4, -(-(2 * n_my + 2) // 8) * 8, width), F32),
        pltpu.VMEM((n_my, cells, coarse_weight.shape[1]), F32),
        pltpu.VMEM((n_my, cells, coarse_weight.shape[1]), F32),
        dma((len(ins),)), dma((3, 4)), dma((3, 4)), dma((n,)), dma((n,)),
        dma((3, n_my)), dma((3, n_my)), dma((n_my,)), dma((n_my,)),
        pltpu.SemaphoreType.REGULAR((max(1, (n_mx - 1).bit_length()), 2)), dma((slots // 16,)),
    ]
    small = (RZ // 2, RY // 2, RX // 2, width)
    rows, coarse = pl.pallas_call(
        functools.partial(level_kernel, slots, chans, cells),
        out_shape=(sds((total, lanes), BF), sds(small, BF)),
        in_specs=[HBM] * len(ins),
        out_specs=(HBM, VM),
        scratch_shapes=scratch,
        compiler_params=pltpu.CompilerParams(collective_id=0, has_side_effects=True),
    )(*ins)
    whole = lambda a: pl.BlockSpec(a.shape, lambda i: (0,) * a.ndim)
    return pl.pallas_call(
        functools.partial(unfold_kernel, chans),
        grid=(slots // 8,),
        out_shape=(sds(features.shape, BF), sds(small, BF)),
        in_specs=[pl.BlockSpec((8 * CUBES, lanes), lambda i: (i, 0))]
        + [whole(a) for a in (coarse, sel, masks)],
        out_specs=(
            pl.BlockSpec((8, chans, SIDE**3), lambda i: (i, 0, 0)), whole(coarse),
        ),
    )(rows, coarse, sel, masks)


def solution(mesh):
    in_specs = (
        P(("mx", "my"), None, None),
        P(None, ("mx", "my")),
        P(("mx", "my")),
        P(None, ("mx", "my")),
        P(),
        P(),
        P(),
        P(),
        P(),
        P(None, "my"),
    )
    out_specs = (P(("mx", "my"), None, None), P("mx", "my", None, None))
    return jax.shard_map(local, mesh=mesh, in_specs=in_specs, out_specs=out_specs, check_vma=False)
```

```python
import functools

import jax
import jax.numpy as jnp
import numpy as np
from jax import lax
from jax.experimental import pallas as pl
from jax.experimental.pallas import tpu as pltpu
from jax.sharding import PartitionSpec as P

GROUPS = 32
SIDE = 8
RZ = 4
RY = 4
RX = 4
HALF = SIDE // 2
CUBES = HALF**3
PLANE = HALF**2
FACE = 16
norm_eps = 1e-05
MESH = pl.DeviceIdType.MESH
BF = jnp.bfloat16
F32 = jnp.float32
I32 = jnp.int32
VM = pl.BlockSpec(memory_space=pltpu.VMEM)
HBM = pl.BlockSpec(memory_space=pl.ANY)
NN = (((1,), (0,)), ((), ()))
NT = (((1,), (1,)), ((), ()))
TN = (((0,), (0,)), ((), ()))


def constants(chans):
    lane = np.arange(4 * chans)
    masks = np.stack([lane < 2 * chans, lane // chans % 2 == 0])
    masks = np.broadcast_to(masks[:, None, :], (2, 32, 4 * chans))
    sel = np.zeros((256, 256))
    for w in range(8):
        vy, vz, vx = w >> 2, w >> 1 & 1, w & 1
        for i in range(32):
            z, y, x = i // 16 * 2 + vz, i // 4 % 4 * 2 + vy, i % 4 * 2 + vx
            sel[w * 32 + i, (z * SIDE + y) * SIDE + x] = 1
    swap = np.zeros((256, 256))
    for i in range(16):
        for s in range(16):
            swap[i * 16 + s, s * 16 + i] = 1
    wide = np.arange(8 * chans)
    same = wide[:, None] % chans == wide[None, :] % chans
    as_bf = lambda a: jnp.asarray(np.asarray(a, np.float32), BF)
    halved = lambda a: as_bf(np.stack([a[:, :128], a[:, 128:]]))
    return as_bf(masks), halved(sel), halved(swap), halved(same)


def dot(a, b, dims=NN):
    return lax.dot_general(a, b, dims, preferred_element_type=F32)


def wide_of(ref, *at):
    return jnp.concatenate([ref[at[:-1] + (t,) + at[-1:]] for t in range(2)], axis=1)


def keep(ref, span, value):
    for t in range(2):
        ref[t, span, :] = value[:, 128 * t : 128 * t + 128]


def silu(x):
    h = 0.5 * x
    return h * jnp.tanh(h) + h


def swap_blocks(parts, low64, low32):
    left, right = [p[0] for p in parts], [p[1] for p in parts]
    m = [(left[i], left[i + 4]) for i in range(4)] + [(right[i], right[i + 4]) for i in range(4)]
    for bit, low, up, down in ((2, low64, 64, 64), (1, low32, 32, 96)):
        n = list(m)
        for j in range(8):
            if j & bit:
                continue
            a, b = m[j], m[j | bit]
            n[j] = tuple(jnp.where(low, a[t], pltpu.roll(b[t], up, 1)) for t in range(2))
            n[j | bit] = tuple(jnp.where(low, pltpu.roll(a[t], down, 1), b[t]) for t in range(2))
        m = n
    return m


def level_kernel(
    slots, chans, cells,
    counts_h, coords_h, neighbours_h, feat_h, fine_w_h, gain_h, bias_h, sel_h, swap_h, same_h,
    masks_h, down_h, up_h, weight_h,
    fine, coarse_out,
    counts, coords, neighbours, feat, fine_w, gain, bias, sel, swap, same, masks, down, up, weight,
    blocks, base, sig, sig2, acc, wts, gx, gyp, gym, gz, faces, halo, term,
    coarse, stats, window, everyone, pad, part, result,
    load, fsend, frecv, ssend, srecv, wsend, wrecv, rsend, rrecv, ready, store,
):
    n_mx, n_my = lax.axis_size("mx"), lax.axis_size("my")
    mx, my = lax.axis_index("mx"), lax.axis_index("my")
    n = n_mx * n_my
    me = mx * n_my + my
    width = 8 * chans
    side = width // 2
    wide_c = gain.shape[1]

    chunks = feat.shape[0]
    order = [
        ("feat", feat_h.at[:, :, pl.ds(128 * k, 128)], feat.at[k]) for k in range(chunks)
    ]
    order += [
        ("sel", sel_h, sel), ("masks", masks_h, masks), ("swap", swap_h, swap),
        ("fine_w", fine_w_h, fine_w), ("counts", counts_h, counts),
        ("coords", coords_h, coords), ("neighbours", neighbours_h, neighbours),
    ]
    late = [("same", same_h, same), ("gain", gain_h, gain), ("bias", bias_h, bias)]
    late += [("down", down_h.at[:, pl.ds(128 * k, 128)], down.at[k]) for k in range(down.shape[0])]
    late += [("weight", weight_h, weight)]
    late += [("up", up_h.at[:, pl.ds(128 * k, 128)], up.at[k]) for k in range(up.shape[0])]
    copies = [
        (name, pltpu.make_async_copy(a, b, load.at[i]))
        for i, (name, a, b) in enumerate(order + late)
    ]
    for _, c in copies[: len(order)]:
        c.start()

    def loaded(*names):
        for name, c in copies:
            if name in names:
                c.wait()

    barrier = pltpu.get_barrier_semaphore()
    low, high = mx > 0, mx < n_mx - 1

    def greet(a, b):
        pl.semaphore_signal(barrier, inc=1, device_id=(a, b), device_id_type=MESH)

    @pl.when(low)
    def _():
        greet(mx - 1, my)

    @pl.when(high)
    def _():
        greet(mx + 1, my)

    for d in range(1, n_my):
        greet(mx, lax.rem(my + d, n_my))

    def entered():
        pl.semaphore_wait(barrier, n_my - 1 + low.astype(I32) + high.astype(I32))

    rounds = max(n_mx - 1, 0).bit_length()

    def tell(k):
        @pl.when(mx + 2**k < n_mx)
        def _():
            pl.semaphore_signal(
                ready.at[k, 0], inc=1, device_id=(mx + 2**k, my), device_id_type=MESH
            )

        @pl.when(mx - 2**k >= 0)
        def _():
            pl.semaphore_signal(
                ready.at[k, 1], inc=1, device_id=(mx - 2**k, my), device_id_type=MESH
            )

    def hear(k):
        @pl.when(mx - 2**k >= 0)
        def _():
            pl.semaphore_wait(ready.at[k, 0], 1)

        @pl.when(mx + 2**k < n_mx)
        def _():
            pl.semaphore_wait(ready.at[k, 1], 1)

    loaded("feat", "sel", "masks")
    for _, c in copies[len(order) :]:
        c.start()

    def at_cube(q):
        return slice(q * slots, (q + 1) * slots)

    def rows(ref, q):
        return wide_of(ref, at_cube(q))

    def left(ref, q):
        return ref[0, at_cube(q), :]

    def right(ref, q):
        return ref[1, at_cube(q), :]

    def pair_of(ref):
        return jnp.concatenate([ref[0], ref[1]], axis=1)

    low64, low32 = masks[0] > 0.5, masks[1] > 0.5
    zero = jnp.zeros((slots, side), BF)

    for g in range(slots // 8):
        for h in range(2):
            x = jnp.concatenate(
                [feat[2 * h + t, 8 * g : 8 * g + 8].reshape(8 * chans, 128) for t in range(2)], axis=1
            )
            r = dot(pair_of(sel), x, NT).astype(BF)
            m = [(r[32 * w : 32 * w + 32, :side], r[32 * w : 32 * w + 32, side:]) for w in range(8)]
            m = swap_blocks(m, low64, low32)
            for s in range(8):
                at = (8 * g + s) * CUBES + 32 * h
                blocks[0, at : at + 32, :] = m[s][0]
                blocks[1, at : at + 32, :] = m[s][1]
    loaded("swap")
    for z in range(HALF):
        for g in range(slots // 16):
            x = jnp.concatenate(
                [wide_of(blocks, pl.ds((16 * g + s) * CUBES + 16 * z, 16)) for s in range(16)], axis=0)
            r = dot(pair_of(swap), x)
            rb = r.astype(BF)
            rs = silu(r).astype(BF)
            for i in range(16):
                at = (16 * z + i) * slots + 16 * g
                keep(base, slice(at, at + 16), rb[16 * i : 16 * i + 16])
                keep(sig, slice(at, at + 16), rs[16 * i : 16 * i + 16])

    loaded("counts", "coords", "neighbours")
    def one_hot(row, count):
        return (lax.broadcasted_iota(I32, (count, slots), 0) == row).astype(F32).astype(BF)

    eye = (
        lax.broadcasted_iota(I32, (slots, slots), 0) == lax.broadcasted_iota(I32, (slots, slots), 1)
    ).astype(F32).astype(BF)

    def turned(table):
        return dot(eye, table, NT).astype(BF)

    pz = coords[0:1, :] - mx * RZ
    py = coords[1:2, :] - my * RY
    px = coords[2:3, :]
    live = lax.broadcasted_iota(I32, (1, slots), 1) < counts[...]

    def link(d):
        g = neighbours[d : d + 1, :]
        here = g - me * slots
        inside = (here >= 0) & (here < slots)
        far = slots + (pz if d < 4 else py) * RX + px
        return jnp.where(g < 0, -1, jnp.where(inside, here, far))

    halo_rows = slots + FACE
    g_x = turned(jnp.concatenate([one_hot(link(d), slots) for d in (0, 1)], axis=0))
    g_yp = turned(one_hot(link(2), halo_rows))
    g_ym = turned(one_hot(link(3), halo_rows))
    g_z = turned(jnp.concatenate([one_hot(link(d), halo_rows) for d in (4, 5)], axis=0))
    edge = (
        jnp.where(live & (py == 0), pz * RX + px, -1),
        jnp.where(live & (py == RY - 1), pz * RX + px, -1),
        jnp.where(live & (pz == 0), py * RX + px, -1),
        jnp.where(live & (pz == RZ - 1), py * RX + px, -1),
    )
    g_edge = [one_hot(e, FACE) for e in edge]
    cell = (pz // 2 * 2 + px // 2) * 2 + py // 2
    place = pz % 2 * 4 + py % 2 * 2 + px % 2
    g_cell = one_hot(jnp.where(live, place * cells + cell, -1), 8 * cells)
    g_lift = turned(g_cell)
    alive = dot(
        jnp.where(live, eye.astype(F32), 0.0).astype(BF), jnp.ones((slots, width), BF)
    ) > 0.5

    peers = (
        (my > 0, mx, my - 1),
        (my < n_my - 1, mx, my + 1),
        (mx > 0, mx - 1, my),
        (mx < n_mx - 1, mx + 1, my),
    )

    def face_copy(r, f):
        _, a, b = peers[f]
        return pltpu.make_async_remote_copy(
            src_ref=faces.at[r, f], dst_ref=halo.at[r, f], send_sem=fsend.at[r, f],
            recv_sem=frecv.at[r, f], device_id=(a, b), device_id_type=MESH,
        )

    low64_face = low64[:FACE]

    def send_face(r, src, f):
        for k in range(PLANE // 2):
            a, x = k // 2, k % 2 * 2
            if f < 2:
                part_of = left if f == 0 else right
                q = a * PLANE + (0 if f == 0 else HALF - 1) * HALF + x
                pair = jnp.concatenate([part_of(src, q), part_of(src, q + 1)], axis=1)
                v = dot(g_edge[f], pair).astype(BF)
                faces[r, f, 2 * k] = v[:, :side]
                faces[r, f, 2 * k + 1] = v[:, side:]
            else:
                q = (0 if f == 2 else HALF - 1) * PLANE + a * HALF + x
                va = dot(g_edge[f], rows(src, q)).astype(BF)
                vb = dot(g_edge[f], rows(src, q + 1)).astype(BF)
                for t in range(2):
                    own = va[:, t * side : (t + 1) * side]
                    other = pltpu.roll(vb[:, t * side : (t + 1) * side], 64, 1)
                    if f == 2:
                        faces[r, f, 2 * k + t] = jnp.where(low64_face, own, other)
                    else:
                        faces[r, f, 2 * k + t] = jnp.where(low64_face, other, own)

        @pl.when(peers[f][0])
        def _():
            face_copy(r, f).start()

        @pl.when(jnp.logical_not(peers[f ^ 1][0]))
        def _():
            halo[r, f] = jnp.zeros_like(halo[r, f])

    def sent_faces(r):
        for f in range(4):
            @pl.when(peers[f][0])
            def _():
                face_copy(r, f).wait_send()

    def take_face(r, f):
        @pl.when(peers[f ^ 1][0])
        def _():
            face_copy(r, f).wait_recv()

    def z_halo(r, f, y, x):
        k = 2 * (y * 2 + x // 2)
        v = [halo[r, f, k + t] for t in range(2)]
        if x % 2:
            v = [pltpu.roll(a, 64, 1) for a in v]
        none = jnp.zeros_like(v[0])
        if f == 2:
            v = [jnp.where(low64_face, a, none) for a in v]
        else:
            v = [jnp.where(low64_face, none, a) for a in v]
        return jnp.concatenate(v, axis=1)

    def both(low, a, b):
        return jnp.concatenate([jnp.where(low, a[t], b[t]) for t in range(2)], axis=1)

    def halves(ref, q):
        return left(ref, q), right(ref, q)

    def run(ref, z, y):
        at = (z * HALF + y) * HALF * slots
        return wide_of(ref, slice(at, at + HALF * slots))

    def spans(runs):
        return [
            slice((z * HALF + y) * HALF * slots, (z * HALF + y + 1) * HALF * slots)
            for z, y in runs
        ]

    def stack(parts):
        return jnp.concatenate(parts, axis=0)

    def x_taps(src, runs):
        taps = []
        for z, y in runs:
            edge_of = halves(gx, z * HALF + y)
            for x in range(HALF):
                q = (z * HALF + y) * HALF + x
                after = halves(src, q + 1) if x < HALF - 1 else edge_of
                before = halves(src, q - 1) if x > 0 else edge_of
                taps.append(both(low32, after, before))
        return stack(taps)

    def y_taps(src, runs):
        taps = []
        for z, y in runs:
            for x in range(HALF):
                q = (z * HALF + y) * HALF + x
                zx = z * HALF + x
                span = slice(zx * slots, (zx + 1) * slots)
                after = left(src, q + HALF) if y < HALF - 1 else gyp[span, :]
                before = right(src, q - HALF) if y > 0 else gym[span, :]
                taps.append(jnp.concatenate([after, before], axis=1))
        return stack(taps)

    def z_taps(src, runs):
        taps = []
        for z, y in runs:
            for x in range(HALF):
                q = (z * HALF + y) * HALF + x
                edge_of = halves(gz, y * HALF + x)
                after = halves(src, q + PLANE) if z < HALF - 1 else edge_of
                before = halves(src, q - PLANE) if z > 0 else edge_of
                taps.append(both(low64, after, before))
        return stack(taps)

    def passes(r, src, runs, kinds):
        taps = {
            0: lambda: stack([run(src, z, y) for z, y in runs]),
            1: lambda: x_taps(src, runs),
            2: lambda: y_taps(src, runs),
            3: lambda: z_taps(src, runs),
        }
        total = None
        for k in kinds:
            v = dot(taps[k](), jnp.concatenate([wts[r, k, 0], wts[r, k, 1]], axis=1))
            total = v if total is None else total + v
        return total

    def add_to(ref, runs, value):
        tall = HALF * slots
        return [
            (span, wide_of(ref, span).astype(F32) + value[i * tall : (i + 1) * tall])
            for i, span in enumerate(spans(runs))
        ]

    inner, outer = range(1, HALF - 1), (0, HALF - 1)

    def near_inner(r, src, finish):
        for zy in range(PLANE):
            first, last = halves(src, zy * HALF), halves(src, zy * HALF + HALF - 1)
            pair = jnp.concatenate(
                [both(low32, first, (zero, zero)), both(low32, (zero, zero), last)], axis=0
            )
            keep(gx, at_cube(zy), dot(g_x, pair).astype(BF))
        for z in outer:
            runs = [(z, y) for y in inner]
            for span, v in add_to(base, runs, passes(r, src, runs, (0, 1, 2))):
                keep(acc, span, v)
        for z in inner:
            runs = [(z, y) for y in inner]
            for span, v in add_to(base, runs, passes(r, src, runs, (0, 1, 2, 3))):
                finish(span, v)

    def near_outer(r, src):
        for y in outer:
            for zs, kinds in ((inner, (0, 1, 3)), (outer, (0, 1))):
                runs = [(z, y) for z in zs]
                for span, v in add_to(base, runs, passes(r, src, runs, kinds)):
                    keep(acc, span, v)

    def far_z(r, src, finish):
        for f in (2, 3):
            take_face(r, f)
        for y in range(HALF):
            for x in range(HALF):
                i = y * HALF + x
                first, last = halves(src, i), halves(src, (HALF - 1) * PLANE + i)
                both_z = jnp.concatenate(
                    [both(low64, first, (zero, zero)), z_halo(r, 2, y, x),
                     both(low64, (zero, zero), last), z_halo(r, 3, y, x)], axis=0,
                )
                keep(gz, at_cube(i), dot(g_z, both_z).astype(BF))
        for z in outer:
            runs = [(z, y) for y in inner]
            for span, v in add_to(acc, runs, passes(r, src, runs, (3,))):
                finish(span, v)
        for y in outer:
            runs = [(z, y) for z in outer]
            for span, v in add_to(acc, runs, passes(r, src, runs, (3,))):
                keep(acc, span, v)

    def far_y(r, src, finish, f):
        take_face(r, f)
        part_of, table, out = ((left, g_yp, gyp), (right, g_ym, gym))[f]
        for k in range(PLANE // 2):
            z, x = k // 2, k % 2 * 2
            q = z * PLANE + (0 if f == 0 else HALF - 1) * HALF + x
            own = jnp.concatenate([part_of(src, q), part_of(src, q + 1)], axis=1)
            got = jnp.concatenate([halo[r, f, 2 * k], halo[r, f, 2 * k + 1]], axis=1)
            v = dot(table, jnp.concatenate([own, got], axis=0)).astype(BF)
            out[2 * k * slots : (2 * k + 1) * slots, :] = v[:, :side]
            out[(2 * k + 1) * slots : (2 * k + 2) * slots, :] = v[:, side:]
        y = HALF - 1 if f == 0 else 0
        for zs in (range(HALF // 2), range(HALF // 2, HALF)):
            runs = [(z, y) for z in zs]
            for span, v in add_to(acc, runs, passes(r, src, runs, (2,))):
                finish(span, v)

    lane_block = lax.broadcasted_iota(I32, (slots, width), 1) // chans
    block_f = lane_block.astype(F32).astype(BF)
    spread = (
        lax.broadcasted_iota(I32, (chans, width), 0)
        == lax.broadcasted_iota(I32, (chans, width), 1) % chans
    ).astype(F32).astype(BF)
    none = jnp.zeros((chans, width), BF)
    is_block = [block_f == float(w) for w in range(8)]

    def fit(r, k, span, v):
        for t in range(2):
            wts[r, k, t, span, :] = v[:, side * t : side * t + side]

    def fill(r):
        t = dot(fine_w[r], spread, TN).astype(BF)
        t = [t[i * chans : (i + 1) * chans] for i in range(7)]
        for w in range(8):
            span = slice(w * chans, (w + 1) * chans)
            vy, vz, vx = w >> 2, w >> 1 & 1, w & 1
            v = jnp.where(is_block[w], t[0], none)
            v = jnp.where(is_block[w ^ 1], t[1] if vx else t[2], v)
            v = jnp.where(is_block[w ^ 4], t[3] if vy else t[4], v)
            v = jnp.where(is_block[w ^ 2], t[5] if vz else t[6], v)
            fit(r, 0, span, v)
            fit(r, 1, span, jnp.where(is_block[w ^ 1], t[2] if vx else t[1], none))
            fit(r, 2, span, jnp.where(is_block[w ^ 4], t[4] if vy else t[3], none))
            fit(r, 3, span, jnp.where(is_block[w ^ 2], t[6] if vz else t[5], none))

    def first_done(span, value):
        keep(base, span, value.astype(BF))

    loaded("fine_w")
    fill(0)
    near_inner(0, sig, first_done)
    entered()
    for f in (0, 1, 2, 3):
        send_face(0, sig, f)
    if rounds:
        tell(0)
    near_outer(0, sig)
    for k in range(1, rounds):
        hear(k - 1)
        tell(k)
        if k == 1:
            far_z(0, sig, first_done)
    if rounds < 2:
        far_z(0, sig, first_done)
    far_y(0, sig, first_done, 1)
    far_y(0, sig, first_done, 0)

    sums = []
    for o in range(8):
        total = None
        for i in range(8):
            z, y, x = (o >> 2) * 2 + (i >> 2), (o >> 1 & 1) * 2 + (i >> 1 & 1), (o & 1) * 2 + (i & 1)
            v = rows(base, (z * HALF + y) * HALF + x).astype(F32)
            total = v if i == 0 else total + v
        hi = total.astype(BF)
        sums += [hi, (total - hi.astype(F32)).astype(BF)]
    loaded("same")
    sums = dot(jnp.concatenate(sums, axis=0), pair_of(same))
    pooled = jnp.zeros((slots, width), F32)
    for o in range(8):
        v = sums[2 * o * slots : (2 * o + 1) * slots] + sums[(2 * o + 1) * slots : (2 * o + 2) * slots]
        pooled = jnp.where(lane_block == o, v, pooled)
    pooled = (pooled * (1.0 / HALF**3)).astype(BF)
    flat = dot(g_cell, pooled).astype(BF)
    loaded("down")
    ci = jnp.zeros((cells, wide_c), F32)
    for p in range(8):
        ci = ci + jnp.dot(
            flat[p * cells : (p + 1) * cells],
            jnp.concatenate([down[t, p * width : (p + 1) * width, :] for t in range(down.shape[0])], axis=1),
            preferred_element_type=F32,
        )
    layer = cells // 2
    coarse[0] = ci[:layer]
    coarse[1] = ci[layer:]
    group = wide_c // GROUPS
    lanes = stats.shape[1]

    def split(v):
        a = v.astype(BF)
        rest = v - a.astype(F32)
        b = rest.astype(BF)
        return [a, b, (rest - b.astype(F32)).astype(BF)]

    def in_three(v, table, dims):
        parts = dot(jnp.concatenate([p.astype(F32) for p in split(v)], axis=0).astype(BF), table, dims)
        tall = v.shape[0]
        return parts[:tall] + (parts[tall : 2 * tall] + parts[2 * tall :])

    grouped = (
        lax.broadcasted_iota(I32, (wide_c, lanes), 0) // group
        == lax.broadcasted_iota(I32, (wide_c, lanes), 1)
    ).astype(F32).astype(BF)
    rest = jnp.zeros((6, wide_c), F32)
    local = jnp.concatenate(
        [jnp.sum(ci, axis=0, keepdims=True), jnp.sum(ci * ci, axis=0, keepdims=True), rest], axis=0
    )
    stats[...] = in_three(local, grouped, NN)[0:2]

    offsets = sorted(range(n_mx), key=lambda i: -min(i, n_mx - i))
    others = [(i, j) for i in offsets for j in range(n_my) if i or j]

    def stat_copy(i, j):
        d = i * n_my + j
        return pltpu.make_async_remote_copy(
            src_ref=stats, dst_ref=everyone.at[me], send_sem=ssend.at[d], recv_sem=srecv.at[d],
            device_id=(lax.rem(mx + i, n_mx), lax.rem(my + j, n_my)), device_id_type=MESH,
        )

    def win_copy(kind, d):
        t = lax.rem(my + d, n_my)
        if kind == 0:
            src, dst, a = coarse, window.at[my, pl.ds(1, 2)], mx
        elif kind == 1:
            src, dst, a = coarse.at[pl.ds(0, 1)], window.at[my, pl.ds(3, 1)], mx - 1
        else:
            src, dst, a = coarse.at[pl.ds(1, 1)], window.at[my, pl.ds(0, 1)], mx + 1
        return pltpu.make_async_remote_copy(
            src_ref=src, dst_ref=dst, send_sem=wsend.at[kind, d], recv_sem=wrecv.at[kind, d],
            device_id=(a, t), device_id_type=MESH,
        )

    if rounds:
        hear(rounds - 1)
    for i, j in others:
        stat_copy(i, j).start()
    for d in range(n_my):
        if d:
            win_copy(0, d).start()

        @pl.when(low)
        def _():
            win_copy(1, d).start()

        @pl.when(high)
        def _():
            win_copy(2, d).start()
    window[my, 1:3] = coarse[...]
    everyone[me] = stats[...]

    @pl.when(jnp.logical_not(low))
    def _():
        for j in range(n_my):
            window[j, 0] = jnp.zeros_like(window[j, 0])

    @pl.when(jnp.logical_not(high))
    def _():
        for j in range(n_my):
            window[j, 3] = jnp.zeros_like(window[j, 3])

    pad[...] = jnp.zeros_like(pad)
    sent_faces(0)
    for r in (1, 2):
        fill(r)
    loaded("gain", "bias", "weight", "up")
    for d in range(n_my):
        if d:
            win_copy(0, d).wait()

        @pl.when(low)
        def _():
            win_copy(1, d).wait_send()
            win_copy(2, d).wait_recv()

        @pl.when(high)
        def _():
            win_copy(2, d).wait_send()
            win_copy(1, d).wait_recv()
    for i, j in others:
        stat_copy(i, j).wait()

    total = float(cells * group) * n
    sums = jnp.sum(everyone[...], axis=0) / total
    mean = sums[0:1]
    std = jnp.sqrt(sums[1:2] - mean * mean + norm_eps)
    both_rows = jnp.concatenate([mean, std, jnp.zeros((6, lanes), F32)], axis=0)
    both_rows = in_three(both_rows, grouped, NT)
    mean, std = both_rows[0:1], both_rows[1:2]
    g = gain[...]
    b = bias[...]
    for zw in range(4):
        for j in range(n_my):
            value = silu((window[j, zw] - mean) / std * g + b)
            if zw == 0:
                value = jnp.where(low, value, 0.0)
            if zw == 3:
                value = jnp.where(high, value, 0.0)
            for x in range(2):
                pad[1 + x, zw, 1 + 2 * j : 3 + 2 * j, :] = value[2 * x : 2 * x + 2]
    tall = 2 * n_my
    sums = jnp.zeros((4 * tall, part.shape[2]), F32)
    t = 0
    for dz in range(3):
        for dy in range(3):
            for dx in range(3):
                lhs = jnp.concatenate(
                    [pad[x + dx, z + dz, dy : dy + tall, :] for z in range(2) for x in range(2)],
                    axis=0,
                ).astype(BF)
                sums = sums + lax.dot_general(
                    lhs, weight[:, t * wide_c : (t + 1) * wide_c], (((1,), (1,)), ((), ())),
                    preferred_element_type=F32,
                )
                t += 1
    for j in range(n_my):
        for zx in range(4):
            part[j, 2 * zx : 2 * zx + 2, :] = sums[zx * tall + 2 * j : zx * tall + 2 * j + 2, :]
    copies = []
    for d in range(1, n_my):
        to = lax.rem(my + d, n_my)
        copies.append(
            pltpu.make_async_remote_copy(
                src_ref=part.at[to], dst_ref=result.at[my], send_sem=rsend.at[d],
                recv_sem=rrecv.at[d], device_id=(mx, to), device_id_type=MESH,
            )
        )
    for c in copies:
        c.start()
    result[my] = part[my]
    for c in copies:
        c.wait()

    whole = jnp.concatenate([result[j] for j in range(n_my)], axis=1)
    co = (whole + jnp.concatenate([coarse[0], coarse[1]], axis=0)).astype(BF)
    cof = co.astype(F32)
    for z in range(2):
        for y in range(2):
            q = z * 4 + y
            pair = jnp.concatenate([cof[q : q + 1], cof[q + 2 : q + 3]], axis=0)
            coarse_out[z, y] = pair.astype(BF)
    wide = dot(co, jnp.concatenate([up[k] for k in range(up.shape[0])], axis=1))
    lifted = jnp.concatenate([wide[:, p * width : (p + 1) * width] for p in range(8)], axis=0)
    hi = lifted.astype(BF)
    lo = (lifted - hi.astype(F32)).astype(BF)
    picked = [dot(g_lift, v).astype(BF) for v in (hi, lo)]
    spots = [jnp.where(is_block[o], v, jnp.zeros_like(v)) for o in range(8) for v in picked]
    sums = dot(jnp.concatenate(spots, axis=0), pair_of(same))
    for o in range(8):
        v = sums[2 * o * slots : (2 * o + 1) * slots] + sums[(2 * o + 1) * slots : (2 * o + 2) * slots]
        term[o * slots : (o + 1) * slots, :] = v

    def join(z, y):
        for x in range(HALF):
            q = (z * HALF + y) * HALF + x
            o = z // 2 * 4 + y // 2 * 2 + x // 2
            span = slice(q * slots, (q + 1) * slots)
            f = (wide_of(base, span).astype(F32) + term[o * slots : (o + 1) * slots, :]).astype(BF)
            keep(base, span, f)
            keep(sig, span, silu(f.astype(F32)).astype(BF))

    for f, y in ((0, 0), (1, HALF - 1)):
        for z in range(HALF):
            join(z, y)
        send_face(1, sig, f)
    for f, z in ((2, 0), (3, HALF - 1)):
        for y in inner:
            join(z, y)
        send_face(1, sig, f)
    for z in inner:
        for y in inner:
            join(z, y)

    def second_done(span, value):
        f = value.astype(BF)
        keep(base, span, f)
        keep(sig2, span, silu(f.astype(F32)).astype(BF))

    near_inner(1, sig, second_done)
    near_outer(1, sig)
    far_z(1, sig, second_done)
    for f in (1, 0):
        far_y(1, sig, second_done, f)
        send_face(2, sig2, f ^ 1)
    for f in (2, 3):
        send_face(2, sig2, f)

    def last_done(span, value):
        for i in range(HALF):
            at = slice(span.start + i * slots, span.start + (i + 1) * slots)
            keep(base, at, jnp.where(alive, value[i * slots : (i + 1) * slots], 0.0).astype(BF))

    near_inner(2, sig2, last_done)
    near_outer(2, sig2)
    far_z(2, sig2, last_done)
    sent_faces(1)
    for f in (1, 0):
        far_y(2, sig2, last_done, f)

    stores = []
    for g in range(slots // 16):
        for z in range(HALF):
            x = jnp.concatenate(
                [wide_of(base, pl.ds((16 * z + i) * slots + 16 * g, 16)) for i in range(16)], axis=0)
            r = dot(pair_of(swap), x).astype(BF)
            for s in range(16):
                at = (16 * g + s) * CUBES + 16 * z
                keep(blocks, slice(at, at + 16), r[16 * s : 16 * s + 16])
        piece = (slice(None), pl.ds(16 * g * CUBES, 16 * CUBES))
        stores.append(pltpu.make_async_copy(blocks.at[piece], fine.at[piece], store.at[g]))
        stores[-1].start()
    sent_faces(2)
    for c in stores:
        c.wait()


def unfold_kernel(chans, rows, coarse, sel, masks, fine, coarse_out):
    low64, low32 = masks[0] > 0.5, masks[1] > 0.5
    for h in range(2):
        m = []
        for s in range(8):
            at = s * CUBES + 32 * h
            m.append((rows[0, at : at + 32, :], rows[1, at : at + 32, :]))
        m = swap_blocks(m, low64, low32)
        x = jnp.concatenate([jnp.concatenate(p, axis=1) for p in m], axis=0)
        r = dot(x.T, jnp.concatenate([sel[0], sel[1]], axis=1)).astype(BF)
        fine[:, :, 256 * h : 256 * h + 256] = r.reshape(8, chans, 256)
    coarse_out[...] = coarse[...]


def local(
    features, coords, counts, neighbours, fine_weights, down_weight, up_weight, norm_gain,
    norm_bias, coarse_weight,
):
    slots, chans, _ = features.shape
    n_mx, n_my = lax.axis_size("mx"), lax.axis_size("my")
    cells = (RZ // 2) * (RY // 2) * (RX // 2)
    width = down_weight.shape[1]
    lanes = 8 * chans
    masks, sel, swap, same = constants(chans)
    n = n_mx * n_my
    sds = jax.ShapeDtypeStruct
    weight_t = coarse_weight.T
    ins = (
        counts[None, :], coords, neighbours, features, fine_weights, norm_gain[None, :],
        norm_bias[None, :], sel, swap, same, masks, down_weight, up_weight, weight_t,
    )
    held = [pltpu.VMEM(a.shape, a.dtype) for a in ins]
    held[3] = pltpu.VMEM((SIDE**3 // 128, slots, chans, 128), BF)
    held[11] = pltpu.VMEM((width // 128, down_weight.shape[0], 128), BF)
    held[12] = pltpu.VMEM((up_weight.shape[1] // 128, width, 128), BF)
    dma = pltpu.SemaphoreType.DMA
    total = slots * CUBES
    plane = slots * PLANE
    scratch = held + [
        pltpu.VMEM((2, total, 128), BF),
        pltpu.VMEM((2, total, 128), BF),
        pltpu.VMEM((2, total, 128), BF),
        pltpu.VMEM((2, total, 128), BF),
        pltpu.VMEM((2, total, 128), F32),
        pltpu.VMEM((3, 4, 2, lanes, 128), BF),
        pltpu.VMEM((2, plane, 128), BF),
        pltpu.VMEM((plane, lanes // 2), BF),
        pltpu.VMEM((plane, lanes // 2), BF),
        pltpu.VMEM((2, plane, 128), BF),
        pltpu.VMEM((3, 4, PLANE, FACE, lanes // 2), BF),
        pltpu.VMEM((3, 4, PLANE, FACE, lanes // 2), BF),
        pltpu.VMEM((8 * slots, lanes), F32),
        pltpu.VMEM((2, cells // 2, width), F32),
        pltpu.VMEM((2, 128), F32),
        pltpu.VMEM((n_my, 4, cells // 2, width), F32),
        pltpu.VMEM((n, 2, 128), F32),
        pltpu.VMEM((4, 4, -(-(2 * n_my + 2) // 8) * 8, width), F32),
        pltpu.VMEM((n_my, cells, coarse_weight.shape[1]), F32),
        pltpu.VMEM((n_my, cells, coarse_weight.shape[1]), F32),
        dma((64,)), dma((3, 4)), dma((3, 4)), dma((n,)), dma((n,)),
        dma((3, n_my)), dma((3, n_my)), dma((n_my,)), dma((n_my,)),
        pltpu.SemaphoreType.REGULAR((max(1, (n_mx - 1).bit_length()), 2)), dma((slots // 16,)),
    ]
    small = (RZ // 2, RY // 2, RX // 2, width)
    rows, coarse = pl.pallas_call(
        functools.partial(level_kernel, slots, chans, cells),
        out_shape=(sds((2, total, 128), BF), sds(small, BF)),
        in_specs=[HBM] * len(ins),
        out_specs=(HBM, VM),
        scratch_shapes=scratch,
        compiler_params=pltpu.CompilerParams(collective_id=0, has_side_effects=True),
    )(*ins)
    whole = lambda a: pl.BlockSpec(a.shape, lambda i: (0,) * a.ndim)
    return pl.pallas_call(
        functools.partial(unfold_kernel, chans),
        grid=(slots // 8,),
        out_shape=(sds(features.shape, BF), sds(small, BF)),
        in_specs=[pl.BlockSpec((2, 8 * CUBES, 128), lambda i: (0, i, 0))]
        + [whole(a) for a in (coarse, sel, masks)],
        out_specs=(
            pl.BlockSpec((8, chans, SIDE**3), lambda i: (i, 0, 0)), whole(coarse),
        ),
    )(rows, coarse, sel, masks)


def solution(mesh):
    in_specs = (
        P(("mx", "my"), None, None),
        P(None, ("mx", "my")),
        P(("mx", "my")),
        P(None, ("mx", "my")),
        P(),
        P(),
        P(),
        P(),
        P(),
        P(None, "my"),
    )
    out_specs = (P(("mx", "my"), None, None), P("mx", "my", None, None))
    return jax.shard_map(local, mesh=mesh, in_specs=in_specs, out_specs=out_specs, check_vma=False)
```

```python
import functools

import jax
import jax.numpy as jnp
import numpy as np
from jax import lax
from jax.experimental import pallas as pl
from jax.experimental.pallas import tpu as pltpu
from jax.sharding import PartitionSpec as P

GROUPS = 32
SIDE = 8
RZ = 4
RY = 4
RX = 4
HALF = SIDE // 2
CUBES = HALF**3
PLANE = HALF**2
FACE = 16
norm_eps = 1e-05
MESH = pl.DeviceIdType.MESH
BF = jnp.bfloat16
F32 = jnp.float32
I32 = jnp.int32
VM = pl.BlockSpec(memory_space=pltpu.VMEM)
HBM = pl.BlockSpec(memory_space=pl.ANY)
NN = (((1,), (0,)), ((), ()))
NT = (((1,), (1,)), ((), ()))
TN = (((0,), (0,)), ((), ()))


def constants(chans):
    lane = np.arange(4 * chans)
    masks = np.stack([lane < 2 * chans, lane // chans % 2 == 0])
    masks = np.broadcast_to(masks[:, None, :], (2, 32, 4 * chans))
    sel = np.zeros((256, 256))
    for w in range(8):
        vy, vz, vx = w >> 2, w >> 1 & 1, w & 1
        for i in range(32):
            z, y, x = i // 16 * 2 + vz, i // 4 % 4 * 2 + vy, i % 4 * 2 + vx
            sel[w * 32 + i, (z * SIDE + y) * SIDE + x] = 1
    swap = np.zeros((256, 256))
    for i in range(16):
        for s in range(16):
            swap[i * 16 + s, s * 16 + i] = 1
    wide = np.arange(8 * chans)
    same = wide[:, None] % chans == wide[None, :] % chans
    as_bf = lambda a: jnp.asarray(np.asarray(a, np.float32), BF)
    halved = lambda a: as_bf(np.stack([a[:, :128], a[:, 128:]]))
    return as_bf(masks), halved(sel), halved(swap), halved(same)


def dot(a, b, dims=NN):
    return lax.dot_general(a, b, dims, preferred_element_type=F32)


def wide_of(ref, *at):
    return jnp.concatenate([ref[at[:-1] + (t,) + at[-1:]] for t in range(2)], axis=1)


def keep(ref, span, value):
    for t in range(2):
        ref[t, span, :] = value[:, 128 * t : 128 * t + 128]


def silu(x):
    h = 0.5 * x
    return h * jnp.tanh(h) + h


def swap_blocks(parts, low64, low32):
    left, right = [p[0] for p in parts], [p[1] for p in parts]
    m = [(left[i], left[i + 4]) for i in range(4)] + [(right[i], right[i + 4]) for i in range(4)]
    for bit, low, up, down in ((2, low64, 64, 64), (1, low32, 32, 96)):
        n = list(m)
        for j in range(8):
            if j & bit:
                continue
            a, b = m[j], m[j | bit]
            n[j] = tuple(jnp.where(low, a[t], pltpu.roll(b[t], up, 1)) for t in range(2))
            n[j | bit] = tuple(jnp.where(low, pltpu.roll(a[t], down, 1), b[t]) for t in range(2))
        m = n
    return m


def level_kernel(
    slots, chans, cells,
    counts_h, coords_h, neighbours_h, feat_h, fine_w_h, gain_h, bias_h, sel_h, swap_h, same_h,
    masks_h, down_h, up_h, weight_h,
    fine, coarse_out,
    counts, coords, neighbours, feat, fine_w, gain, bias, sel, swap, same, masks, down, up, weight,
    blocks, base, sig, sig2, acc, wts, gx, gyp, gym, gz, faces, halo, term,
    coarse, stats, window, everyone, pad, part, result,
    load, fsend, frecv, ssend, srecv, wsend, wrecv, rsend, rrecv, ready,
):
    n_mx, n_my = lax.axis_size("mx"), lax.axis_size("my")
    mx, my = lax.axis_index("mx"), lax.axis_index("my")
    n = n_mx * n_my
    me = mx * n_my + my
    width = 8 * chans
    side = width // 2
    wide_c = gain.shape[1]

    chunks = feat.shape[0]
    order = [
        ("feat", feat_h.at[:, :, pl.ds(128 * k, 128)], feat.at[k]) for k in range(chunks)
    ]
    order += [
        ("sel", sel_h, sel), ("masks", masks_h, masks), ("swap", swap_h, swap),
        ("fine_w", fine_w_h, fine_w), ("counts", counts_h, counts),
        ("coords", coords_h, coords), ("neighbours", neighbours_h, neighbours),
    ]
    late = [("same", same_h, same), ("gain", gain_h, gain), ("bias", bias_h, bias)]
    late += [("down", down_h.at[:, pl.ds(128 * k, 128)], down.at[k]) for k in range(down.shape[0])]
    late += [("weight", weight_h, weight)]
    late += [("up", up_h.at[:, pl.ds(128 * k, 128)], up.at[k]) for k in range(up.shape[0])]
    copies = [
        (name, pltpu.make_async_copy(a, b, load.at[i]))
        for i, (name, a, b) in enumerate(order + late)
    ]
    for _, c in copies[: len(order)]:
        c.start()

    def loaded(*names):
        for name, c in copies:
            if name in names:
                c.wait()

    barrier = pltpu.get_barrier_semaphore()
    low, high = mx > 0, mx < n_mx - 1

    def greet(a, b):
        pl.semaphore_signal(barrier, inc=1, device_id=(a, b), device_id_type=MESH)

    @pl.when(low)
    def _():
        greet(mx - 1, my)

    @pl.when(high)
    def _():
        greet(mx + 1, my)

    for d in range(1, n_my):
        greet(mx, lax.rem(my + d, n_my))

    def entered():
        pl.semaphore_wait(barrier, n_my - 1 + low.astype(I32) + high.astype(I32))

    rounds = max(n_mx - 1, 0).bit_length()

    def tell(k):
        @pl.when(mx + 2**k < n_mx)
        def _():
            pl.semaphore_signal(
                ready.at[k, 0], inc=1, device_id=(mx + 2**k, my), device_id_type=MESH
            )

        @pl.when(mx - 2**k >= 0)
        def _():
            pl.semaphore_signal(
                ready.at[k, 1], inc=1, device_id=(mx - 2**k, my), device_id_type=MESH
            )

    def hear(k):
        @pl.when(mx - 2**k >= 0)
        def _():
            pl.semaphore_wait(ready.at[k, 0], 1)

        @pl.when(mx + 2**k < n_mx)
        def _():
            pl.semaphore_wait(ready.at[k, 1], 1)

    loaded("feat", "sel", "masks")
    for _, c in copies[len(order) :]:
        c.start()

    def at_cube(q):
        return slice(q * slots, (q + 1) * slots)

    def rows(ref, q):
        return wide_of(ref, at_cube(q))

    def left(ref, q):
        return ref[0, at_cube(q), :]

    def right(ref, q):
        return ref[1, at_cube(q), :]

    def pair_of(ref):
        return jnp.concatenate([ref[0], ref[1]], axis=1)

    low64, low32 = masks[0] > 0.5, masks[1] > 0.5
    zero = jnp.zeros((slots, side), BF)

    for g in range(slots // 8):
        for h in range(2):
            x = jnp.concatenate(
                [feat[2 * h + t, 8 * g : 8 * g + 8].reshape(8 * chans, 128) for t in range(2)], axis=1
            )
            r = dot(pair_of(sel), x, NT).astype(BF)
            m = [(r[32 * w : 32 * w + 32, :side], r[32 * w : 32 * w + 32, side:]) for w in range(8)]
            m = swap_blocks(m, low64, low32)
            for s in range(8):
                at = (8 * g + s) * CUBES + 32 * h
                blocks[0, at : at + 32, :] = m[s][0]
                blocks[1, at : at + 32, :] = m[s][1]
    loaded("swap")
    for z in range(HALF):
        for g in range(slots // 16):
            x = jnp.concatenate(
                [wide_of(blocks, pl.ds((16 * g + s) * CUBES + 16 * z, 16)) for s in range(16)], axis=0)
            r = dot(pair_of(swap), x)
            rb = r.astype(BF)
            rs = silu(r).astype(BF)
            for i in range(16):
                at = (16 * z + i) * slots + 16 * g
                keep(base, slice(at, at + 16), rb[16 * i : 16 * i + 16])
                keep(sig, slice(at, at + 16), rs[16 * i : 16 * i + 16])

    loaded("counts", "coords", "neighbours")
    def one_hot(row, count):
        return (lax.broadcasted_iota(I32, (count, slots), 0) == row).astype(F32).astype(BF)

    eye = (
        lax.broadcasted_iota(I32, (slots, slots), 0) == lax.broadcasted_iota(I32, (slots, slots), 1)
    ).astype(F32).astype(BF)

    def turned(table):
        return dot(eye, table, NT).astype(BF)

    pz = coords[0:1, :] - mx * RZ
    py = coords[1:2, :] - my * RY
    px = coords[2:3, :]
    live = lax.broadcasted_iota(I32, (1, slots), 1) < counts[...]

    def link(d):
        g = neighbours[d : d + 1, :]
        here = g - me * slots
        inside = (here >= 0) & (here < slots)
        far = slots + (pz if d < 4 else py) * RX + px
        return jnp.where(g < 0, -1, jnp.where(inside, here, far))

    halo_rows = slots + FACE
    g_x = turned(jnp.concatenate([one_hot(link(d), slots) for d in (0, 1)], axis=0))
    g_yp = turned(one_hot(link(2), halo_rows))
    g_ym = turned(one_hot(link(3), halo_rows))
    g_z = turned(jnp.concatenate([one_hot(link(d), halo_rows) for d in (4, 5)], axis=0))
    edge = (
        jnp.where(live & (py == 0), pz * RX + px, -1),
        jnp.where(live & (py == RY - 1), pz * RX + px, -1),
        jnp.where(live & (pz == 0), py * RX + px, -1),
        jnp.where(live & (pz == RZ - 1), py * RX + px, -1),
    )
    g_edge = [one_hot(e, FACE) for e in edge]
    cell = (pz // 2 * 2 + px // 2) * 2 + py // 2
    place = pz % 2 * 4 + py % 2 * 2 + px % 2
    g_cell = one_hot(jnp.where(live, place * cells + cell, -1), 8 * cells)
    g_lift = turned(g_cell)
    alive = dot(
        jnp.where(live, eye.astype(F32), 0.0).astype(BF), jnp.ones((slots, width), BF)
    ) > 0.5

    peers = (
        (my > 0, mx, my - 1),
        (my < n_my - 1, mx, my + 1),
        (mx > 0, mx - 1, my),
        (mx < n_mx - 1, mx + 1, my),
    )

    def face_copy(r, f):
        _, a, b = peers[f]
        return pltpu.make_async_remote_copy(
            src_ref=faces.at[r, f], dst_ref=halo.at[r, f], send_sem=fsend.at[r, f],
            recv_sem=frecv.at[r, f], device_id=(a, b), device_id_type=MESH,
        )

    low64_face = low64[:FACE]

    def send_face(r, src, f):
        for k in range(PLANE // 2):
            a, x = k // 2, k % 2 * 2
            if f < 2:
                part_of = left if f == 0 else right
                q = a * PLANE + (0 if f == 0 else HALF - 1) * HALF + x
                pair = jnp.concatenate([part_of(src, q), part_of(src, q + 1)], axis=1)
                v = dot(g_edge[f], pair).astype(BF)
                faces[r, f, 2 * k] = v[:, :side]
                faces[r, f, 2 * k + 1] = v[:, side:]
            else:
                q = (0 if f == 2 else HALF - 1) * PLANE + a * HALF + x
                va = dot(g_edge[f], rows(src, q)).astype(BF)
                vb = dot(g_edge[f], rows(src, q + 1)).astype(BF)
                for t in range(2):
                    own = va[:, t * side : (t + 1) * side]
                    other = pltpu.roll(vb[:, t * side : (t + 1) * side], 64, 1)
                    if f == 2:
                        faces[r, f, 2 * k + t] = jnp.where(low64_face, own, other)
                    else:
                        faces[r, f, 2 * k + t] = jnp.where(low64_face, other, own)

        @pl.when(peers[f][0])
        def _():
            face_copy(r, f).start()

        @pl.when(jnp.logical_not(peers[f ^ 1][0]))
        def _():
            halo[r, f] = jnp.zeros_like(halo[r, f])

    def sent_faces(r):
        for f in range(4):
            @pl.when(peers[f][0])
            def _():
                face_copy(r, f).wait_send()

    def take_face(r, f):
        @pl.when(peers[f ^ 1][0])
        def _():
            face_copy(r, f).wait_recv()

    def z_halo(r, f, y, x):
        k = 2 * (y * 2 + x // 2)
        v = [halo[r, f, k + t] for t in range(2)]
        if x % 2:
            v = [pltpu.roll(a, 64, 1) for a in v]
        none = jnp.zeros_like(v[0])
        if f == 2:
            v = [jnp.where(low64_face, a, none) for a in v]
        else:
            v = [jnp.where(low64_face, none, a) for a in v]
        return jnp.concatenate(v, axis=1)

    def both(low, a, b):
        return jnp.concatenate([jnp.where(low, a[t], b[t]) for t in range(2)], axis=1)

    def halves(ref, q):
        return left(ref, q), right(ref, q)

    def run(ref, z, y):
        at = (z * HALF + y) * HALF * slots
        return wide_of(ref, slice(at, at + HALF * slots))

    def spans(runs):
        return [
            slice((z * HALF + y) * HALF * slots, (z * HALF + y + 1) * HALF * slots)
            for z, y in runs
        ]

    def stack(parts):
        return jnp.concatenate(parts, axis=0)

    def x_taps(src, runs):
        taps = []
        for z, y in runs:
            edge_of = halves(gx, z * HALF + y)
            for x in range(HALF):
                q = (z * HALF + y) * HALF + x
                after = halves(src, q + 1) if x < HALF - 1 else edge_of
                before = halves(src, q - 1) if x > 0 else edge_of
                taps.append(both(low32, after, before))
        return stack(taps)

    def y_taps(src, runs):
        taps = []
        for z, y in runs:
            for x in range(HALF):
                q = (z * HALF + y) * HALF + x
                zx = z * HALF + x
                span = slice(zx * slots, (zx + 1) * slots)
                after = left(src, q + HALF) if y < HALF - 1 else gyp[span, :]
                before = right(src, q - HALF) if y > 0 else gym[span, :]
                taps.append(jnp.concatenate([after, before], axis=1))
        return stack(taps)

    def z_taps(src, runs):
        taps = []
        for z, y in runs:
            for x in range(HALF):
                q = (z * HALF + y) * HALF + x
                edge_of = halves(gz, y * HALF + x)
                after = halves(src, q + PLANE) if z < HALF - 1 else edge_of
                before = halves(src, q - PLANE) if z > 0 else edge_of
                taps.append(both(low64, after, before))
        return stack(taps)

    def passes(r, src, runs, kinds):
        taps = {
            0: lambda: stack([run(src, z, y) for z, y in runs]),
            1: lambda: x_taps(src, runs),
            2: lambda: y_taps(src, runs),
            3: lambda: z_taps(src, runs),
        }
        total = None
        for k in kinds:
            v = dot(taps[k](), jnp.concatenate([wts[r, k, 0], wts[r, k, 1]], axis=1))
            total = v if total is None else total + v
        return total

    def add_to(ref, runs, value):
        tall = HALF * slots
        return [
            (span, wide_of(ref, span).astype(F32) + value[i * tall : (i + 1) * tall])
            for i, span in enumerate(spans(runs))
        ]

    inner, outer = range(1, HALF - 1), (0, HALF - 1)

    def near_inner(r, src, finish):
        for zy in range(PLANE):
            first, last = halves(src, zy * HALF), halves(src, zy * HALF + HALF - 1)
            pair = jnp.concatenate(
                [both(low32, first, (zero, zero)), both(low32, (zero, zero), last)], axis=0
            )
            keep(gx, at_cube(zy), dot(g_x, pair).astype(BF))
        for z in outer:
            runs = [(z, y) for y in inner]
            for span, v in add_to(base, runs, passes(r, src, runs, (0, 1, 2))):
                keep(acc, span, v)
        for z in inner:
            runs = [(z, y) for y in inner]
            for span, v in add_to(base, runs, passes(r, src, runs, (0, 1, 2, 3))):
                finish(span, v)

    def near_outer(r, src):
        for y in outer:
            for zs, kinds in ((inner, (0, 1, 3)), (outer, (0, 1))):
                runs = [(z, y) for z in zs]
                for span, v in add_to(base, runs, passes(r, src, runs, kinds)):
                    keep(acc, span, v)

    def far_z(r, src, finish):
        for f in (2, 3):
            take_face(r, f)
        for y in range(HALF):
            for x in range(HALF):
                i = y * HALF + x
                first, last = halves(src, i), halves(src, (HALF - 1) * PLANE + i)
                both_z = jnp.concatenate(
                    [both(low64, first, (zero, zero)), z_halo(r, 2, y, x),
                     both(low64, (zero, zero), last), z_halo(r, 3, y, x)], axis=0,
                )
                keep(gz, at_cube(i), dot(g_z, both_z).astype(BF))
        for z in outer:
            runs = [(z, y) for y in inner]
            for span, v in add_to(acc, runs, passes(r, src, runs, (3,))):
                finish(span, v)
        for y in outer:
            runs = [(z, y) for z in outer]
            for span, v in add_to(acc, runs, passes(r, src, runs, (3,))):
                keep(acc, span, v)

    def far_y(r, src, finish, f):
        take_face(r, f)
        part_of, table, out = ((left, g_yp, gyp), (right, g_ym, gym))[f]
        for k in range(PLANE // 2):
            z, x = k // 2, k % 2 * 2
            q = z * PLANE + (0 if f == 0 else HALF - 1) * HALF + x
            own = jnp.concatenate([part_of(src, q), part_of(src, q + 1)], axis=1)
            got = jnp.concatenate([halo[r, f, 2 * k], halo[r, f, 2 * k + 1]], axis=1)
            v = dot(table, jnp.concatenate([own, got], axis=0)).astype(BF)
            out[2 * k * slots : (2 * k + 1) * slots, :] = v[:, :side]
            out[(2 * k + 1) * slots : (2 * k + 2) * slots, :] = v[:, side:]
        y = HALF - 1 if f == 0 else 0
        for zs in (range(HALF // 2), range(HALF // 2, HALF)):
            runs = [(z, y) for z in zs]
            for span, v in add_to(acc, runs, passes(r, src, runs, (2,))):
                finish(span, v)

    lane_block = lax.broadcasted_iota(I32, (slots, width), 1) // chans
    block_f = lane_block.astype(F32).astype(BF)
    spread = (
        lax.broadcasted_iota(I32, (chans, width), 0)
        == lax.broadcasted_iota(I32, (chans, width), 1) % chans
    ).astype(F32).astype(BF)
    none = jnp.zeros((chans, width), BF)
    is_block = [block_f == float(w) for w in range(8)]

    def fit(r, k, span, v):
        for t in range(2):
            wts[r, k, t, span, :] = v[:, side * t : side * t + side]

    def fill(r):
        t = dot(fine_w[r], spread, TN).astype(BF)
        t = [t[i * chans : (i + 1) * chans] for i in range(7)]
        for w in range(8):
            span = slice(w * chans, (w + 1) * chans)
            vy, vz, vx = w >> 2, w >> 1 & 1, w & 1
            v = jnp.where(is_block[w], t[0], none)
            v = jnp.where(is_block[w ^ 1], t[1] if vx else t[2], v)
            v = jnp.where(is_block[w ^ 4], t[3] if vy else t[4], v)
            v = jnp.where(is_block[w ^ 2], t[5] if vz else t[6], v)
            fit(r, 0, span, v)
            fit(r, 1, span, jnp.where(is_block[w ^ 1], t[2] if vx else t[1], none))
            fit(r, 2, span, jnp.where(is_block[w ^ 4], t[4] if vy else t[3], none))
            fit(r, 3, span, jnp.where(is_block[w ^ 2], t[6] if vz else t[5], none))

    def first_done(span, value):
        keep(base, span, value.astype(BF))

    entered()
    for f in (0, 1, 2, 3):
        send_face(0, sig, f)
    if rounds:
        tell(0)
    loaded("fine_w")
    fill(0)
    near_inner(0, sig, first_done)
    near_outer(0, sig)
    for k in range(1, rounds):
        hear(k - 1)
        tell(k)
        if k == 1:
            far_z(0, sig, first_done)
    if rounds < 2:
        far_z(0, sig, first_done)
    far_y(0, sig, first_done, 1)
    far_y(0, sig, first_done, 0)

    sums = []
    for o in range(8):
        total = None
        for i in range(8):
            z, y, x = (o >> 2) * 2 + (i >> 2), (o >> 1 & 1) * 2 + (i >> 1 & 1), (o & 1) * 2 + (i & 1)
            v = rows(base, (z * HALF + y) * HALF + x).astype(F32)
            total = v if i == 0 else total + v
        hi = total.astype(BF)
        sums += [hi, (total - hi.astype(F32)).astype(BF)]
    loaded("same")
    sums = dot(jnp.concatenate(sums, axis=0), pair_of(same))
    pooled = jnp.zeros((slots, width), F32)
    for o in range(8):
        v = sums[2 * o * slots : (2 * o + 1) * slots] + sums[(2 * o + 1) * slots : (2 * o + 2) * slots]
        pooled = jnp.where(lane_block == o, v, pooled)
    pooled = (pooled * (1.0 / HALF**3)).astype(BF)
    flat = dot(g_cell, pooled).astype(BF)
    loaded("down")
    ci = jnp.zeros((cells, wide_c), F32)
    for p in range(8):
        ci = ci + jnp.dot(
            flat[p * cells : (p + 1) * cells],
            jnp.concatenate([down[t, p * width : (p + 1) * width, :] for t in range(down.shape[0])], axis=1),
            preferred_element_type=F32,
        )
    layer = cells // 2
    coarse[0] = ci[:layer]
    coarse[1] = ci[layer:]
    group = wide_c // GROUPS
    lanes = stats.shape[1]

    def split(v):
        a = v.astype(BF)
        rest = v - a.astype(F32)
        b = rest.astype(BF)
        return [a, b, (rest - b.astype(F32)).astype(BF)]

    def in_three(v, table, dims):
        parts = dot(jnp.concatenate([p.astype(F32) for p in split(v)], axis=0).astype(BF), table, dims)
        tall = v.shape[0]
        return parts[:tall] + (parts[tall : 2 * tall] + parts[2 * tall :])

    grouped = (
        lax.broadcasted_iota(I32, (wide_c, lanes), 0) // group
        == lax.broadcasted_iota(I32, (wide_c, lanes), 1)
    ).astype(F32).astype(BF)
    rest = jnp.zeros((6, wide_c), F32)
    local = jnp.concatenate(
        [jnp.sum(ci, axis=0, keepdims=True), jnp.sum(ci * ci, axis=0, keepdims=True), rest], axis=0
    )
    stats[...] = in_three(local, grouped, NN)[0:2]

    offsets = sorted(range(n_mx), key=lambda i: -min(i, n_mx - i))
    others = [(i, j) for i in offsets for j in range(n_my) if i or j]

    def stat_copy(i, j):
        d = i * n_my + j
        return pltpu.make_async_remote_copy(
            src_ref=stats, dst_ref=everyone.at[me], send_sem=ssend.at[d], recv_sem=srecv.at[d],
            device_id=(lax.rem(mx + i, n_mx), lax.rem(my + j, n_my)), device_id_type=MESH,
        )

    def win_copy(kind, d):
        t = lax.rem(my + d, n_my)
        if kind == 0:
            src, dst, a = coarse, window.at[my, pl.ds(1, 2)], mx
        elif kind == 1:
            src, dst, a = coarse.at[pl.ds(0, 1)], window.at[my, pl.ds(3, 1)], mx - 1
        else:
            src, dst, a = coarse.at[pl.ds(1, 1)], window.at[my, pl.ds(0, 1)], mx + 1
        return pltpu.make_async_remote_copy(
            src_ref=src, dst_ref=dst, send_sem=wsend.at[kind, d], recv_sem=wrecv.at[kind, d],
            device_id=(a, t), device_id_type=MESH,
        )

    if rounds:
        hear(rounds - 1)
    for i, j in others:
        stat_copy(i, j).start()
    for d in range(n_my):
        if d:
            win_copy(0, d).start()

        @pl.when(low)
        def _():
            win_copy(1, d).start()

        @pl.when(high)
        def _():
            win_copy(2, d).start()
    window[my, 1:3] = coarse[...]
    everyone[me] = stats[...]

    @pl.when(jnp.logical_not(low))
    def _():
        for j in range(n_my):
            window[j, 0] = jnp.zeros_like(window[j, 0])

    @pl.when(jnp.logical_not(high))
    def _():
        for j in range(n_my):
            window[j, 3] = jnp.zeros_like(window[j, 3])

    pad[...] = jnp.zeros_like(pad)
    sent_faces(0)
    for r in (1, 2):
        fill(r)
    loaded("gain", "bias", "weight", "up")
    for d in range(n_my):
        if d:
            win_copy(0, d).wait()

        @pl.when(low)
        def _():
            win_copy(1, d).wait_send()
            win_copy(2, d).wait_recv()

        @pl.when(high)
        def _():
            win_copy(2, d).wait_send()
            win_copy(1, d).wait_recv()
    for i, j in others:
        stat_copy(i, j).wait()

    total = float(cells * group) * n
    sums = jnp.sum(everyone[...], axis=0) / total
    mean = sums[0:1]
    std = jnp.sqrt(sums[1:2] - mean * mean + norm_eps)
    both_rows = jnp.concatenate([mean, std, jnp.zeros((6, lanes), F32)], axis=0)
    both_rows = in_three(both_rows, grouped, NT)
    mean, std = both_rows[0:1], both_rows[1:2]
    g = gain[...]
    b = bias[...]
    for zw in range(4):
        for j in range(n_my):
            value = silu((window[j, zw] - mean) / std * g + b)
            if zw == 0:
                value = jnp.where(low, value, 0.0)
            if zw == 3:
                value = jnp.where(high, value, 0.0)
            for x in range(2):
                pad[1 + x, zw, 1 + 2 * j : 3 + 2 * j, :] = value[2 * x : 2 * x + 2]
    tall = 2 * n_my
    sums = jnp.zeros((4 * tall, part.shape[2]), F32)
    t = 0
    for dz in range(3):
        for dy in range(3):
            for dx in range(3):
                lhs = jnp.concatenate(
                    [pad[x + dx, z + dz, dy : dy + tall, :] for z in range(2) for x in range(2)],
                    axis=0,
                ).astype(BF)
                sums = sums + lax.dot_general(
                    lhs, weight[:, t * wide_c : (t + 1) * wide_c], (((1,), (1,)), ((), ())),
                    preferred_element_type=F32,
                )
                t += 1
    for j in range(n_my):
        for zx in range(4):
            part[j, 2 * zx : 2 * zx + 2, :] = sums[zx * tall + 2 * j : zx * tall + 2 * j + 2, :]
    copies = []
    for d in range(1, n_my):
        to = lax.rem(my + d, n_my)
        copies.append(
            pltpu.make_async_remote_copy(
                src_ref=part.at[to], dst_ref=result.at[my], send_sem=rsend.at[d],
                recv_sem=rrecv.at[d], device_id=(mx, to), device_id_type=MESH,
            )
        )
    for c in copies:
        c.start()
    result[my] = part[my]
    for c in copies:
        c.wait()

    whole = jnp.concatenate([result[j] for j in range(n_my)], axis=1)
    co = (whole + jnp.concatenate([coarse[0], coarse[1]], axis=0)).astype(BF)
    cof = co.astype(F32)
    for z in range(2):
        for y in range(2):
            q = z * 4 + y
            pair = jnp.concatenate([cof[q : q + 1], cof[q + 2 : q + 3]], axis=0)
            coarse_out[z, y] = pair.astype(BF)
    wide = dot(co, jnp.concatenate([up[k] for k in range(up.shape[0])], axis=1))
    lifted = jnp.concatenate([wide[:, p * width : (p + 1) * width] for p in range(8)], axis=0)
    hi = lifted.astype(BF)
    lo = (lifted - hi.astype(F32)).astype(BF)
    picked = [dot(g_lift, v).astype(BF) for v in (hi, lo)]
    spots = [jnp.where(is_block[o], v, jnp.zeros_like(v)) for o in range(8) for v in picked]
    sums = dot(jnp.concatenate(spots, axis=0), pair_of(same))
    for o in range(8):
        v = sums[2 * o * slots : (2 * o + 1) * slots] + sums[(2 * o + 1) * slots : (2 * o + 2) * slots]
        term[o * slots : (o + 1) * slots, :] = v

    def join(z, y):
        for x in range(HALF):
            q = (z * HALF + y) * HALF + x
            o = z // 2 * 4 + y // 2 * 2 + x // 2
            span = slice(q * slots, (q + 1) * slots)
            f = (wide_of(base, span).astype(F32) + term[o * slots : (o + 1) * slots, :]).astype(BF)
            keep(base, span, f)
            keep(sig, span, silu(f.astype(F32)).astype(BF))

    for f, y in ((0, 0), (1, HALF - 1)):
        for z in range(HALF):
            join(z, y)
        send_face(1, sig, f)
    for f, z in ((2, 0), (3, HALF - 1)):
        for y in inner:
            join(z, y)
        send_face(1, sig, f)
    for z in inner:
        for y in inner:
            join(z, y)

    def second_done(span, value):
        f = value.astype(BF)
        keep(base, span, f)
        keep(sig2, span, silu(f.astype(F32)).astype(BF))

    near_inner(1, sig, second_done)
    near_outer(1, sig)
    far_z(1, sig, second_done)
    for f in (1, 0):
        far_y(1, sig, second_done, f)
        send_face(2, sig2, f ^ 1)
    for f in (2, 3):
        send_face(2, sig2, f)

    def last_done(span, value):
        for i in range(HALF):
            at = slice(span.start + i * slots, span.start + (i + 1) * slots)
            keep(base, at, jnp.where(alive, value[i * slots : (i + 1) * slots], 0.0).astype(BF))

    near_inner(2, sig2, last_done)
    near_outer(2, sig2)
    far_z(2, sig2, last_done)
    sent_faces(1)
    for f in (1, 0):
        far_y(2, sig2, last_done, f)

    sent_faces(2)
    for g in range(slots // 16):
        for z in range(HALF):
            x = jnp.concatenate(
                [wide_of(base, pl.ds((16 * z + i) * slots + 16 * g, 16)) for i in range(16)], axis=0)
            r = dot(pair_of(swap), x).astype(BF)
            for s in range(16):
                at = (16 * g + s) * CUBES + 16 * z
                keep(fine, slice(at, at + 16), r[16 * s : 16 * s + 16])


def unfold_kernel(chans, slots, rows, coarse, sel_h, masks_h, fine_h, coarse_h, sel, masks, fine, kept, sem):
    loads = [
        pltpu.make_async_copy(a, b, sem.at[i])
        for i, (a, b) in enumerate(((sel_h, sel), (masks_h, masks)))
    ]
    for c in loads:
        c.start()
    kept[...] = coarse[...]
    for c in loads:
        c.wait()
    stores = [pltpu.make_async_copy(kept, coarse_h, sem.at[2])]
    stores[0].start()
    low64, low32 = masks[0] > 0.5, masks[1] > 0.5
    for g in range(slots // 8):
        for h in range(2):
            m = []
            for s in range(8):
                at = (8 * g + s) * CUBES + 32 * h
                m.append((rows[0, at : at + 32, :], rows[1, at : at + 32, :]))
            m = swap_blocks(m, low64, low32)
            x = jnp.concatenate([jnp.concatenate(p, axis=1) for p in m], axis=0)
            r = dot(x.T, jnp.concatenate([sel[0], sel[1]], axis=1)).astype(BF)
            fine[8 * g : 8 * g + 8, :, 256 * h : 256 * h + 256] = r.reshape(8, chans, 256)
        part = pl.ds(8 * g, 8)
        stores.append(pltpu.make_async_copy(fine.at[part], fine_h.at[part], sem.at[3 + g]))
        stores[-1].start()
    for c in stores:
        c.wait()


def local(
    features, coords, counts, neighbours, fine_weights, down_weight, up_weight, norm_gain,
    norm_bias, coarse_weight,
):
    slots, chans, _ = features.shape
    n_mx, n_my = lax.axis_size("mx"), lax.axis_size("my")
    cells = (RZ // 2) * (RY // 2) * (RX // 2)
    width = down_weight.shape[1]
    lanes = 8 * chans
    masks, sel, swap, same = constants(chans)
    n = n_mx * n_my
    sds = jax.ShapeDtypeStruct
    weight_t = coarse_weight.T
    ins = (
        counts[None, :], coords, neighbours, features, fine_weights, norm_gain[None, :],
        norm_bias[None, :], sel, swap, same, masks, down_weight, up_weight, weight_t,
    )
    held = [pltpu.VMEM(a.shape, a.dtype) for a in ins]
    held[3] = pltpu.VMEM((SIDE**3 // 128, slots, chans, 128), BF)
    held[11] = pltpu.VMEM((width // 128, down_weight.shape[0], 128), BF)
    held[12] = pltpu.VMEM((up_weight.shape[1] // 128, width, 128), BF)
    dma = pltpu.SemaphoreType.DMA
    total = slots * CUBES
    plane = slots * PLANE
    scratch = held + [
        pltpu.VMEM((2, total, 128), BF),
        pltpu.VMEM((2, total, 128), BF),
        pltpu.VMEM((2, total, 128), BF),
        pltpu.VMEM((2, total, 128), BF),
        pltpu.VMEM((2, total, 128), F32),
        pltpu.VMEM((3, 4, 2, lanes, 128), BF),
        pltpu.VMEM((2, plane, 128), BF),
        pltpu.VMEM((plane, lanes // 2), BF),
        pltpu.VMEM((plane, lanes // 2), BF),
        pltpu.VMEM((2, plane, 128), BF),
        pltpu.VMEM((3, 4, PLANE, FACE, lanes // 2), BF),
        pltpu.VMEM((3, 4, PLANE, FACE, lanes // 2), BF),
        pltpu.VMEM((8 * slots, lanes), F32),
        pltpu.VMEM((2, cells // 2, width), F32),
        pltpu.VMEM((2, 128), F32),
        pltpu.VMEM((n_my, 4, cells // 2, width), F32),
        pltpu.VMEM((n, 2, 128), F32),
        pltpu.VMEM((4, 4, -(-(2 * n_my + 2) // 8) * 8, width), F32),
        pltpu.VMEM((n_my, cells, coarse_weight.shape[1]), F32),
        pltpu.VMEM((n_my, cells, coarse_weight.shape[1]), F32),
        dma((64,)), dma((3, 4)), dma((3, 4)), dma((n,)), dma((n,)),
        dma((3, n_my)), dma((3, n_my)), dma((n_my,)), dma((n_my,)),
        pltpu.SemaphoreType.REGULAR((max(1, (n_mx - 1).bit_length()), 2)),
    ]
    small = (RZ // 2, RY // 2, RX // 2, width)
    rows, coarse = pl.pallas_call(
        functools.partial(level_kernel, slots, chans, cells),
        out_shape=(pltpu.VMEM((2, total, 128), BF), pltpu.VMEM(small, BF)),
        in_specs=[HBM] * len(ins),
        out_specs=(VM, VM),
        scratch_shapes=scratch,
        compiler_params=pltpu.CompilerParams(collective_id=0, has_side_effects=True),
    )(*ins)
    return pl.pallas_call(
        functools.partial(unfold_kernel, chans, slots),
        out_shape=(sds(features.shape, BF), sds(small, BF)),
        in_specs=[VM, VM, HBM, HBM],
        out_specs=(HBM, HBM),
        scratch_shapes=[
            pltpu.VMEM(sel.shape, BF), pltpu.VMEM(masks.shape, BF), pltpu.VMEM(features.shape, BF),
            pltpu.VMEM(small, BF), dma((3 + slots // 8,)),
        ],
    )(*[pltpu.with_memory_space_constraint(a, pltpu.VMEM) for a in (rows, coarse)], sel, masks)


def solution(mesh):
    in_specs = (
        P(("mx", "my"), None, None),
        P(None, ("mx", "my")),
        P(("mx", "my")),
        P(None, ("mx", "my")),
        P(),
        P(),
        P(),
        P(),
        P(),
        P(None, "my"),
    )
    out_specs = (P(("mx", "my"), None, None), P("mx", "my", None, None))
    return jax.shard_map(local, mesh=mesh, in_specs=in_specs, out_specs=out_specs, check_vma=False)
```

```python
import functools

import jax
import jax.numpy as jnp
import numpy as np
from jax import lax
from jax.experimental import pallas as pl
from jax.experimental.pallas import tpu as pltpu
from jax.sharding import PartitionSpec as P

GROUPS = 32
SIDE = 8
RZ = 4
RY = 4
RX = 4
HALF = SIDE // 2
CUBES = HALF**3
PLANE = HALF**2
FACE = 16
norm_eps = 1e-05
MESH = pl.DeviceIdType.MESH
BF = jnp.bfloat16
F32 = jnp.float32
I32 = jnp.int32
VM = pl.BlockSpec(memory_space=pltpu.VMEM)
HBM = pl.BlockSpec(memory_space=pl.ANY)
NN = (((1,), (0,)), ((), ()))
NT = (((1,), (1,)), ((), ()))
TN = (((0,), (0,)), ((), ()))


def constants(chans):
    lane = np.arange(4 * chans)
    masks = np.stack([lane < 2 * chans, lane // chans % 2 == 0])
    masks = np.broadcast_to(masks[:, None, :], (2, 32, 4 * chans))
    sel = np.zeros((256, 256))
    for w in range(8):
        vy, vz, vx = w >> 2, w >> 1 & 1, w & 1
        for i in range(32):
            z, y, x = i // 16 * 2 + vz, i // 4 % 4 * 2 + vy, i % 4 * 2 + vx
            sel[w * 32 + i, (z * SIDE + y) * SIDE + x] = 1
    swap = np.zeros((256, 256))
    for i in range(16):
        for s in range(16):
            swap[i * 16 + s, s * 16 + i] = 1
    wide = np.arange(8 * chans)
    same = wide[:, None] % chans == wide[None, :] % chans
    as_bf = lambda a: jnp.asarray(np.asarray(a, np.float32), BF)
    halved = lambda a: as_bf(np.stack([a[:, :128], a[:, 128:]]))
    return as_bf(masks), halved(sel), halved(swap), halved(same)


def dot(a, b, dims=NN):
    return lax.dot_general(a, b, dims, preferred_element_type=F32)


def wide_of(ref, *at):
    return jnp.concatenate([ref[at[:-1] + (t,) + at[-1:]] for t in range(2)], axis=1)


def keep(ref, span, value):
    for t in range(2):
        ref[t, span, :] = value[:, 128 * t : 128 * t + 128]


def silu(x):
    h = 0.5 * x
    return h * jnp.tanh(h) + h


def swap_blocks(parts, low64, low32):
    left, right = [p[0] for p in parts], [p[1] for p in parts]
    m = [(left[i], left[i + 4]) for i in range(4)] + [(right[i], right[i + 4]) for i in range(4)]
    for bit, low, up, down in ((2, low64, 64, 64), (1, low32, 32, 96)):
        n = list(m)
        for j in range(8):
            if j & bit:
                continue
            a, b = m[j], m[j | bit]
            n[j] = tuple(jnp.where(low, a[t], pltpu.roll(b[t], up, 1)) for t in range(2))
            n[j | bit] = tuple(jnp.where(low, pltpu.roll(a[t], down, 1), b[t]) for t in range(2))
        m = n
    return m


def level_kernel(
    slots, chans, cells,
    counts_h, coords_h, neighbours_h, feat_h, fine_w_h, gain_h, bias_h, sel_h, swap_h, same_h,
    masks_h, down_h, up_h, weight_h,
    fine, coarse_out, sel_out, masks_out,
    counts, coords, neighbours, feat, fine_w, gain, bias, sel, swap, same, masks, down, up, weight,
    blocks, base, sig, sig2, acc, wts, gx, gyp, gym, gz, faces, halo, term,
    coarse, stats, window, everyone, pad, part, result,
    load, fsend, frecv, ssend, srecv, wsend, wrecv, rsend, rrecv, ready,
):
    n_mx, n_my = lax.axis_size("mx"), lax.axis_size("my")
    mx, my = lax.axis_index("mx"), lax.axis_index("my")
    n = n_mx * n_my
    me = mx * n_my + my
    width = 8 * chans
    side = width // 2
    wide_c = gain.shape[1]

    chunks = feat.shape[0]
    order = [
        ("feat", feat_h.at[:, :, pl.ds(128 * k, 128)], feat.at[k]) for k in range(chunks)
    ]
    order += [
        ("sel", sel_h, sel), ("masks", masks_h, masks), ("swap", swap_h, swap),
        ("fine_w", fine_w_h, fine_w), ("counts", counts_h, counts),
        ("coords", coords_h, coords), ("neighbours", neighbours_h, neighbours),
    ]
    late = [("same", same_h, same), ("gain", gain_h, gain), ("bias", bias_h, bias)]
    late += [("down", down_h.at[:, pl.ds(128 * k, 128)], down.at[k]) for k in range(down.shape[0])]
    late += [("weight", weight_h, weight)]
    late += [("up", up_h.at[:, pl.ds(128 * k, 128)], up.at[k]) for k in range(up.shape[0])]
    copies = [
        (name, pltpu.make_async_copy(a, b, load.at[i]))
        for i, (name, a, b) in enumerate(order + late)
    ]
    for _, c in copies[: len(order)]:
        c.start()

    def loaded(*names):
        for name, c in copies:
            if name in names:
                c.wait()

    barrier = pltpu.get_barrier_semaphore()
    low, high = mx > 0, mx < n_mx - 1

    def greet(a, b):
        pl.semaphore_signal(barrier, inc=1, device_id=(a, b), device_id_type=MESH)

    @pl.when(low)
    def _():
        greet(mx - 1, my)

    @pl.when(high)
    def _():
        greet(mx + 1, my)

    for d in range(1, n_my):
        greet(mx, lax.rem(my + d, n_my))

    def entered():
        pl.semaphore_wait(barrier, n_my - 1 + low.astype(I32) + high.astype(I32))

    rounds = max(n_mx - 1, 0).bit_length()

    def tell(k):
        @pl.when(mx + 2**k < n_mx)
        def _():
            pl.semaphore_signal(
                ready.at[k, 0], inc=1, device_id=(mx + 2**k, my), device_id_type=MESH
            )

        @pl.when(mx - 2**k >= 0)
        def _():
            pl.semaphore_signal(
                ready.at[k, 1], inc=1, device_id=(mx - 2**k, my), device_id_type=MESH
            )

    def hear(k):
        @pl.when(mx - 2**k >= 0)
        def _():
            pl.semaphore_wait(ready.at[k, 0], 1)

        @pl.when(mx + 2**k < n_mx)
        def _():
            pl.semaphore_wait(ready.at[k, 1], 1)

    loaded("feat", "sel", "masks")
    for _, c in copies[len(order) :]:
        c.start()

    def at_cube(q):
        return slice(q * slots, (q + 1) * slots)

    def rows(ref, q):
        return wide_of(ref, at_cube(q))

    def left(ref, q):
        return ref[0, at_cube(q), :]

    def right(ref, q):
        return ref[1, at_cube(q), :]

    def pair_of(ref):
        return jnp.concatenate([ref[0], ref[1]], axis=1)

    low64, low32 = masks[0] > 0.5, masks[1] > 0.5
    zero = jnp.zeros((slots, side), BF)

    for g in range(slots // 8):
        for h in range(2):
            x = jnp.concatenate(
                [feat[2 * h + t, 8 * g : 8 * g + 8].reshape(8 * chans, 128) for t in range(2)], axis=1
            )
            r = dot(pair_of(sel), x, NT).astype(BF)
            m = [(r[32 * w : 32 * w + 32, :side], r[32 * w : 32 * w + 32, side:]) for w in range(8)]
            m = swap_blocks(m, low64, low32)
            for s in range(8):
                at = (8 * g + s) * CUBES + 32 * h
                blocks[0, at : at + 32, :] = m[s][0]
                blocks[1, at : at + 32, :] = m[s][1]
    loaded("swap")
    for z in range(HALF):
        for g in range(slots // 16):
            x = jnp.concatenate(
                [wide_of(blocks, pl.ds((16 * g + s) * CUBES + 16 * z, 16)) for s in range(16)], axis=0)
            r = dot(pair_of(swap), x)
            rb = r.astype(BF)
            rs = silu(r).astype(BF)
            for i in range(16):
                at = (16 * z + i) * slots + 16 * g
                keep(base, slice(at, at + 16), rb[16 * i : 16 * i + 16])
                keep(sig, slice(at, at + 16), rs[16 * i : 16 * i + 16])

    loaded("counts", "coords", "neighbours")
    def one_hot(row, count):
        return (lax.broadcasted_iota(I32, (count, slots), 0) == row).astype(F32).astype(BF)

    eye = (
        lax.broadcasted_iota(I32, (slots, slots), 0) == lax.broadcasted_iota(I32, (slots, slots), 1)
    ).astype(F32).astype(BF)

    def turned(table):
        return dot(eye, table, NT).astype(BF)

    pz = coords[0:1, :] - mx * RZ
    py = coords[1:2, :] - my * RY
    px = coords[2:3, :]
    live = lax.broadcasted_iota(I32, (1, slots), 1) < counts[...]

    def link(d):
        g = neighbours[d : d + 1, :]
        here = g - me * slots
        inside = (here >= 0) & (here < slots)
        far = slots + (pz if d < 4 else py) * RX + px
        return jnp.where(g < 0, -1, jnp.where(inside, here, far))

    halo_rows = slots + FACE
    g_x = turned(jnp.concatenate([one_hot(link(d), slots) for d in (0, 1)], axis=0))
    g_yp = turned(one_hot(link(2), halo_rows))
    g_ym = turned(one_hot(link(3), halo_rows))
    g_z = turned(jnp.concatenate([one_hot(link(d), halo_rows) for d in (4, 5)], axis=0))
    edge = (
        jnp.where(live & (py == 0), pz * RX + px, -1),
        jnp.where(live & (py == RY - 1), pz * RX + px, -1),
        jnp.where(live & (pz == 0), py * RX + px, -1),
        jnp.where(live & (pz == RZ - 1), py * RX + px, -1),
    )
    g_edge = [one_hot(e, FACE) for e in edge]
    cell = (pz // 2 * 2 + px // 2) * 2 + py // 2
    place = pz % 2 * 4 + py % 2 * 2 + px % 2
    g_cell = one_hot(jnp.where(live, place * cells + cell, -1), 8 * cells)
    g_lift = turned(g_cell)
    alive = dot(
        jnp.where(live, eye.astype(F32), 0.0).astype(BF), jnp.ones((slots, width), BF)
    ) > 0.5

    peers = (
        (my > 0, mx, my - 1),
        (my < n_my - 1, mx, my + 1),
        (mx > 0, mx - 1, my),
        (mx < n_mx - 1, mx + 1, my),
    )

    def face_copy(r, f):
        _, a, b = peers[f]
        return pltpu.make_async_remote_copy(
            src_ref=faces.at[r, f], dst_ref=halo.at[r, f], send_sem=fsend.at[r, f],
            recv_sem=frecv.at[r, f], device_id=(a, b), device_id_type=MESH,
        )

    low64_face = low64[:FACE]

    def send_face(r, src, f):
        for k in range(PLANE // 2):
            a, x = k // 2, k % 2 * 2
            if f < 2:
                part_of = left if f == 0 else right
                q = a * PLANE + (0 if f == 0 else HALF - 1) * HALF + x
                pair = jnp.concatenate([part_of(src, q), part_of(src, q + 1)], axis=1)
                v = dot(g_edge[f], pair).astype(BF)
                faces[r, f, 2 * k] = v[:, :side]
                faces[r, f, 2 * k + 1] = v[:, side:]
            else:
                q = (0 if f == 2 else HALF - 1) * PLANE + a * HALF + x
                va = dot(g_edge[f], rows(src, q)).astype(BF)
                vb = dot(g_edge[f], rows(src, q + 1)).astype(BF)
                for t in range(2):
                    own = va[:, t * side : (t + 1) * side]
                    other = pltpu.roll(vb[:, t * side : (t + 1) * side], 64, 1)
                    if f == 2:
                        faces[r, f, 2 * k + t] = jnp.where(low64_face, own, other)
                    else:
                        faces[r, f, 2 * k + t] = jnp.where(low64_face, other, own)

        @pl.when(peers[f][0])
        def _():
            face_copy(r, f).start()

        @pl.when(jnp.logical_not(peers[f ^ 1][0]))
        def _():
            halo[r, f] = jnp.zeros_like(halo[r, f])

    def sent_faces(r):
        for f in range(4):
            @pl.when(peers[f][0])
            def _():
                face_copy(r, f).wait_send()

    def take_face(r, f):
        @pl.when(peers[f ^ 1][0])
        def _():
            face_copy(r, f).wait_recv()

    def z_halo(r, f, y, x):
        k = 2 * (y * 2 + x // 2)
        v = [halo[r, f, k + t] for t in range(2)]
        if x % 2:
            v = [pltpu.roll(a, 64, 1) for a in v]
        none = jnp.zeros_like(v[0])
        if f == 2:
            v = [jnp.where(low64_face, a, none) for a in v]
        else:
            v = [jnp.where(low64_face, none, a) for a in v]
        return jnp.concatenate(v, axis=1)

    def both(low, a, b):
        return jnp.concatenate([jnp.where(low, a[t], b[t]) for t in range(2)], axis=1)

    def halves(ref, q):
        return left(ref, q), right(ref, q)

    def run(ref, z, y):
        at = (z * HALF + y) * HALF * slots
        return wide_of(ref, slice(at, at + HALF * slots))

    def spans(runs):
        return [
            slice((z * HALF + y) * HALF * slots, (z * HALF + y + 1) * HALF * slots)
            for z, y in runs
        ]

    def stack(parts):
        return jnp.concatenate(parts, axis=0)

    def x_taps(src, runs):
        taps = []
        for z, y in runs:
            edge_of = halves(gx, z * HALF + y)
            for x in range(HALF):
                q = (z * HALF + y) * HALF + x
                after = halves(src, q + 1) if x < HALF - 1 else edge_of
                before = halves(src, q - 1) if x > 0 else edge_of
                taps.append(both(low32, after, before))
        return stack(taps)

    def y_taps(src, runs):
        taps = []
        for z, y in runs:
            for x in range(HALF):
                q = (z * HALF + y) * HALF + x
                zx = z * HALF + x
                span = slice(zx * slots, (zx + 1) * slots)
                after = left(src, q + HALF) if y < HALF - 1 else gyp[span, :]
                before = right(src, q - HALF) if y > 0 else gym[span, :]
                taps.append(jnp.concatenate([after, before], axis=1))
        return stack(taps)

    def z_taps(src, runs):
        taps = []
        for z, y in runs:
            for x in range(HALF):
                q = (z * HALF + y) * HALF + x
                edge_of = halves(gz, y * HALF + x)
                after = halves(src, q + PLANE) if z < HALF - 1 else edge_of
                before = halves(src, q - PLANE) if z > 0 else edge_of
                taps.append(both(low64, after, before))
        return stack(taps)

    def passes(r, src, runs, kinds):
        taps = {
            0: lambda: stack([run(src, z, y) for z, y in runs]),
            1: lambda: x_taps(src, runs),
            2: lambda: y_taps(src, runs),
            3: lambda: z_taps(src, runs),
        }
        total = None
        for k in kinds:
            v = dot(taps[k](), jnp.concatenate([wts[r, k, 0], wts[r, k, 1]], axis=1))
            total = v if total is None else total + v
        return total

    def add_to(ref, runs, value):
        tall = HALF * slots
        return [
            (span, wide_of(ref, span).astype(F32) + value[i * tall : (i + 1) * tall])
            for i, span in enumerate(spans(runs))
        ]

    inner, outer = range(1, HALF - 1), (0, HALF - 1)

    def near_inner(r, src, finish):
        for zy in range(PLANE):
            first, last = halves(src, zy * HALF), halves(src, zy * HALF + HALF - 1)
            pair = jnp.concatenate(
                [both(low32, first, (zero, zero)), both(low32, (zero, zero), last)], axis=0
            )
            keep(gx, at_cube(zy), dot(g_x, pair).astype(BF))
        for z in outer:
            runs = [(z, y) for y in inner]
            for span, v in add_to(base, runs, passes(r, src, runs, (0, 1, 2))):
                keep(acc, span, v)
        for z in inner:
            runs = [(z, y) for y in inner]
            for span, v in add_to(base, runs, passes(r, src, runs, (0, 1, 2, 3))):
                finish(span, v)

    def near_outer(r, src):
        for y in outer:
            for zs, kinds in ((inner, (0, 1, 3)), (outer, (0, 1))):
                runs = [(z, y) for z in zs]
                for span, v in add_to(base, runs, passes(r, src, runs, kinds)):
                    keep(acc, span, v)

    def gather_z(r, src):
        for f in (2, 3):
            take_face(r, f)
        for y in range(HALF):
            for x in range(HALF):
                i = y * HALF + x
                first, last = halves(src, i), halves(src, (HALF - 1) * PLANE + i)
                both_z = jnp.concatenate(
                    [both(low64, first, (zero, zero)), z_halo(r, 2, y, x),
                     both(low64, (zero, zero), last), z_halo(r, 3, y, x)], axis=0,
                )
                keep(gz, at_cube(i), dot(g_z, both_z).astype(BF))

    def gather_y(r, src, f):
        part_of, table, out = ((left, g_yp, gyp), (right, g_ym, gym))[f]
        for k in range(PLANE // 2):
            z, x = k // 2, k % 2 * 2
            q = z * PLANE + (0 if f == 0 else HALF - 1) * HALF + x
            own = jnp.concatenate([part_of(src, q), part_of(src, q + 1)], axis=1)
            got = jnp.concatenate([halo[r, f, 2 * k], halo[r, f, 2 * k + 1]], axis=1)
            v = dot(table, jnp.concatenate([own, got], axis=0)).astype(BF)
            out[2 * k * slots : (2 * k + 1) * slots, :] = v[:, :side]
            out[(2 * k + 1) * slots : (2 * k + 2) * slots, :] = v[:, side:]

    def more(r, src, runs, kind, finish=None):
        for span, v in add_to(acc, runs, passes(r, src, runs, (kind,))):
            if finish is None:
                keep(acc, span, v)
            else:
                finish(span, v)

    def far_z(r, src, finish):
        gather_z(r, src)
        for z in outer:
            more(r, src, [(z, y) for y in inner], 3, finish)
        for y in outer:
            more(r, src, [(z, y) for z in outer], 3)

    def far_y(r, src, finish, f):
        take_face(r, f)
        gather_y(r, src, f)
        y = HALF - 1 if f == 0 else 0
        for zs in (range(HALF // 2), range(HALF // 2, HALF)):
            more(r, src, [(z, y) for z in zs], 2, finish)

    lane_block = lax.broadcasted_iota(I32, (slots, width), 1) // chans
    block_f = lane_block.astype(F32).astype(BF)
    spread = (
        lax.broadcasted_iota(I32, (chans, width), 0)
        == lax.broadcasted_iota(I32, (chans, width), 1) % chans
    ).astype(F32).astype(BF)
    none = jnp.zeros((chans, width), BF)
    is_block = [block_f == float(w) for w in range(8)]

    def fit(r, k, span, v):
        for t in range(2):
            wts[r, k, t, span, :] = v[:, side * t : side * t + side]

    def fill(r):
        t = dot(fine_w[r], spread, TN).astype(BF)
        t = [t[i * chans : (i + 1) * chans] for i in range(7)]
        for w in range(8):
            span = slice(w * chans, (w + 1) * chans)
            vy, vz, vx = w >> 2, w >> 1 & 1, w & 1
            v = jnp.where(is_block[w], t[0], none)
            v = jnp.where(is_block[w ^ 1], t[1] if vx else t[2], v)
            v = jnp.where(is_block[w ^ 4], t[3] if vy else t[4], v)
            v = jnp.where(is_block[w ^ 2], t[5] if vz else t[6], v)
            fit(r, 0, span, v)
            fit(r, 1, span, jnp.where(is_block[w ^ 1], t[2] if vx else t[1], none))
            fit(r, 2, span, jnp.where(is_block[w ^ 4], t[4] if vy else t[3], none))
            fit(r, 3, span, jnp.where(is_block[w ^ 2], t[6] if vz else t[5], none))

    def first_done(span, value):
        keep(base, span, value.astype(BF))

    entered()
    for f in (0, 1, 2, 3):
        send_face(0, sig, f)
    if rounds:
        tell(0)
    loaded("fine_w")
    fill(0)
    near_inner(0, sig, first_done)
    near_outer(0, sig)
    for k in range(1, rounds):
        hear(k - 1)
        tell(k)
        if k == 1:
            far_z(0, sig, first_done)
    if rounds < 2:
        far_z(0, sig, first_done)
    far_y(0, sig, first_done, 1)
    send_face(1, base, 0)
    far_y(0, sig, first_done, 0)
    send_face(1, base, 1)

    sums = []
    for o in range(8):
        total = None
        for i in range(8):
            z, y, x = (o >> 2) * 2 + (i >> 2), (o >> 1 & 1) * 2 + (i >> 1 & 1), (o & 1) * 2 + (i & 1)
            v = rows(base, (z * HALF + y) * HALF + x).astype(F32)
            total = v if i == 0 else total + v
        hi = total.astype(BF)
        sums += [hi, (total - hi.astype(F32)).astype(BF)]
    loaded("same")
    sums = dot(jnp.concatenate(sums, axis=0), pair_of(same))
    pooled = jnp.zeros((slots, width), F32)
    for o in range(8):
        v = sums[2 * o * slots : (2 * o + 1) * slots] + sums[(2 * o + 1) * slots : (2 * o + 2) * slots]
        pooled = jnp.where(lane_block == o, v, pooled)
    pooled = (pooled * (1.0 / HALF**3)).astype(BF)
    flat = dot(g_cell, pooled).astype(BF)
    loaded("down")
    ci = jnp.zeros((cells, wide_c), F32)
    for p in range(8):
        ci = ci + jnp.dot(
            flat[p * cells : (p + 1) * cells],
            jnp.concatenate([down[t, p * width : (p + 1) * width, :] for t in range(down.shape[0])], axis=1),
            preferred_element_type=F32,
        )
    layer = cells // 2
    coarse[0] = ci[:layer]
    coarse[1] = ci[layer:]
    group = wide_c // GROUPS
    lanes = stats.shape[1]

    def split(v):
        a = v.astype(BF)
        rest = v - a.astype(F32)
        b = rest.astype(BF)
        return [a, b, (rest - b.astype(F32)).astype(BF)]

    def in_three(v, table, dims):
        parts = dot(jnp.concatenate([p.astype(F32) for p in split(v)], axis=0).astype(BF), table, dims)
        tall = v.shape[0]
        return parts[:tall] + (parts[tall : 2 * tall] + parts[2 * tall :])

    grouped = (
        lax.broadcasted_iota(I32, (wide_c, lanes), 0) // group
        == lax.broadcasted_iota(I32, (wide_c, lanes), 1)
    ).astype(F32).astype(BF)
    rest = jnp.zeros((6, wide_c), F32)
    local = jnp.concatenate(
        [jnp.sum(ci, axis=0, keepdims=True), jnp.sum(ci * ci, axis=0, keepdims=True), rest], axis=0
    )
    stats[...] = in_three(local, grouped, NN)[0:2]

    offsets = sorted(range(n_mx), key=lambda i: -min(i, n_mx - i))
    others = [(i, j) for i in offsets for j in range(n_my) if i or j]

    def stat_copy(i, j):
        d = i * n_my + j
        return pltpu.make_async_remote_copy(
            src_ref=stats, dst_ref=everyone.at[me], send_sem=ssend.at[d], recv_sem=srecv.at[d],
            device_id=(lax.rem(mx + i, n_mx), lax.rem(my + j, n_my)), device_id_type=MESH,
        )

    def win_copy(kind, d):
        t = lax.rem(my + d, n_my)
        if kind == 0:
            src, dst, a = coarse, window.at[my, pl.ds(1, 2)], mx
        elif kind == 1:
            src, dst, a = coarse.at[pl.ds(0, 1)], window.at[my, pl.ds(3, 1)], mx - 1
        else:
            src, dst, a = coarse.at[pl.ds(1, 1)], window.at[my, pl.ds(0, 1)], mx + 1
        return pltpu.make_async_remote_copy(
            src_ref=src, dst_ref=dst, send_sem=wsend.at[kind, d], recv_sem=wrecv.at[kind, d],
            device_id=(a, t), device_id_type=MESH,
        )

    if rounds:
        hear(rounds - 1)
    for i, j in others:
        stat_copy(i, j).start()
    for d in range(n_my):
        if d:
            win_copy(0, d).start()

        @pl.when(low)
        def _():
            win_copy(1, d).start()

        @pl.when(high)
        def _():
            win_copy(2, d).start()
    window[my, 1:3] = coarse[...]
    everyone[me] = stats[...]

    @pl.when(jnp.logical_not(low))
    def _():
        for j in range(n_my):
            window[j, 0] = jnp.zeros_like(window[j, 0])

    @pl.when(jnp.logical_not(high))
    def _():
        for j in range(n_my):
            window[j, 3] = jnp.zeros_like(window[j, 3])

    pad[...] = jnp.zeros_like(pad)
    sel_out[...] = sel[...]
    masks_out[...] = masks[...]
    sent_faces(0)
    for r in (1, 2):
        fill(r)
    loaded("gain", "bias", "weight", "up")
    for d in range(n_my):
        if d:
            win_copy(0, d).wait()

        @pl.when(low)
        def _():
            win_copy(1, d).wait_send()
            win_copy(2, d).wait_recv()

        @pl.when(high)
        def _():
            win_copy(2, d).wait_send()
            win_copy(1, d).wait_recv()
    for i, j in others:
        stat_copy(i, j).wait()

    total = float(cells * group) * n
    sums = jnp.sum(everyone[...], axis=0) / total
    mean = sums[0:1]
    std = jnp.sqrt(sums[1:2] - mean * mean + norm_eps)
    both_rows = jnp.concatenate([mean, std, jnp.zeros((6, lanes), F32)], axis=0)
    both_rows = in_three(both_rows, grouped, NT)
    mean, std = both_rows[0:1], both_rows[1:2]
    g = gain[...]
    b = bias[...]
    for zw in range(4):
        for j in range(n_my):
            value = silu((window[j, zw] - mean) / std * g + b)
            if zw == 0:
                value = jnp.where(low, value, 0.0)
            if zw == 3:
                value = jnp.where(high, value, 0.0)
            for x in range(2):
                pad[1 + x, zw, 1 + 2 * j : 3 + 2 * j, :] = value[2 * x : 2 * x + 2]
    tall = 2 * n_my
    sums = jnp.zeros((4 * tall, part.shape[2]), F32)
    t = 0
    for dz in range(3):
        for dy in range(3):
            for dx in range(3):
                lhs = jnp.concatenate(
                    [pad[x + dx, z + dz, dy : dy + tall, :] for z in range(2) for x in range(2)],
                    axis=0,
                ).astype(BF)
                sums = sums + lax.dot_general(
                    lhs, weight[:, t * wide_c : (t + 1) * wide_c], (((1,), (1,)), ((), ())),
                    preferred_element_type=F32,
                )
                t += 1
    for j in range(n_my):
        for zx in range(4):
            part[j, 2 * zx : 2 * zx + 2, :] = sums[zx * tall + 2 * j : zx * tall + 2 * j + 2, :]
            above, below = zx * tall + 2 * min(j + 1, n_my - 1), zx * tall + 2 * max(j - 1, 0) + 1
            part[j, cells + zx : cells + zx + 1, :] = sums[above : above + 1, :]
            part[j, cells + 4 + zx : cells + 5 + zx, :] = sums[below : below + 1, :]
    copies = []
    for d in range(1, n_my):
        to = lax.rem(my + d, n_my)
        copies.append(
            pltpu.make_async_remote_copy(
                src_ref=part.at[to], dst_ref=result.at[my], send_sem=rsend.at[d],
                recv_sem=rrecv.at[d], device_id=(mx, to), device_id_type=MESH,
            )
        )
    for c in copies:
        c.start()
    result[my] = part[my]
    for c in copies:
        c.wait()

    whole = jnp.concatenate([result[j] for j in range(n_my)], axis=1)
    above, below = jnp.minimum(my + 1, n_my - 1), jnp.maximum(my - 1, 0)
    beside = [window[above, 1], window[above, 2], window[below, 1], window[below, 2]]
    beside = [
        v[r : r + 1] for i, v in enumerate(beside) for r in ((0, 2) if i < 2 else (1, 3))
    ]
    co = (whole + jnp.concatenate([coarse[0], coarse[1]] + beside, axis=0)).astype(BF)
    cof = co.astype(F32)
    for z in range(2):
        for y in range(2):
            q = z * 4 + y
            pair = jnp.concatenate([cof[q : q + 1], cof[q + 2 : q + 3]], axis=0)
            coarse_out[z, y] = pair.astype(BF)
    wide = dot(co, jnp.concatenate([up[k] for k in range(up.shape[0])], axis=1))
    def in_two(v):
        hi = v.astype(BF)
        return hi, (v - hi.astype(F32)).astype(BF)

    def lifted(at):
        return jnp.concatenate(
            [wide[at : at + cells, p * width : (p + 1) * width] for p in range(8)], axis=0
        )

    picked = [dot(g_lift, v).astype(BF) for v in in_two(lifted(0))]
    spots = [jnp.where(is_block[o], v, jnp.zeros_like(v)) for o in range(8) for v in picked]

    k = lax.broadcasted_iota(I32, (2 * FACE, 8 * cells), 0)
    down_side = k // FACE
    kz, kx = k % FACE // RX, k % RX
    row = (kz % 2 * 4 + down_side * 2 + kx % 2) * cells + down_side * 4 + kz // 2 * 2 + kx // 2
    g_halo = (lax.broadcasted_iota(I32, (2 * FACE, 8 * cells), 1) == row).astype(F32).astype(BF)
    picked = [dot(g_halo, v).astype(BF) for v in in_two(lifted(cells))]
    for zx in range(4):
        for v in picked:
            for f in range(2):
                o = zx // 2 * 4 + f * 2 + zx % 2
                v_f = v[f * FACE : (f + 1) * FACE]
                spots.append(jnp.where(is_block[o][:FACE], v_f, jnp.zeros_like(v_f)))
    sums = dot(jnp.concatenate(spots, axis=0), pair_of(same))
    for o in range(8):
        v = sums[2 * o * slots : (2 * o + 1) * slots] + sums[(2 * o + 1) * slots : (2 * o + 2) * slots]
        term[o * slots : (o + 1) * slots, :] = v

    def join(z, y):
        for x in range(HALF):
            q = (z * HALF + y) * HALF + x
            o = z // 2 * 4 + y // 2 * 2 + x // 2
            span = slice(q * slots, (q + 1) * slots)
            f = (wide_of(base, span).astype(F32) + term[o * slots : (o + 1) * slots, :]).astype(BF)
            keep(base, span, f)
            keep(sig, span, silu(f.astype(F32)).astype(BF))

    for f, z in ((2, 0), (3, HALF - 1)):
        for y in range(HALF):
            join(z, y)
        send_face(1, sig, f)
    for z in inner:
        for y in range(HALF):
            join(z, y)
    for f in range(2):
        take_face(1, f)
        for zx in range(PLANE):
            at = 16 * slots + (zx // 8 * 2 + zx % 4 // 2) * 4 * FACE + f * FACE
            lift = sums[at : at + FACE, :side] + sums[at + 2 * FACE : at + 3 * FACE, :side]
            v = (halo[1, f, zx].astype(F32) + lift).astype(BF)
            halo[1, f, zx] = silu(v.astype(F32)).astype(BF)

    def second_done(span, value):
        f = value.astype(BF)
        keep(base, span, f)
        keep(sig2, span, silu(f.astype(F32)).astype(BF))

    near_inner(1, sig, second_done)
    near_outer(1, sig)
    for f, y in ((1, 0), (0, HALF - 1)):
        gather_y(1, sig, f)
        more(1, sig, [(z, y) for z in inner], 2, second_done)
        more(1, sig, [(z, y) for z in outer], 2)
    gather_z(1, sig)
    for f, y in ((0, 0), (1, HALF - 1)):
        more(1, sig, [(z, y) for z in outer], 3, second_done)
        send_face(2, sig2, f)
    for f, z in ((2, 0), (3, HALF - 1)):
        more(1, sig, [(z, y) for y in inner], 3, second_done)
        send_face(2, sig2, f)

    def last_done(span, value):
        for i in range(HALF):
            at = slice(span.start + i * slots, span.start + (i + 1) * slots)
            keep(base, at, jnp.where(alive, value[i * slots : (i + 1) * slots], 0.0).astype(BF))

    near_inner(2, sig2, last_done)
    near_outer(2, sig2)
    far_z(2, sig2, last_done)
    sent_faces(1)
    for f in (1, 0):
        far_y(2, sig2, last_done, f)

    sent_faces(2)
    for g in range(slots // 16):
        for z in range(HALF):
            x = jnp.concatenate(
                [wide_of(base, pl.ds((16 * z + i) * slots + 16 * g, 16)) for i in range(16)], axis=0)
            r = dot(pair_of(swap), x).astype(BF)
            for s in range(16):
                at = (16 * g + s) * CUBES + 16 * z
                keep(fine, slice(at, at + 16), r[16 * s : 16 * s + 16])


def unfold_kernel(chans, slots, rows, coarse, sel, masks, fine_h, coarse_h, fine, kept, sem):
    kept[...] = coarse[...]
    stores = [pltpu.make_async_copy(kept, coarse_h, sem.at[0])]
    stores[0].start()
    low64, low32 = masks[0] > 0.5, masks[1] > 0.5
    for g in range(slots // 8):
        for h in range(2):
            m = []
            for s in range(8):
                at = (8 * g + s) * CUBES + 32 * h
                m.append((rows[0, at : at + 32, :], rows[1, at : at + 32, :]))
            m = swap_blocks(m, low64, low32)
            x = jnp.concatenate([jnp.concatenate(p, axis=1) for p in m], axis=0)
            r = dot(x.T, jnp.concatenate([sel[0], sel[1]], axis=1)).astype(BF)
            fine[8 * g : 8 * g + 8, :, 256 * h : 256 * h + 256] = r.reshape(8, chans, 256)
        part = pl.ds(8 * g, 8)
        stores.append(pltpu.make_async_copy(fine.at[part], fine_h.at[part], sem.at[1 + g]))
        stores[-1].start()
    for c in stores:
        c.wait()


def local(
    features, coords, counts, neighbours, fine_weights, down_weight, up_weight, norm_gain,
    norm_bias, coarse_weight,
):
    slots, chans, _ = features.shape
    n_mx, n_my = lax.axis_size("mx"), lax.axis_size("my")
    cells = (RZ // 2) * (RY // 2) * (RX // 2)
    width = down_weight.shape[1]
    lanes = 8 * chans
    masks, sel, swap, same = constants(chans)
    n = n_mx * n_my
    sds = jax.ShapeDtypeStruct
    weight_t = coarse_weight.T
    ins = (
        counts[None, :], coords, neighbours, features, fine_weights, norm_gain[None, :],
        norm_bias[None, :], sel, swap, same, masks, down_weight, up_weight, weight_t,
    )
    held = [pltpu.VMEM(a.shape, a.dtype) for a in ins]
    held[3] = pltpu.VMEM((SIDE**3 // 128, slots, chans, 128), BF)
    held[11] = pltpu.VMEM((width // 128, down_weight.shape[0], 128), BF)
    held[12] = pltpu.VMEM((up_weight.shape[1] // 128, width, 128), BF)
    dma = pltpu.SemaphoreType.DMA
    total = slots * CUBES
    plane = slots * PLANE
    scratch = held + [
        pltpu.VMEM((2, total, 128), BF),
        pltpu.VMEM((2, total, 128), BF),
        pltpu.VMEM((2, total, 128), BF),
        pltpu.VMEM((2, total, 128), BF),
        pltpu.VMEM((2, total, 128), F32),
        pltpu.VMEM((3, 4, 2, lanes, 128), BF),
        pltpu.VMEM((2, plane, 128), BF),
        pltpu.VMEM((plane, lanes // 2), BF),
        pltpu.VMEM((plane, lanes // 2), BF),
        pltpu.VMEM((2, plane, 128), BF),
        pltpu.VMEM((3, 4, PLANE, FACE, lanes // 2), BF),
        pltpu.VMEM((3, 4, PLANE, FACE, lanes // 2), BF),
        pltpu.VMEM((8 * slots, lanes), F32),
        pltpu.VMEM((2, cells // 2, width), F32),
        pltpu.VMEM((2, 128), F32),
        pltpu.VMEM((n_my, 4, cells // 2, width), F32),
        pltpu.VMEM((n, 2, 128), F32),
        pltpu.VMEM((4, 4, -(-(2 * n_my + 2) // 8) * 8, width), F32),
        pltpu.VMEM((n_my, 2 * cells, coarse_weight.shape[1]), F32),
        pltpu.VMEM((n_my, 2 * cells, coarse_weight.shape[1]), F32),
        dma((64,)), dma((3, 4)), dma((3, 4)), dma((n,)), dma((n,)),
        dma((3, n_my)), dma((3, n_my)), dma((n_my,)), dma((n_my,)),
        pltpu.SemaphoreType.REGULAR((max(1, (n_mx - 1).bit_length()), 2)),
    ]
    small = (RZ // 2, RY // 2, RX // 2, width)
    held_on = pl.pallas_call(
        functools.partial(level_kernel, slots, chans, cells),
        out_shape=(
            pltpu.VMEM((2, total, 128), BF), pltpu.VMEM(small, BF),
            pltpu.VMEM(sel.shape, BF), pltpu.VMEM(masks.shape, BF),
        ),
        in_specs=[HBM] * len(ins),
        out_specs=(VM,) * 4,
        scratch_shapes=scratch,
        compiler_params=pltpu.CompilerParams(collective_id=0, has_side_effects=True),
    )(*ins)
    return pl.pallas_call(
        functools.partial(unfold_kernel, chans, slots),
        out_shape=(sds(features.shape, BF), sds(small, BF)),
        in_specs=[VM] * 4,
        out_specs=(HBM, HBM),
        scratch_shapes=[
            pltpu.VMEM(features.shape, BF), pltpu.VMEM(small, BF), dma((1 + slots // 8,)),
        ],
    )(*[pltpu.with_memory_space_constraint(a, pltpu.VMEM) for a in held_on])


def solution(mesh):
    in_specs = (
        P(("mx", "my"), None, None),
        P(None, ("mx", "my")),
        P(("mx", "my")),
        P(None, ("mx", "my")),
        P(),
        P(),
        P(),
        P(),
        P(),
        P(None, "my"),
    )
    out_specs = (P(("mx", "my"), None, None), P("mx", "my", None, None))
    return jax.shard_map(local, mesh=mesh, in_specs=in_specs, out_specs=out_specs, check_vma=False)
```

```python
import functools

import jax
import jax.numpy as jnp
import numpy as np
from jax import lax
from jax.experimental import pallas as pl
from jax.experimental.pallas import tpu as pltpu
from jax.sharding import PartitionSpec as P

GROUPS = 32
SIDE = 8
RZ = 4
RY = 4
RX = 4
HALF = SIDE // 2
CUBES = HALF**3
PLANE = HALF**2
FACE = 16
norm_eps = 1e-05
MESH = pl.DeviceIdType.MESH
BF = jnp.bfloat16
F32 = jnp.float32
I32 = jnp.int32
VM = pl.BlockSpec(memory_space=pltpu.VMEM)
HBM = pl.BlockSpec(memory_space=pl.ANY)
NN = (((1,), (0,)), ((), ()))
NT = (((1,), (1,)), ((), ()))
TN = (((0,), (0,)), ((), ()))


def constants(chans):
    lane = np.arange(4 * chans)
    masks = np.stack([lane < 2 * chans, lane // chans % 2 == 0])
    masks = np.broadcast_to(masks[:, None, :], (2, 32, 4 * chans))
    sel = np.zeros((256, 256))
    for w in range(8):
        vy, vz, vx = w >> 2, w >> 1 & 1, w & 1
        for i in range(32):
            y, z, x = i // 8 * 2 + vy, i // 4 % 2 * 2 + vz, i % 4 * 2 + vx
            sel[w * 32 + i, (z * SIDE + y) * SIDE + x] = 1
    swap = np.zeros((256, 256))
    for i in range(16):
        for s in range(16):
            swap[i * 16 + s, s * 16 + i] = 1
    wide = np.arange(8 * chans)
    same = wide[:, None] % chans == wide[None, :] % chans
    as_bf = lambda a: jnp.asarray(np.asarray(a, np.float32), BF)
    halved = lambda a: as_bf(np.stack([a[:, :128], a[:, 128:]]))
    return as_bf(masks), halved(sel), halved(swap), halved(same)


def dot(a, b, dims=NN):
    return lax.dot_general(a, b, dims, preferred_element_type=F32)


def wide_of(ref, *at):
    return jnp.concatenate([ref[at[:-1] + (t,) + at[-1:]] for t in range(2)], axis=1)


def keep(ref, span, value):
    for t in range(2):
        ref[t, span, :] = value[:, 128 * t : 128 * t + 128]


def silu(x):
    h = 0.5 * x
    return h * jnp.tanh(h) + h


def swap_blocks(parts, low64, low32):
    left, right = [p[0] for p in parts], [p[1] for p in parts]
    m = [(left[i], left[i + 4]) for i in range(4)] + [(right[i], right[i + 4]) for i in range(4)]
    for bit, low, up, down in ((2, low64, 64, 64), (1, low32, 32, 96)):
        n = list(m)
        for j in range(8):
            if j & bit:
                continue
            a, b = m[j], m[j | bit]
            n[j] = tuple(jnp.where(low, a[t], pltpu.roll(b[t], up, 1)) for t in range(2))
            n[j | bit] = tuple(jnp.where(low, pltpu.roll(a[t], down, 1), b[t]) for t in range(2))
        m = n
    return m


def level_kernel(
    slots, chans, cells,
    counts_h, coords_h, neighbours_h, feat_h, fine_w_h, gain_h, bias_h, sel_h, swap_h, same_h,
    masks_h, down_h, up_h, weight_h,
    fine, coarse_out, sel_out, masks_out,
    counts, coords, neighbours, feat, fine_w, gain, bias, sel, swap, same, masks, down, up, weight,
    blocks, base, sig, sig2, acc, wts, gx, gyp, gym, gz, faces, halo, term,
    coarse, stats, window, everyone, pad, part, result,
    load, fsend, frecv, ssend, srecv, wsend, wrecv, rsend, rrecv, ready,
):
    n_mx, n_my = lax.axis_size("mx"), lax.axis_size("my")
    mx, my = lax.axis_index("mx"), lax.axis_index("my")
    n = n_mx * n_my
    me = mx * n_my + my
    width = 8 * chans
    side = width // 2
    wide_c = gain.shape[1]

    chunks = feat.shape[0]
    order = [
        ("feat", feat_h.at[:, :, pl.ds(128 * k, 128)], feat.at[k]) for k in range(chunks)
    ]
    order += [
        ("sel", sel_h, sel), ("masks", masks_h, masks), ("swap", swap_h, swap),
        ("fine_w", fine_w_h, fine_w), ("counts", counts_h, counts),
        ("coords", coords_h, coords), ("neighbours", neighbours_h, neighbours),
    ]
    late = [("same", same_h, same), ("gain", gain_h, gain), ("bias", bias_h, bias)]
    late += [("down", down_h.at[:, pl.ds(128 * k, 128)], down.at[k]) for k in range(down.shape[0])]
    late += [("weight", weight_h, weight)]
    late += [("up", up_h.at[:, pl.ds(128 * k, 128)], up.at[k]) for k in range(up.shape[0])]
    copies = [
        (name, pltpu.make_async_copy(a, b, load.at[i]))
        for i, (name, a, b) in enumerate(order + late)
    ]
    for _, c in copies[: len(order)]:
        c.start()

    def loaded(*names):
        for name, c in copies:
            if name in names:
                c.wait()

    barrier = pltpu.get_barrier_semaphore()
    low, high = mx > 0, mx < n_mx - 1

    def greet(a, b):
        pl.semaphore_signal(barrier, inc=1, device_id=(a, b), device_id_type=MESH)

    @pl.when(low)
    def _():
        greet(mx - 1, my)

    @pl.when(high)
    def _():
        greet(mx + 1, my)

    for d in range(1, n_my):
        greet(mx, lax.rem(my + d, n_my))

    def entered():
        pl.semaphore_wait(barrier, n_my - 1 + low.astype(I32) + high.astype(I32))

    rounds = max(n_mx - 1, 0).bit_length()

    def tell(k):
        @pl.when(mx + 2**k < n_mx)
        def _():
            pl.semaphore_signal(
                ready.at[k, 0], inc=1, device_id=(mx + 2**k, my), device_id_type=MESH
            )

        @pl.when(mx - 2**k >= 0)
        def _():
            pl.semaphore_signal(
                ready.at[k, 1], inc=1, device_id=(mx - 2**k, my), device_id_type=MESH
            )

    def hear(k):
        @pl.when(mx - 2**k >= 0)
        def _():
            pl.semaphore_wait(ready.at[k, 0], 1)

        @pl.when(mx + 2**k < n_mx)
        def _():
            pl.semaphore_wait(ready.at[k, 1], 1)

    loaded("feat", "sel", "masks")
    for _, c in copies[len(order) :]:
        c.start()

    def at_cube(q):
        return slice(q * slots, (q + 1) * slots)

    def rows(ref, q):
        return wide_of(ref, at_cube(q))

    def left(ref, q):
        return ref[0, at_cube(q), :]

    def right(ref, q):
        return ref[1, at_cube(q), :]

    def pair_of(ref):
        return jnp.concatenate([ref[0], ref[1]], axis=1)

    low64, low32 = masks[0] > 0.5, masks[1] > 0.5
    zero = jnp.zeros((slots, side), BF)

    for g in range(slots // 8):
        for h in range(2):
            x = jnp.concatenate(
                [feat[2 * h + t, 8 * g : 8 * g + 8].reshape(8 * chans, 128) for t in range(2)], axis=1
            )
            r = dot(pair_of(sel), x, NT).astype(BF)
            m = [(r[32 * w : 32 * w + 32, :side], r[32 * w : 32 * w + 32, side:]) for w in range(8)]
            m = swap_blocks(m, low64, low32)
            for s in range(8):
                at = (8 * g + s) * CUBES + 32 * h
                blocks[0, at : at + 32, :] = m[s][0]
                blocks[1, at : at + 32, :] = m[s][1]
    def cube_rows(slot, y):
        return [slice(slot * CUBES + 32 * h + 8 * y, slot * CUBES + 32 * h + 8 * y + 8) for h in range(2)]

    def by_cube(y):
        for g in range(slots // 16):
            x = jnp.concatenate(
                [wide_of(blocks, span) for s in range(16) for span in cube_rows(16 * g + s, y)], axis=0)
            r = dot(pair_of(swap), x)
            rb = r.astype(BF)
            rs = silu(r).astype(BF)
            for i in range(16):
                at = ((i // HALF * HALF + y) * HALF + i % HALF) * slots + 16 * g
                keep(base, slice(at, at + 16), rb[16 * i : 16 * i + 16])
                keep(sig, slice(at, at + 16), rs[16 * i : 16 * i + 16])

    def by_slot(y):
        for g in range(slots // 16):
            x = jnp.concatenate(
                [wide_of(base, pl.ds(((i // HALF * HALF + y) * HALF + i % HALF) * slots + 16 * g, 16))
                 for i in range(16)], axis=0)
            r = dot(pair_of(swap), x).astype(BF)
            for s in range(16):
                for h, span in enumerate(cube_rows(16 * g + s, y)):
                    keep(fine, span, r[16 * s + 8 * h : 16 * s + 8 * h + 8])

    loaded("counts", "coords", "neighbours")
    def one_hot(row, count):
        return (lax.broadcasted_iota(I32, (count, slots), 0) == row).astype(F32).astype(BF)

    eye = (
        lax.broadcasted_iota(I32, (slots, slots), 0) == lax.broadcasted_iota(I32, (slots, slots), 1)
    ).astype(F32).astype(BF)

    def turned(table):
        return dot(eye, table, NT).astype(BF)

    pz = coords[0:1, :] - mx * RZ
    py = coords[1:2, :] - my * RY
    px = coords[2:3, :]
    live = lax.broadcasted_iota(I32, (1, slots), 1) < counts[...]

    def link(d):
        g = neighbours[d : d + 1, :]
        here = g - me * slots
        inside = (here >= 0) & (here < slots)
        far = slots + (pz if d < 4 else py) * RX + px
        return jnp.where(g < 0, -1, jnp.where(inside, here, far))

    halo_rows = slots + FACE
    g_x = turned(jnp.concatenate([one_hot(link(d), slots) for d in (0, 1)], axis=0))
    g_yp = turned(one_hot(link(2), halo_rows))
    g_ym = turned(one_hot(link(3), halo_rows))
    g_z = turned(jnp.concatenate([one_hot(link(d), halo_rows) for d in (4, 5)], axis=0))
    edge = (
        jnp.where(live & (py == 0), pz * RX + px, -1),
        jnp.where(live & (py == RY - 1), pz * RX + px, -1),
        jnp.where(live & (pz == 0), py * RX + px, -1),
        jnp.where(live & (pz == RZ - 1), py * RX + px, -1),
    )
    g_edge = [one_hot(e, FACE) for e in edge]
    cell = (pz // 2 * 2 + px // 2) * 2 + py // 2
    place = pz % 2 * 4 + py % 2 * 2 + px % 2
    g_cell = one_hot(jnp.where(live, place * cells + cell, -1), 8 * cells)
    g_lift = turned(g_cell)
    alive = dot(
        jnp.where(live, eye.astype(F32), 0.0).astype(BF), jnp.ones((slots, width), BF)
    ) > 0.5

    peers = (
        (my > 0, mx, my - 1),
        (my < n_my - 1, mx, my + 1),
        (mx > 0, mx - 1, my),
        (mx < n_mx - 1, mx + 1, my),
    )

    def pieces(r, f):
        return ((4, 8), (0, 4), (12, 4)) if r == 2 and f < 2 else ((0, PLANE),)

    def face_copy(r, f, i):
        _, a, b = peers[f]
        span = pl.ds(*pieces(r, f)[i])
        return pltpu.make_async_remote_copy(
            src_ref=faces.at[r, f, span], dst_ref=halo.at[r, f, span], send_sem=fsend.at[r, f, i],
            recv_sem=frecv.at[r, f, i], device_id=(a, b), device_id_type=MESH,
        )

    low64_face = low64[:FACE]

    def send_face(r, src, f, zs=range(HALF), sent=(0,)):
        for k in [2 * z + i for z in zs for i in range(2)]:
            a, x = k // 2, k % 2 * 2
            if f < 2:
                part_of = left if f == 0 else right
                q = a * PLANE + (0 if f == 0 else HALF - 1) * HALF + x
                pair = jnp.concatenate([part_of(src, q), part_of(src, q + 1)], axis=1)
                v = dot(g_edge[f], pair).astype(BF)
                faces[r, f, 2 * k] = v[:, :side]
                faces[r, f, 2 * k + 1] = v[:, side:]
            else:
                q = (0 if f == 2 else HALF - 1) * PLANE + a * HALF + x
                va = dot(g_edge[f], rows(src, q)).astype(BF)
                vb = dot(g_edge[f], rows(src, q + 1)).astype(BF)
                for t in range(2):
                    own = va[:, t * side : (t + 1) * side]
                    other = pltpu.roll(vb[:, t * side : (t + 1) * side], 64, 1)
                    if f == 2:
                        faces[r, f, 2 * k + t] = jnp.where(low64_face, own, other)
                    else:
                        faces[r, f, 2 * k + t] = jnp.where(low64_face, other, own)

        @pl.when(peers[f][0])
        def _():
            for i in sent:
                face_copy(r, f, i).start()

        if 0 in sent:
            @pl.when(jnp.logical_not(peers[f ^ 1][0]))
            def _():
                halo[r, f] = jnp.zeros_like(halo[r, f])

    def sent_faces(r):
        for f in range(4):
            @pl.when(peers[f][0])
            def _():
                for i in range(len(pieces(r, f))):
                    face_copy(r, f, i).wait_send()

    def take_face(r, f):
        @pl.when(peers[f ^ 1][0])
        def _():
            for i in range(len(pieces(r, f))):
                face_copy(r, f, i).wait_recv()

    def z_halo(r, f, y, x):
        k = 2 * (y * 2 + x // 2)
        v = [halo[r, f, k + t] for t in range(2)]
        if x % 2:
            v = [pltpu.roll(a, 64, 1) for a in v]
        none = jnp.zeros_like(v[0])
        if f == 2:
            v = [jnp.where(low64_face, a, none) for a in v]
        else:
            v = [jnp.where(low64_face, none, a) for a in v]
        return jnp.concatenate(v, axis=1)

    def both(low, a, b):
        return jnp.concatenate([jnp.where(low, a[t], b[t]) for t in range(2)], axis=1)

    def halves(ref, q):
        return left(ref, q), right(ref, q)

    def run(ref, z, y):
        at = (z * HALF + y) * HALF * slots
        return wide_of(ref, slice(at, at + HALF * slots))

    def spans(runs):
        return [
            slice((z * HALF + y) * HALF * slots, (z * HALF + y + 1) * HALF * slots)
            for z, y in runs
        ]

    def stack(parts):
        return jnp.concatenate(parts, axis=0)

    def x_taps(src, runs):
        taps = []
        for z, y in runs:
            edge_of = halves(gx, z * HALF + y)
            for x in range(HALF):
                q = (z * HALF + y) * HALF + x
                after = halves(src, q + 1) if x < HALF - 1 else edge_of
                before = halves(src, q - 1) if x > 0 else edge_of
                taps.append(both(low32, after, before))
        return stack(taps)

    def y_taps(src, runs):
        taps = []
        for z, y in runs:
            for x in range(HALF):
                q = (z * HALF + y) * HALF + x
                zx = z * HALF + x
                span = slice(zx * slots, (zx + 1) * slots)
                after = left(src, q + HALF) if y < HALF - 1 else gyp[span, :]
                before = right(src, q - HALF) if y > 0 else gym[span, :]
                taps.append(jnp.concatenate([after, before], axis=1))
        return stack(taps)

    def z_taps(src, runs):
        taps = []
        for z, y in runs:
            for x in range(HALF):
                q = (z * HALF + y) * HALF + x
                edge_of = halves(gz, y * HALF + x)
                after = halves(src, q + PLANE) if z < HALF - 1 else edge_of
                before = halves(src, q - PLANE) if z > 0 else edge_of
                taps.append(both(low64, after, before))
        return stack(taps)

    def passes(r, src, runs, kinds):
        taps = {
            0: lambda: stack([run(src, z, y) for z, y in runs]),
            1: lambda: x_taps(src, runs),
            2: lambda: y_taps(src, runs),
            3: lambda: z_taps(src, runs),
        }
        total = None
        for k in kinds:
            v = dot(taps[k](), jnp.concatenate([wts[r, k, 0], wts[r, k, 1]], axis=1))
            total = v if total is None else total + v
        return total

    def add_to(ref, runs, value):
        tall = HALF * slots
        return [
            (span, wide_of(ref, span).astype(F32) + value[i * tall : (i + 1) * tall])
            for i, span in enumerate(spans(runs))
        ]

    inner, outer = range(1, HALF - 1), (0, HALF - 1)

    def near_inner(r, src, finish):
        for zy in range(PLANE):
            first, last = halves(src, zy * HALF), halves(src, zy * HALF + HALF - 1)
            pair = jnp.concatenate(
                [both(low32, first, (zero, zero)), both(low32, (zero, zero), last)], axis=0
            )
            keep(gx, at_cube(zy), dot(g_x, pair).astype(BF))
        for z in outer:
            runs = [(z, y) for y in inner]
            for span, v in add_to(base, runs, passes(r, src, runs, (0, 1, 2))):
                keep(acc, span, v)
        for z in inner:
            runs = [(z, y) for y in inner]
            for span, v in add_to(base, runs, passes(r, src, runs, (0, 1, 2, 3))):
                finish(span, v)

    def near_outer(r, src):
        for y in outer:
            for zs, kinds in ((inner, (0, 1, 3)), (outer, (0, 1))):
                runs = [(z, y) for z in zs]
                for span, v in add_to(base, runs, passes(r, src, runs, kinds)):
                    keep(acc, span, v)

    def gather_z(r, src):
        for f in (2, 3):
            take_face(r, f)
        for y in range(HALF):
            for x in range(HALF):
                i = y * HALF + x
                first, last = halves(src, i), halves(src, (HALF - 1) * PLANE + i)
                both_z = jnp.concatenate(
                    [both(low64, first, (zero, zero)), z_halo(r, 2, y, x),
                     both(low64, (zero, zero), last), z_halo(r, 3, y, x)], axis=0,
                )
                keep(gz, at_cube(i), dot(g_z, both_z).astype(BF))

    def gather_y(r, src, f):
        part_of, table, out = ((left, g_yp, gyp), (right, g_ym, gym))[f]
        for k in range(PLANE // 2):
            z, x = k // 2, k % 2 * 2
            q = z * PLANE + (0 if f == 0 else HALF - 1) * HALF + x
            own = jnp.concatenate([part_of(src, q), part_of(src, q + 1)], axis=1)
            got = jnp.concatenate([halo[r, f, 2 * k], halo[r, f, 2 * k + 1]], axis=1)
            v = dot(table, jnp.concatenate([own, got], axis=0)).astype(BF)
            out[2 * k * slots : (2 * k + 1) * slots, :] = v[:, :side]
            out[(2 * k + 1) * slots : (2 * k + 2) * slots, :] = v[:, side:]

    def more(r, src, runs, kind, finish=None):
        for span, v in add_to(acc, runs, passes(r, src, runs, (kind,))):
            if finish is None:
                keep(acc, span, v)
            else:
                finish(span, v)

    def far_z(r, src, finish):
        gather_z(r, src)
        for z in outer:
            more(r, src, [(z, y) for y in inner], 3, finish)
        for y in outer:
            more(r, src, [(z, y) for z in outer], 3)

    def far_y(r, src, finish, f):
        take_face(r, f)
        gather_y(r, src, f)
        y = HALF - 1 if f == 0 else 0
        for zs in (range(HALF // 2), range(HALF // 2, HALF)):
            more(r, src, [(z, y) for z in zs], 2, finish)

    lane_block = lax.broadcasted_iota(I32, (slots, width), 1) // chans
    block_f = lane_block.astype(F32).astype(BF)
    spread = (
        lax.broadcasted_iota(I32, (chans, width), 0)
        == lax.broadcasted_iota(I32, (chans, width), 1) % chans
    ).astype(F32).astype(BF)
    none = jnp.zeros((chans, width), BF)
    is_block = [block_f == float(w) for w in range(8)]

    def fit(r, k, span, v):
        for t in range(2):
            wts[r, k, t, span, :] = v[:, side * t : side * t + side]

    def fill(r):
        t = dot(fine_w[r], spread, TN).astype(BF)
        t = [t[i * chans : (i + 1) * chans] for i in range(7)]
        for w in range(8):
            span = slice(w * chans, (w + 1) * chans)
            vy, vz, vx = w >> 2, w >> 1 & 1, w & 1
            v = jnp.where(is_block[w], t[0], none)
            v = jnp.where(is_block[w ^ 1], t[1] if vx else t[2], v)
            v = jnp.where(is_block[w ^ 4], t[3] if vy else t[4], v)
            v = jnp.where(is_block[w ^ 2], t[5] if vz else t[6], v)
            fit(r, 0, span, v)
            fit(r, 1, span, jnp.where(is_block[w ^ 1], t[2] if vx else t[1], none))
            fit(r, 2, span, jnp.where(is_block[w ^ 4], t[4] if vy else t[3], none))
            fit(r, 3, span, jnp.where(is_block[w ^ 2], t[6] if vz else t[5], none))

    def first_done(span, value):
        keep(base, span, value.astype(BF))

    loaded("swap")
    by_cube(0)
    entered()
    send_face(0, sig, 0)
    by_cube(HALF - 1)
    send_face(0, sig, 1)
    for y in inner:
        by_cube(y)
    for f in (2, 3):
        send_face(0, sig, f)
    if rounds:
        tell(0)
    loaded("fine_w")
    fill(0)
    near_inner(0, sig, first_done)
    near_outer(0, sig)
    for k in range(1, rounds):
        hear(k - 1)
        tell(k)
        if k == 1:
            far_z(0, sig, first_done)
    if rounds < 2:
        far_z(0, sig, first_done)
    far_y(0, sig, first_done, 1)
    send_face(1, base, 0)
    far_y(0, sig, first_done, 0)
    send_face(1, base, 1)

    sums = []
    for o in range(8):
        total = None
        for i in range(8):
            z, y, x = (o >> 2) * 2 + (i >> 2), (o >> 1 & 1) * 2 + (i >> 1 & 1), (o & 1) * 2 + (i & 1)
            v = rows(base, (z * HALF + y) * HALF + x).astype(F32)
            total = v if i == 0 else total + v
        hi = total.astype(BF)
        sums += [hi, (total - hi.astype(F32)).astype(BF)]
    loaded("same")
    sums = dot(jnp.concatenate(sums, axis=0), pair_of(same))
    pooled = jnp.zeros((slots, width), F32)
    for o in range(8):
        v = sums[2 * o * slots : (2 * o + 1) * slots] + sums[(2 * o + 1) * slots : (2 * o + 2) * slots]
        pooled = jnp.where(lane_block == o, v, pooled)
    pooled = (pooled * (1.0 / HALF**3)).astype(BF)
    flat = dot(g_cell, pooled).astype(BF)
    loaded("down")
    ci = jnp.zeros((cells, wide_c), F32)
    for p in range(8):
        ci = ci + jnp.dot(
            flat[p * cells : (p + 1) * cells],
            jnp.concatenate([down[t, p * width : (p + 1) * width, :] for t in range(down.shape[0])], axis=1),
            preferred_element_type=F32,
        )
    layer = cells // 2
    coarse[0] = ci[:layer]
    coarse[1] = ci[layer:]
    group = wide_c // GROUPS
    lanes = stats.shape[1]

    def split(v):
        a = v.astype(BF)
        rest = v - a.astype(F32)
        b = rest.astype(BF)
        return [a, b, (rest - b.astype(F32)).astype(BF)]

    def in_three(v, table, dims):
        parts = dot(jnp.concatenate([p.astype(F32) for p in split(v)], axis=0).astype(BF), table, dims)
        tall = v.shape[0]
        return parts[:tall] + (parts[tall : 2 * tall] + parts[2 * tall :])

    grouped = (
        lax.broadcasted_iota(I32, (wide_c, lanes), 0) // group
        == lax.broadcasted_iota(I32, (wide_c, lanes), 1)
    ).astype(F32).astype(BF)
    rest = jnp.zeros((6, wide_c), F32)
    local = jnp.concatenate(
        [jnp.sum(ci, axis=0, keepdims=True), jnp.sum(ci * ci, axis=0, keepdims=True), rest], axis=0
    )
    stats[...] = in_three(local, grouped, NN)[0:2]

    offsets = sorted(range(n_mx), key=lambda i: -min(i, n_mx - i))
    others = [(i, j) for i in offsets for j in range(n_my) if i or j]

    def stat_copy(i, j):
        d = i * n_my + j
        return pltpu.make_async_remote_copy(
            src_ref=stats, dst_ref=everyone.at[me], send_sem=ssend.at[d], recv_sem=srecv.at[d],
            device_id=(lax.rem(mx + i, n_mx), lax.rem(my + j, n_my)), device_id_type=MESH,
        )

    def win_copy(kind, d):
        t = lax.rem(my + d, n_my)
        if kind == 0:
            src, dst, a = coarse, window.at[my, pl.ds(1, 2)], mx
        elif kind == 1:
            src, dst, a = coarse.at[pl.ds(0, 1)], window.at[my, pl.ds(3, 1)], mx - 1
        else:
            src, dst, a = coarse.at[pl.ds(1, 1)], window.at[my, pl.ds(0, 1)], mx + 1
        return pltpu.make_async_remote_copy(
            src_ref=src, dst_ref=dst, send_sem=wsend.at[kind, d], recv_sem=wrecv.at[kind, d],
            device_id=(a, t), device_id_type=MESH,
        )

    if rounds:
        hear(rounds - 1)
    for i, j in others:
        stat_copy(i, j).start()
    for d in range(n_my):
        if d:
            win_copy(0, d).start()

        @pl.when(low)
        def _():
            win_copy(1, d).start()

        @pl.when(high)
        def _():
            win_copy(2, d).start()
    window[my, 1:3] = coarse[...]
    everyone[me] = stats[...]

    @pl.when(jnp.logical_not(low))
    def _():
        for j in range(n_my):
            window[j, 0] = jnp.zeros_like(window[j, 0])

    @pl.when(jnp.logical_not(high))
    def _():
        for j in range(n_my):
            window[j, 3] = jnp.zeros_like(window[j, 3])

    pad[...] = jnp.zeros_like(pad)
    sel_out[...] = sel[...]
    masks_out[...] = masks[...]
    sent_faces(0)
    for r in (1, 2):
        fill(r)
    loaded("gain", "bias", "weight", "up")
    for d in range(n_my):
        if d:
            win_copy(0, d).wait()

        @pl.when(low)
        def _():
            win_copy(1, d).wait_send()
            win_copy(2, d).wait_recv()

        @pl.when(high)
        def _():
            win_copy(2, d).wait_send()
            win_copy(1, d).wait_recv()
    for i, j in others:
        stat_copy(i, j).wait()

    total = float(cells * group) * n
    sums = jnp.sum(everyone[...], axis=0) / total
    mean = sums[0:1]
    std = jnp.sqrt(sums[1:2] - mean * mean + norm_eps)
    both_rows = jnp.concatenate([mean, std, jnp.zeros((6, lanes), F32)], axis=0)
    both_rows = in_three(both_rows, grouped, NT)
    mean, std = both_rows[0:1], both_rows[1:2]
    g = gain[...]
    b = bias[...]
    for zw in range(4):
        for j in range(n_my):
            value = silu((window[j, zw] - mean) / std * g + b)
            if zw == 0:
                value = jnp.where(low, value, 0.0)
            if zw == 3:
                value = jnp.where(high, value, 0.0)
            for x in range(2):
                pad[1 + x, zw, 1 + 2 * j : 3 + 2 * j, :] = value[2 * x : 2 * x + 2]
    tall = 2 * n_my
    sums = jnp.zeros((4 * tall, part.shape[2]), F32)
    t = 0
    for dz in range(3):
        for dy in range(3):
            for dx in range(3):
                lhs = jnp.concatenate(
                    [pad[x + dx, z + dz, dy : dy + tall, :] for z in range(2) for x in range(2)],
                    axis=0,
                ).astype(BF)
                sums = sums + lax.dot_general(
                    lhs, weight[:, t * wide_c : (t + 1) * wide_c], (((1,), (1,)), ((), ())),
                    preferred_element_type=F32,
                )
                t += 1
    for j in range(n_my):
        for zx in range(4):
            part[j, 2 * zx : 2 * zx + 2, :] = sums[zx * tall + 2 * j : zx * tall + 2 * j + 2, :]
            above, below = zx * tall + 2 * min(j + 1, n_my - 1), zx * tall + 2 * max(j - 1, 0) + 1
            part[j, cells + zx : cells + zx + 1, :] = sums[above : above + 1, :]
            part[j, cells + 4 + zx : cells + 5 + zx, :] = sums[below : below + 1, :]
    copies = []
    for d in range(1, n_my):
        to = lax.rem(my + d, n_my)
        copies.append(
            pltpu.make_async_remote_copy(
                src_ref=part.at[to], dst_ref=result.at[my], send_sem=rsend.at[d],
                recv_sem=rrecv.at[d], device_id=(mx, to), device_id_type=MESH,
            )
        )
    for c in copies:
        c.start()
    result[my] = part[my]
    for c in copies:
        c.wait()

    whole = jnp.concatenate([result[j] for j in range(n_my)], axis=1)
    above, below = jnp.minimum(my + 1, n_my - 1), jnp.maximum(my - 1, 0)
    beside = [window[above, 1], window[above, 2], window[below, 1], window[below, 2]]
    beside = [
        v[r : r + 1] for i, v in enumerate(beside) for r in ((0, 2) if i < 2 else (1, 3))
    ]
    co = (whole + jnp.concatenate([coarse[0], coarse[1]] + beside, axis=0)).astype(BF)
    cof = co.astype(F32)
    for z in range(2):
        for y in range(2):
            q = z * 4 + y
            pair = jnp.concatenate([cof[q : q + 1], cof[q + 2 : q + 3]], axis=0)
            coarse_out[z, y] = pair.astype(BF)
    wide = dot(co, jnp.concatenate([up[k] for k in range(up.shape[0])], axis=1))
    def in_two(v):
        hi = v.astype(BF)
        return hi, (v - hi.astype(F32)).astype(BF)

    def lifted(at):
        return jnp.concatenate(
            [wide[at : at + cells, p * width : (p + 1) * width] for p in range(8)], axis=0
        )

    picked = [dot(g_lift, v).astype(BF) for v in in_two(lifted(0))]
    spots = [jnp.where(is_block[o], v, jnp.zeros_like(v)) for o in range(8) for v in picked]

    k = lax.broadcasted_iota(I32, (2 * FACE, 8 * cells), 0)
    down_side = k // FACE
    kz, kx = k % FACE // RX, k % RX
    row = (kz % 2 * 4 + down_side * 2 + kx % 2) * cells + down_side * 4 + kz // 2 * 2 + kx // 2
    g_halo = (lax.broadcasted_iota(I32, (2 * FACE, 8 * cells), 1) == row).astype(F32).astype(BF)
    picked = [dot(g_halo, v).astype(BF) for v in in_two(lifted(cells))]
    for zx in range(4):
        for v in picked:
            for f in range(2):
                o = zx // 2 * 4 + f * 2 + zx % 2
                v_f = v[f * FACE : (f + 1) * FACE]
                spots.append(jnp.where(is_block[o][:FACE], v_f, jnp.zeros_like(v_f)))
    sums = dot(jnp.concatenate(spots, axis=0), pair_of(same))
    for o in range(8):
        v = sums[2 * o * slots : (2 * o + 1) * slots] + sums[(2 * o + 1) * slots : (2 * o + 2) * slots]
        term[o * slots : (o + 1) * slots, :] = v

    def join(z, y):
        for x in range(HALF):
            q = (z * HALF + y) * HALF + x
            o = z // 2 * 4 + y // 2 * 2 + x // 2
            span = slice(q * slots, (q + 1) * slots)
            f = (wide_of(base, span).astype(F32) + term[o * slots : (o + 1) * slots, :]).astype(BF)
            keep(base, span, f)
            keep(sig, span, silu(f.astype(F32)).astype(BF))

    for f, z in ((2, 0), (3, HALF - 1)):
        for y in range(HALF):
            join(z, y)
        send_face(1, sig, f)
    for z in inner:
        for y in range(HALF):
            join(z, y)
    for f in range(2):
        take_face(1, f)
        for zx in range(PLANE):
            at = 16 * slots + (zx // 8 * 2 + zx % 4 // 2) * 4 * FACE + f * FACE
            lift = sums[at : at + FACE, :side] + sums[at + 2 * FACE : at + 3 * FACE, :side]
            v = (halo[1, f, zx].astype(F32) + lift).astype(BF)
            halo[1, f, zx] = silu(v.astype(F32)).astype(BF)

    def second_done(span, value):
        f = value.astype(BF)
        keep(base, span, f)
        keep(sig2, span, silu(f.astype(F32)).astype(BF))

    near_inner(1, sig, second_done)
    near_outer(1, sig)
    for f, y in ((1, 0), (0, HALF - 1)):
        gather_y(1, sig, f)
        more(1, sig, [(z, y) for z in inner], 2, second_done)
        send_face(2, sig2, f ^ 1, inner)
        more(1, sig, [(z, y) for z in outer], 2)
    gather_z(1, sig)
    for f, y in ((0, 0), (1, HALF - 1)):
        more(1, sig, [(z, y) for z in outer], 3, second_done)
        send_face(2, sig2, f, outer, (1, 2))
    for f, z in ((2, 0), (3, HALF - 1)):
        more(1, sig, [(z, y) for y in inner], 3, second_done)
        send_face(2, sig2, f)

    def last_done(span, value):
        for i in range(HALF):
            at = slice(span.start + i * slots, span.start + (i + 1) * slots)
            keep(base, at, jnp.where(alive, value[i * slots : (i + 1) * slots], 0.0).astype(BF))

    near_inner(2, sig2, last_done)
    near_outer(2, sig2)
    far_z(2, sig2, last_done)
    sent_faces(1)
    for y in inner:
        by_slot(y)
    for f, y in ((1, 0), (0, HALF - 1)):
        far_y(2, sig2, last_done, f)
        by_slot(y)
    sent_faces(2)


def unfold_kernel(chans, slots, rows, coarse, sel, masks, fine_h, coarse_h, fine, kept, sem):
    kept[...] = coarse[...]
    stores = [pltpu.make_async_copy(kept, coarse_h, sem.at[0])]
    stores[0].start()
    low64, low32 = masks[0] > 0.5, masks[1] > 0.5
    for g in range(slots // 8):
        for h in range(2):
            m = []
            for s in range(8):
                at = (8 * g + s) * CUBES + 32 * h
                m.append((rows[0, at : at + 32, :], rows[1, at : at + 32, :]))
            m = swap_blocks(m, low64, low32)
            x = jnp.concatenate([jnp.concatenate(p, axis=1) for p in m], axis=0)
            r = dot(x.T, jnp.concatenate([sel[0], sel[1]], axis=1)).astype(BF)
            fine[8 * g : 8 * g + 8, :, 256 * h : 256 * h + 256] = r.reshape(8, chans, 256)
        part = pl.ds(8 * g, 8)
        stores.append(pltpu.make_async_copy(fine.at[part], fine_h.at[part], sem.at[1 + g]))
        stores[-1].start()
    for c in stores:
        c.wait()


def local(
    features, coords, counts, neighbours, fine_weights, down_weight, up_weight, norm_gain,
    norm_bias, coarse_weight,
):
    slots, chans, _ = features.shape
    n_mx, n_my = lax.axis_size("mx"), lax.axis_size("my")
    cells = (RZ // 2) * (RY // 2) * (RX // 2)
    width = down_weight.shape[1]
    lanes = 8 * chans
    masks, sel, swap, same = constants(chans)
    n = n_mx * n_my
    sds = jax.ShapeDtypeStruct
    weight_t = coarse_weight.T
    ins = (
        counts[None, :], coords, neighbours, features, fine_weights, norm_gain[None, :],
        norm_bias[None, :], sel, swap, same, masks, down_weight, up_weight, weight_t,
    )
    held = [pltpu.VMEM(a.shape, a.dtype) for a in ins]
    held[3] = pltpu.VMEM((SIDE**3 // 128, slots, chans, 128), BF)
    held[11] = pltpu.VMEM((width // 128, down_weight.shape[0], 128), BF)
    held[12] = pltpu.VMEM((up_weight.shape[1] // 128, width, 128), BF)
    dma = pltpu.SemaphoreType.DMA
    total = slots * CUBES
    plane = slots * PLANE
    scratch = held + [
        pltpu.VMEM((2, total, 128), BF),
        pltpu.VMEM((2, total, 128), BF),
        pltpu.VMEM((2, total, 128), BF),
        pltpu.VMEM((2, total, 128), BF),
        pltpu.VMEM((2, total, 128), F32),
        pltpu.VMEM((3, 4, 2, lanes, 128), BF),
        pltpu.VMEM((2, plane, 128), BF),
        pltpu.VMEM((plane, lanes // 2), BF),
        pltpu.VMEM((plane, lanes // 2), BF),
        pltpu.VMEM((2, plane, 128), BF),
        pltpu.VMEM((3, 4, PLANE, FACE, lanes // 2), BF),
        pltpu.VMEM((3, 4, PLANE, FACE, lanes // 2), BF),
        pltpu.VMEM((8 * slots, lanes), F32),
        pltpu.VMEM((2, cells // 2, width), F32),
        pltpu.VMEM((2, 128), F32),
        pltpu.VMEM((n_my, 4, cells // 2, width), F32),
        pltpu.VMEM((n, 2, 128), F32),
        pltpu.VMEM((4, 4, -(-(2 * n_my + 2) // 8) * 8, width), F32),
        pltpu.VMEM((n_my, 2 * cells, coarse_weight.shape[1]), F32),
        pltpu.VMEM((n_my, 2 * cells, coarse_weight.shape[1]), F32),
        dma((64,)), dma((3, 4, 3)), dma((3, 4, 3)), dma((n,)), dma((n,)),
        dma((3, n_my)), dma((3, n_my)), dma((n_my,)), dma((n_my,)),
        pltpu.SemaphoreType.REGULAR((max(1, (n_mx - 1).bit_length()), 2)),
    ]
    small = (RZ // 2, RY // 2, RX // 2, width)
    held_on = pl.pallas_call(
        functools.partial(level_kernel, slots, chans, cells),
        out_shape=(
            pltpu.VMEM((2, total, 128), BF), pltpu.VMEM(small, BF),
            pltpu.VMEM(sel.shape, BF), pltpu.VMEM(masks.shape, BF),
        ),
        in_specs=[HBM] * len(ins),
        out_specs=(VM,) * 4,
        scratch_shapes=scratch,
        compiler_params=pltpu.CompilerParams(collective_id=0, has_side_effects=True),
    )(*ins)
    return pl.pallas_call(
        functools.partial(unfold_kernel, chans, slots),
        out_shape=(sds(features.shape, BF), sds(small, BF)),
        in_specs=[VM] * 4,
        out_specs=(HBM, HBM),
        scratch_shapes=[
            pltpu.VMEM(features.shape, BF), pltpu.VMEM(small, BF), dma((1 + slots // 8,)),
        ],
    )(*[pltpu.with_memory_space_constraint(a, pltpu.VMEM) for a in held_on])


def solution(mesh):
    in_specs = (
        P(("mx", "my"), None, None),
        P(None, ("mx", "my")),
        P(("mx", "my")),
        P(None, ("mx", "my")),
        P(),
        P(),
        P(),
        P(),
        P(),
        P(None, "my"),
    )
    out_specs = (P(("mx", "my"), None, None), P("mx", "my", None, None))
    return jax.shard_map(local, mesh=mesh, in_specs=in_specs, out_specs=out_specs, check_vma=False)
```

```python
import functools

import jax
import jax.numpy as jnp
import numpy as np
from jax import lax
from jax.experimental import pallas as pl
from jax.experimental.pallas import tpu as pltpu
from jax.sharding import PartitionSpec as P

GROUPS = 32
SIDE = 8
RZ = 4
RY = 4
RX = 4
HALF = SIDE // 2
CUBES = HALF**3
PLANE = HALF**2
FACE = 16
norm_eps = 1e-05
MESH = pl.DeviceIdType.MESH
BF = jnp.bfloat16
F32 = jnp.float32
I32 = jnp.int32
VM = pl.BlockSpec(memory_space=pltpu.VMEM)
HBM = pl.BlockSpec(memory_space=pl.ANY)
NN = (((1,), (0,)), ((), ()))
NT = (((1,), (1,)), ((), ()))
TN = (((0,), (0,)), ((), ()))


def constants(chans):
    lane = np.arange(4 * chans)
    masks = np.stack([lane < 2 * chans, lane // chans % 2 == 0])
    masks = np.broadcast_to(masks[:, None, :], (2, 32, 4 * chans))
    sel = np.zeros((256, 256))
    for w in range(8):
        vy, vz, vx = w >> 2, w >> 1 & 1, w & 1
        for i in range(32):
            z, y, x = i // 16 * 2 + vz, i // 4 % 4 * 2 + vy, i % 4 * 2 + vx
            sel[w * 32 + i, (z * SIDE + y) * SIDE + x] = 1
    swap = np.zeros((256, 256))
    for i in range(16):
        for s in range(16):
            swap[i * 16 + s, s * 16 + i] = 1
    wide = np.arange(8 * chans)
    same = wide[:, None] % chans == wide[None, :] % chans
    as_bf = lambda a: jnp.asarray(np.asarray(a, np.float32), BF)
    halved = lambda a: as_bf(np.stack([a[:, :128], a[:, 128:]]))
    return as_bf(masks), halved(sel), halved(swap), halved(same)


def dot(a, b, dims=NN):
    return lax.dot_general(a, b, dims, preferred_element_type=F32)


def wide_of(ref, *at):
    return jnp.concatenate([ref[at[:-1] + (t,) + at[-1:]] for t in range(2)], axis=1)


def keep(ref, span, value):
    for t in range(2):
        ref[t, span, :] = value[:, 128 * t : 128 * t + 128]


def silu(x):
    h = 0.5 * x
    return h * jnp.tanh(h) + h


def swap_blocks(parts, low64, low32):
    left, right = [p[0] for p in parts], [p[1] for p in parts]
    m = [(left[i], left[i + 4]) for i in range(4)] + [(right[i], right[i + 4]) for i in range(4)]
    for bit, low, up, down in ((2, low64, 64, 64), (1, low32, 32, 96)):
        n = list(m)
        for j in range(8):
            if j & bit:
                continue
            a, b = m[j], m[j | bit]
            n[j] = tuple(jnp.where(low, a[t], pltpu.roll(b[t], up, 1)) for t in range(2))
            n[j | bit] = tuple(jnp.where(low, pltpu.roll(a[t], down, 1), b[t]) for t in range(2))
        m = n
    return m


def level_kernel(
    slots, chans, cells,
    counts_h, coords_h, neighbours_h, feat_h, fine_w_h, gain_h, bias_h, sel_h, swap_h, same_h,
    masks_h, down_h, up_h, weight_h,
    fine, coarse_out, sel_out, masks_out,
    counts, coords, neighbours, feat, fine_w, gain, bias, sel, swap, same, masks, down, up, weight,
    blocks, base, sig, sig2, acc, wts, gx, gyp, gym, gz, faces, halo, term,
    coarse, stats, window, everyone, pad, part, result,
    load, fsend, frecv, ssend, srecv, wsend, wrecv, rsend, rrecv, ready,
):
    n_mx, n_my = lax.axis_size("mx"), lax.axis_size("my")
    mx, my = lax.axis_index("mx"), lax.axis_index("my")
    n = n_mx * n_my
    me = mx * n_my + my
    width = 8 * chans
    side = width // 2
    wide_c = gain.shape[1]

    chunks = feat.shape[0]
    order = [
        ("feat", feat_h.at[:, :, pl.ds(128 * k, 128)], feat.at[k]) for k in range(chunks)
    ]
    order += [
        ("sel", sel_h, sel), ("masks", masks_h, masks), ("swap", swap_h, swap),
        ("fine_w", fine_w_h, fine_w), ("counts", counts_h, counts),
        ("coords", coords_h, coords), ("neighbours", neighbours_h, neighbours),
    ]
    late = [("same", same_h, same), ("gain", gain_h, gain), ("bias", bias_h, bias)]
    late += [("down", down_h.at[:, pl.ds(128 * k, 128)], down.at[k]) for k in range(down.shape[0])]
    late += [("weight", weight_h, weight)]
    late += [("up", up_h.at[:, pl.ds(128 * k, 128)], up.at[k]) for k in range(up.shape[0])]
    copies = [
        (name, pltpu.make_async_copy(a, b, load.at[i]))
        for i, (name, a, b) in enumerate(order + late)
    ]
    for _, c in copies[: len(order)]:
        c.start()

    def loaded(*names):
        for name, c in copies:
            if name in names:
                c.wait()

    barrier = pltpu.get_barrier_semaphore()
    low, high = mx > 0, mx < n_mx - 1

    def greet(a, b):
        pl.semaphore_signal(barrier, inc=1, device_id=(a, b), device_id_type=MESH)

    @pl.when(low)
    def _():
        greet(mx - 1, my)

    @pl.when(high)
    def _():
        greet(mx + 1, my)

    for d in range(1, n_my):
        greet(mx, lax.rem(my + d, n_my))

    def entered():
        pl.semaphore_wait(barrier, n_my - 1 + low.astype(I32) + high.astype(I32))

    rounds = max(n_mx - 1, 0).bit_length()

    def tell(k):
        @pl.when(mx + 2**k < n_mx)
        def _():
            pl.semaphore_signal(
                ready.at[k, 0], inc=1, device_id=(mx + 2**k, my), device_id_type=MESH
            )

        @pl.when(mx - 2**k >= 0)
        def _():
            pl.semaphore_signal(
                ready.at[k, 1], inc=1, device_id=(mx - 2**k, my), device_id_type=MESH
            )

    def hear(k):
        @pl.when(mx - 2**k >= 0)
        def _():
            pl.semaphore_wait(ready.at[k, 0], 1)

        @pl.when(mx + 2**k < n_mx)
        def _():
            pl.semaphore_wait(ready.at[k, 1], 1)

    loaded("feat", "sel", "masks")
    for _, c in copies[len(order) :]:
        c.start()

    def at_cube(q):
        return slice(q * slots, (q + 1) * slots)

    def rows(ref, q):
        return wide_of(ref, at_cube(q))

    def left(ref, q):
        return ref[0, at_cube(q), :]

    def right(ref, q):
        return ref[1, at_cube(q), :]

    def pair_of(ref):
        return jnp.concatenate([ref[0], ref[1]], axis=1)

    low64, low32 = masks[0] > 0.5, masks[1] > 0.5
    zero = jnp.zeros((slots, side), BF)

    for g in range(slots // 8):
        for h in range(2):
            x = jnp.concatenate(
                [feat[2 * h + t, 8 * g : 8 * g + 8].reshape(8 * chans, 128) for t in range(2)], axis=1
            )
            r = dot(pair_of(sel), x, NT).astype(BF)
            m = [(r[32 * w : 32 * w + 32, :side], r[32 * w : 32 * w + 32, side:]) for w in range(8)]
            m = swap_blocks(m, low64, low32)
            for s in range(8):
                at = (8 * g + s) * CUBES + 32 * h
                blocks[0, at : at + 32, :] = m[s][0]
                blocks[1, at : at + 32, :] = m[s][1]
    loaded("swap")
    for z in range(HALF):
        for g in range(slots // 16):
            x = jnp.concatenate(
                [wide_of(blocks, pl.ds((16 * g + s) * CUBES + 16 * z, 16)) for s in range(16)], axis=0)
            r = dot(pair_of(swap), x)
            rb = r.astype(BF)
            rs = silu(r).astype(BF)
            for i in range(16):
                at = (16 * z + i) * slots + 16 * g
                keep(base, slice(at, at + 16), rb[16 * i : 16 * i + 16])
                keep(sig, slice(at, at + 16), rs[16 * i : 16 * i + 16])

    loaded("counts", "coords", "neighbours")
    def one_hot(row, count):
        return (lax.broadcasted_iota(I32, (count, slots), 0) == row).astype(F32).astype(BF)

    eye = (
        lax.broadcasted_iota(I32, (slots, slots), 0) == lax.broadcasted_iota(I32, (slots, slots), 1)
    ).astype(F32).astype(BF)

    def turned(table):
        return dot(eye, table, NT).astype(BF)

    pz = coords[0:1, :] - mx * RZ
    py = coords[1:2, :] - my * RY
    px = coords[2:3, :]
    live = lax.broadcasted_iota(I32, (1, slots), 1) < counts[...]

    def link(d):
        g = neighbours[d : d + 1, :]
        here = g - me * slots
        inside = (here >= 0) & (here < slots)
        far = slots + (pz if d < 4 else py) * RX + px
        return jnp.where(g < 0, -1, jnp.where(inside, here, far))

    halo_rows = slots + FACE
    g_x = turned(jnp.concatenate([one_hot(link(d), slots) for d in (0, 1)], axis=0))
    g_yp = turned(one_hot(link(2), halo_rows))
    g_ym = turned(one_hot(link(3), halo_rows))
    g_z = turned(jnp.concatenate([one_hot(link(d), halo_rows) for d in (4, 5)], axis=0))
    edge = (
        jnp.where(live & (py == 0), pz * RX + px, -1),
        jnp.where(live & (py == RY - 1), pz * RX + px, -1),
        jnp.where(live & (pz == 0), py * RX + px, -1),
        jnp.where(live & (pz == RZ - 1), py * RX + px, -1),
    )
    g_edge = [one_hot(e, FACE) for e in edge]
    cell = (pz // 2 * 2 + px // 2) * 2 + py // 2
    place = pz % 2 * 4 + py % 2 * 2 + px % 2
    g_cell = one_hot(jnp.where(live, place * cells + cell, -1), 8 * cells)
    g_lift = turned(g_cell)
    alive = dot(
        jnp.where(live, eye.astype(F32), 0.0).astype(BF), jnp.ones((slots, width), BF)
    ) > 0.5

    peers = (
        (my > 0, mx, my - 1),
        (my < n_my - 1, mx, my + 1),
        (mx > 0, mx - 1, my),
        (mx < n_mx - 1, mx + 1, my),
    )

    def face_copy(r, f):
        _, a, b = peers[f]
        return pltpu.make_async_remote_copy(
            src_ref=faces.at[r, f], dst_ref=halo.at[r, f], send_sem=fsend.at[r, f],
            recv_sem=frecv.at[r, f], device_id=(a, b), device_id_type=MESH,
        )

    low64_face = low64[:FACE]

    def send_face(r, src, f):
        for k in range(PLANE // 2):
            a, x = k // 2, k % 2 * 2
            if f < 2:
                part_of = left if f == 0 else right
                q = a * PLANE + (0 if f == 0 else HALF - 1) * HALF + x
                pair = jnp.concatenate([part_of(src, q), part_of(src, q + 1)], axis=1)
                v = dot(g_edge[f], pair).astype(BF)
                faces[r, f, 2 * k] = v[:, :side]
                faces[r, f, 2 * k + 1] = v[:, side:]
            else:
                q = (0 if f == 2 else HALF - 1) * PLANE + a * HALF + x
                va = dot(g_edge[f], rows(src, q)).astype(BF)
                vb = dot(g_edge[f], rows(src, q + 1)).astype(BF)
                for t in range(2):
                    own = va[:, t * side : (t + 1) * side]
                    other = pltpu.roll(vb[:, t * side : (t + 1) * side], 64, 1)
                    if f == 2:
                        faces[r, f, 2 * k + t] = jnp.where(low64_face, own, other)
                    else:
                        faces[r, f, 2 * k + t] = jnp.where(low64_face, other, own)

        @pl.when(peers[f][0])
        def _():
            face_copy(r, f).start()

        @pl.when(jnp.logical_not(peers[f ^ 1][0]))
        def _():
            halo[r, f] = jnp.zeros_like(halo[r, f])

    def sent_faces(r):
        for f in range(4):
            @pl.when(peers[f][0])
            def _():
                face_copy(r, f).wait_send()

    def take_face(r, f):
        @pl.when(peers[f ^ 1][0])
        def _():
            face_copy(r, f).wait_recv()

    def z_halo(r, f, y, x):
        k = 2 * (y * 2 + x // 2)
        v = [halo[r, f, k + t] for t in range(2)]
        if x % 2:
            v = [pltpu.roll(a, 64, 1) for a in v]
        none = jnp.zeros_like(v[0])
        if f == 2:
            v = [jnp.where(low64_face, a, none) for a in v]
        else:
            v = [jnp.where(low64_face, none, a) for a in v]
        return jnp.concatenate(v, axis=1)

    def both(low, a, b):
        return jnp.concatenate([jnp.where(low, a[t], b[t]) for t in range(2)], axis=1)

    def halves(ref, q):
        return left(ref, q), right(ref, q)

    def run(ref, z, y):
        at = (z * HALF + y) * HALF * slots
        return wide_of(ref, slice(at, at + HALF * slots))

    def spans(runs):
        return [
            slice((z * HALF + y) * HALF * slots, (z * HALF + y + 1) * HALF * slots)
            for z, y in runs
        ]

    def stack(parts):
        return jnp.concatenate(parts, axis=0)

    def x_taps(src, runs):
        taps = []
        for z, y in runs:
            edge_of = halves(gx, z * HALF + y)
            for x in range(HALF):
                q = (z * HALF + y) * HALF + x
                after = halves(src, q + 1) if x < HALF - 1 else edge_of
                before = halves(src, q - 1) if x > 0 else edge_of
                taps.append(both(low32, after, before))
        return stack(taps)

    def y_taps(src, runs):
        taps = []
        for z, y in runs:
            for x in range(HALF):
                q = (z * HALF + y) * HALF + x
                zx = z * HALF + x
                span = slice(zx * slots, (zx + 1) * slots)
                after = left(src, q + HALF) if y < HALF - 1 else gyp[span, :]
                before = right(src, q - HALF) if y > 0 else gym[span, :]
                taps.append(jnp.concatenate([after, before], axis=1))
        return stack(taps)

    def z_taps(src, runs):
        taps = []
        for z, y in runs:
            for x in range(HALF):
                q = (z * HALF + y) * HALF + x
                edge_of = halves(gz, y * HALF + x)
                after = halves(src, q + PLANE) if z < HALF - 1 else edge_of
                before = halves(src, q - PLANE) if z > 0 else edge_of
                taps.append(both(low64, after, before))
        return stack(taps)

    def passes(r, src, runs, kinds):
        taps = {
            0: lambda: stack([run(src, z, y) for z, y in runs]),
            1: lambda: x_taps(src, runs),
            2: lambda: y_taps(src, runs),
            3: lambda: z_taps(src, runs),
        }
        total = None
        for k in kinds:
            v = dot(taps[k](), jnp.concatenate([wts[r, k, 0], wts[r, k, 1]], axis=1))
            total = v if total is None else total + v
        return total

    def add_to(ref, runs, value):
        tall = HALF * slots
        return [
            (span, wide_of(ref, span).astype(F32) + value[i * tall : (i + 1) * tall])
            for i, span in enumerate(spans(runs))
        ]

    inner, outer = range(1, HALF - 1), (0, HALF - 1)

    def near_inner(r, src, finish):
        for zy in range(PLANE):
            first, last = halves(src, zy * HALF), halves(src, zy * HALF + HALF - 1)
            pair = jnp.concatenate(
                [both(low32, first, (zero, zero)), both(low32, (zero, zero), last)], axis=0
            )
            keep(gx, at_cube(zy), dot(g_x, pair).astype(BF))
        for z in outer:
            runs = [(z, y) for y in inner]
            for span, v in add_to(base, runs, passes(r, src, runs, (0, 1, 2))):
                keep(acc, span, v)
        for z in inner:
            runs = [(z, y) for y in inner]
            for span, v in add_to(base, runs, passes(r, src, runs, (0, 1, 2, 3))):
                finish(span, v)

    def near_outer(r, src):
        for y in outer:
            for zs, kinds in ((inner, (0, 1, 3)), (outer, (0, 1))):
                runs = [(z, y) for z in zs]
                for span, v in add_to(base, runs, passes(r, src, runs, kinds)):
                    keep(acc, span, v)

    def gather_z(r, src):
        for f in (2, 3):
            take_face(r, f)
        for y in range(HALF):
            for x in range(HALF):
                i = y * HALF + x
                first, last = halves(src, i), halves(src, (HALF - 1) * PLANE + i)
                both_z = jnp.concatenate(
                    [both(low64, first, (zero, zero)), z_halo(r, 2, y, x),
                     both(low64, (zero, zero), last), z_halo(r, 3, y, x)], axis=0,
                )
                keep(gz, at_cube(i), dot(g_z, both_z).astype(BF))

    def gather_y(r, src, f):
        part_of, table, out = ((left, g_yp, gyp), (right, g_ym, gym))[f]
        for k in range(PLANE // 2):
            z, x = k // 2, k % 2 * 2
            q = z * PLANE + (0 if f == 0 else HALF - 1) * HALF + x
            own = jnp.concatenate([part_of(src, q), part_of(src, q + 1)], axis=1)
            got = jnp.concatenate([halo[r, f, 2 * k], halo[r, f, 2 * k + 1]], axis=1)
            v = dot(table, jnp.concatenate([own, got], axis=0)).astype(BF)
            out[2 * k * slots : (2 * k + 1) * slots, :] = v[:, :side]
            out[(2 * k + 1) * slots : (2 * k + 2) * slots, :] = v[:, side:]

    def more(r, src, runs, kind, finish=None):
        for span, v in add_to(acc, runs, passes(r, src, runs, (kind,))):
            if finish is None:
                keep(acc, span, v)
            else:
                finish(span, v)

    def far_z(r, src, finish):
        gather_z(r, src)
        for z in outer:
            more(r, src, [(z, y) for y in inner], 3, finish)
        for y in outer:
            more(r, src, [(z, y) for z in outer], 3)

    def far_y(r, src, finish, f):
        take_face(r, f)
        gather_y(r, src, f)
        y = HALF - 1 if f == 0 else 0
        for zs in (range(HALF // 2), range(HALF // 2, HALF)):
            more(r, src, [(z, y) for z in zs], 2, finish)

    lane_block = lax.broadcasted_iota(I32, (slots, width), 1) // chans
    block_f = lane_block.astype(F32).astype(BF)
    spread = (
        lax.broadcasted_iota(I32, (chans, width), 0)
        == lax.broadcasted_iota(I32, (chans, width), 1) % chans
    ).astype(F32).astype(BF)
    none = jnp.zeros((chans, width), BF)
    is_block = [block_f == float(w) for w in range(8)]

    def fit(r, k, span, v):
        for t in range(2):
            wts[r, k, t, span, :] = v[:, side * t : side * t + side]

    def fill(r):
        t = dot(fine_w[r], spread, TN).astype(BF)
        t = [t[i * chans : (i + 1) * chans] for i in range(7)]
        for w in range(8):
            span = slice(w * chans, (w + 1) * chans)
            vy, vz, vx = w >> 2, w >> 1 & 1, w & 1
            v = jnp.where(is_block[w], t[0], none)
            v = jnp.where(is_block[w ^ 1], t[1] if vx else t[2], v)
            v = jnp.where(is_block[w ^ 4], t[3] if vy else t[4], v)
            v = jnp.where(is_block[w ^ 2], t[5] if vz else t[6], v)
            fit(r, 0, span, v)
            fit(r, 1, span, jnp.where(is_block[w ^ 1], t[2] if vx else t[1], none))
            fit(r, 2, span, jnp.where(is_block[w ^ 4], t[4] if vy else t[3], none))
            fit(r, 3, span, jnp.where(is_block[w ^ 2], t[6] if vz else t[5], none))

    def first_done(span, value):
        keep(base, span, value.astype(BF))

    entered()
    for f in (0, 1, 2, 3):
        send_face(0, sig, f)
    if rounds:
        tell(0)
    loaded("fine_w")
    fill(0)
    near_inner(0, sig, first_done)
    near_outer(0, sig)
    for k in range(1, rounds):
        hear(k - 1)
        tell(k)
        if k == 1:
            far_z(0, sig, first_done)
    if rounds < 2:
        far_z(0, sig, first_done)
    far_y(0, sig, first_done, 1)
    far_y(0, sig, first_done, 0)

    sums = []
    for o in range(8):
        total = None
        for i in range(8):
            z, y, x = (o >> 2) * 2 + (i >> 2), (o >> 1 & 1) * 2 + (i >> 1 & 1), (o & 1) * 2 + (i & 1)
            v = rows(base, (z * HALF + y) * HALF + x).astype(F32)
            total = v if i == 0 else total + v
        hi = total.astype(BF)
        sums += [hi, (total - hi.astype(F32)).astype(BF)]
    loaded("same")
    sums = dot(jnp.concatenate(sums, axis=0), pair_of(same))
    pooled = jnp.zeros((slots, width), F32)
    for o in range(8):
        v = sums[2 * o * slots : (2 * o + 1) * slots] + sums[(2 * o + 1) * slots : (2 * o + 2) * slots]
        pooled = jnp.where(lane_block == o, v, pooled)
    pooled = (pooled * (1.0 / HALF**3)).astype(BF)
    flat = dot(g_cell, pooled).astype(BF)
    loaded("down")
    ci = jnp.zeros((cells, wide_c), F32)
    for p in range(8):
        ci = ci + jnp.dot(
            flat[p * cells : (p + 1) * cells],
            jnp.concatenate([down[t, p * width : (p + 1) * width, :] for t in range(down.shape[0])], axis=1),
            preferred_element_type=F32,
        )
    layer = cells // 2
    coarse[0] = ci[:layer]
    coarse[1] = ci[layer:]
    group = wide_c // GROUPS
    lanes = stats.shape[1]

    def split(v):
        a = v.astype(BF)
        rest = v - a.astype(F32)
        b = rest.astype(BF)
        return [a, b, (rest - b.astype(F32)).astype(BF)]

    def in_three(v, table, dims):
        parts = dot(jnp.concatenate([p.astype(F32) for p in split(v)], axis=0).astype(BF), table, dims)
        tall = v.shape[0]
        return parts[:tall] + (parts[tall : 2 * tall] + parts[2 * tall :])

    grouped = (
        lax.broadcasted_iota(I32, (wide_c, lanes), 0) // group
        == lax.broadcasted_iota(I32, (wide_c, lanes), 1)
    ).astype(F32).astype(BF)
    rest = jnp.zeros((6, wide_c), F32)
    local = jnp.concatenate(
        [jnp.sum(ci, axis=0, keepdims=True), jnp.sum(ci * ci, axis=0, keepdims=True), rest], axis=0
    )
    stats[...] = in_three(local, grouped, NN)[0:2]

    offsets = sorted(range(n_mx), key=lambda i: -min(i, n_mx - i))
    others = [(i, j) for i in offsets for j in range(n_my) if i or j]

    def stat_copy(i, j):
        d = i * n_my + j
        return pltpu.make_async_remote_copy(
            src_ref=stats, dst_ref=everyone.at[me], send_sem=ssend.at[d], recv_sem=srecv.at[d],
            device_id=(lax.rem(mx + i, n_mx), lax.rem(my + j, n_my)), device_id_type=MESH,
        )

    def win_copy(kind, d):
        t = lax.rem(my + d, n_my)
        if kind == 0:
            src, dst, a = coarse, window.at[my, pl.ds(1, 2)], mx
        elif kind == 1:
            src, dst, a = coarse.at[pl.ds(0, 1)], window.at[my, pl.ds(3, 1)], mx - 1
        else:
            src, dst, a = coarse.at[pl.ds(1, 1)], window.at[my, pl.ds(0, 1)], mx + 1
        return pltpu.make_async_remote_copy(
            src_ref=src, dst_ref=dst, send_sem=wsend.at[kind, d], recv_sem=wrecv.at[kind, d],
            device_id=(a, t), device_id_type=MESH,
        )

    if rounds:
        hear(rounds - 1)
    for i, j in others:
        stat_copy(i, j).start()
    for d in range(n_my):
        if d:
            win_copy(0, d).start()

        @pl.when(low)
        def _():
            win_copy(1, d).start()

        @pl.when(high)
        def _():
            win_copy(2, d).start()
    for f in range(2):
        send_face(1, base, f)
    window[my, 1:3] = coarse[...]
    everyone[me] = stats[...]

    @pl.when(jnp.logical_not(low))
    def _():
        for j in range(n_my):
            window[j, 0] = jnp.zeros_like(window[j, 0])

    @pl.when(jnp.logical_not(high))
    def _():
        for j in range(n_my):
            window[j, 3] = jnp.zeros_like(window[j, 3])

    pad[...] = jnp.zeros_like(pad)
    sel_out[...] = sel[...]
    masks_out[...] = masks[...]
    sent_faces(0)
    for r in (1, 2):
        fill(r)
    loaded("gain", "bias", "weight", "up")
    for d in range(n_my):
        if d:
            win_copy(0, d).wait()

        @pl.when(low)
        def _():
            win_copy(1, d).wait_send()
            win_copy(2, d).wait_recv()

        @pl.when(high)
        def _():
            win_copy(2, d).wait_send()
            win_copy(1, d).wait_recv()
    for i, j in others:
        stat_copy(i, j).wait()

    total = float(cells * group) * n
    sums = jnp.sum(everyone[...], axis=0) / total
    mean = sums[0:1]
    std = jnp.sqrt(sums[1:2] - mean * mean + norm_eps)
    both_rows = jnp.concatenate([mean, std, jnp.zeros((6, lanes), F32)], axis=0)
    both_rows = in_three(both_rows, grouped, NT)
    mean, std = both_rows[0:1], both_rows[1:2]
    g = gain[...]
    b = bias[...]
    for zw in range(4):
        for j in range(n_my):
            value = silu((window[j, zw] - mean) / std * g + b)
            if zw == 0:
                value = jnp.where(low, value, 0.0)
            if zw == 3:
                value = jnp.where(high, value, 0.0)
            for x in range(2):
                pad[1 + x, zw, 1 + 2 * j : 3 + 2 * j, :] = value[2 * x : 2 * x + 2]
    tall = 2 * n_my
    sums = jnp.zeros((4 * tall, part.shape[2]), F32)
    t = 0
    for dz in range(3):
        for dy in range(3):
            for dx in range(3):
                lhs = jnp.concatenate(
                    [pad[x + dx, z + dz, dy : dy + tall, :] for z in range(2) for x in range(2)],
                    axis=0,
                ).astype(BF)
                sums = sums + lax.dot_general(
                    lhs, weight[:, t * wide_c : (t + 1) * wide_c], (((1,), (1,)), ((), ())),
                    preferred_element_type=F32,
                )
                t += 1
    for j in range(n_my):
        for zx in range(4):
            part[j, 2 * zx : 2 * zx + 2, :] = sums[zx * tall + 2 * j : zx * tall + 2 * j + 2, :]
            above, below = zx * tall + 2 * min(j + 1, n_my - 1), zx * tall + 2 * max(j - 1, 0) + 1
            part[j, cells + zx : cells + zx + 1, :] = sums[above : above + 1, :]
            part[j, cells + 4 + zx : cells + 5 + zx, :] = sums[below : below + 1, :]
    copies = []
    for d in range(1, n_my):
        to = lax.rem(my + d, n_my)
        copies.append(
            pltpu.make_async_remote_copy(
                src_ref=part.at[to], dst_ref=result.at[my], send_sem=rsend.at[d],
                recv_sem=rrecv.at[d], device_id=(mx, to), device_id_type=MESH,
            )
        )
    for c in copies:
        c.start()
    result[my] = part[my]
    for c in copies:
        c.wait()

    whole = jnp.concatenate([result[j] for j in range(n_my)], axis=1)
    above, below = jnp.minimum(my + 1, n_my - 1), jnp.maximum(my - 1, 0)
    beside = [window[above, 1], window[above, 2], window[below, 1], window[below, 2]]
    beside = [
        v[r : r + 1] for i, v in enumerate(beside) for r in ((0, 2) if i < 2 else (1, 3))
    ]
    co = (whole + jnp.concatenate([coarse[0], coarse[1]] + beside, axis=0)).astype(BF)
    cof = co.astype(F32)
    for z in range(2):
        for y in range(2):
            q = z * 4 + y
            pair = jnp.concatenate([cof[q : q + 1], cof[q + 2 : q + 3]], axis=0)
            coarse_out[z, y] = pair.astype(BF)
    wide = dot(co, jnp.concatenate([up[k] for k in range(up.shape[0])], axis=1))
    def in_two(v):
        hi = v.astype(BF)
        return hi, (v - hi.astype(F32)).astype(BF)

    def lifted(at):
        return jnp.concatenate(
            [wide[at : at + cells, p * width : (p + 1) * width] for p in range(8)], axis=0
        )

    picked = [dot(g_lift, v).astype(BF) for v in in_two(lifted(0))]
    spots = [jnp.where(is_block[o], v, jnp.zeros_like(v)) for o in range(8) for v in picked]

    k = lax.broadcasted_iota(I32, (2 * FACE, 8 * cells), 0)
    down_side = k // FACE
    kz, kx = k % FACE // RX, k % RX
    row = (kz % 2 * 4 + down_side * 2 + kx % 2) * cells + down_side * 4 + kz // 2 * 2 + kx // 2
    g_halo = (lax.broadcasted_iota(I32, (2 * FACE, 8 * cells), 1) == row).astype(F32).astype(BF)
    picked = [dot(g_halo, v).astype(BF) for v in in_two(lifted(cells))]
    for zx in range(4):
        for v in picked:
            for f in range(2):
                o = zx // 2 * 4 + f * 2 + zx % 2
                v_f = v[f * FACE : (f + 1) * FACE]
                spots.append(jnp.where(is_block[o][:FACE], v_f, jnp.zeros_like(v_f)))
    sums = dot(jnp.concatenate(spots, axis=0), pair_of(same))
    for o in range(8):
        v = sums[2 * o * slots : (2 * o + 1) * slots] + sums[(2 * o + 1) * slots : (2 * o + 2) * slots]
        term[o * slots : (o + 1) * slots, :] = v

    def join(z, y):
        for x in range(HALF):
            q = (z * HALF + y) * HALF + x
            o = z // 2 * 4 + y // 2 * 2 + x // 2
            span = slice(q * slots, (q + 1) * slots)
            f = (wide_of(base, span).astype(F32) + term[o * slots : (o + 1) * slots, :]).astype(BF)
            keep(base, span, f)
            keep(sig, span, silu(f.astype(F32)).astype(BF))

    for f, z in ((2, 0), (3, HALF - 1)):
        for y in range(HALF):
            join(z, y)
        send_face(1, sig, f)
    for z in inner:
        for y in range(HALF):
            join(z, y)
    for f in range(2):
        take_face(1, f)
        for zx in range(PLANE):
            at = 16 * slots + (zx // 8 * 2 + zx % 4 // 2) * 4 * FACE + f * FACE
            lift = sums[at : at + FACE, :side] + sums[at + 2 * FACE : at + 3 * FACE, :side]
            v = (halo[1, f, zx].astype(F32) + lift).astype(BF)
            halo[1, f, zx] = silu(v.astype(F32)).astype(BF)

    def second_done(span, value):
        f = value.astype(BF)
        keep(base, span, f)
        keep(sig2, span, silu(f.astype(F32)).astype(BF))

    near_inner(1, sig, second_done)
    near_outer(1, sig)
    for f, y in ((1, 0), (0, HALF - 1)):
        gather_y(1, sig, f)
        more(1, sig, [(z, y) for z in inner], 2, second_done)
        more(1, sig, [(z, y) for z in outer], 2)
    gather_z(1, sig)
    for f, y in ((0, 0), (1, HALF - 1)):
        more(1, sig, [(z, y) for z in outer], 3, second_done)
        send_face(2, sig2, f)
    for f, z in ((2, 0), (3, HALF - 1)):
        more(1, sig, [(z, y) for y in inner], 3, second_done)
        send_face(2, sig2, f)

    def last_done(span, value):
        for i in range(HALF):
            at = slice(span.start + i * slots, span.start + (i + 1) * slots)
            keep(base, at, jnp.where(alive, value[i * slots : (i + 1) * slots], 0.0).astype(BF))

    near_inner(2, sig2, last_done)
    near_outer(2, sig2)
    far_z(2, sig2, last_done)
    sent_faces(1)
    for f in (1, 0):
        far_y(2, sig2, last_done, f)

    sent_faces(2)
    for g in range(slots // 16):
        for z in range(HALF):
            x = jnp.concatenate(
                [wide_of(base, pl.ds((16 * z + i) * slots + 16 * g, 16)) for i in range(16)], axis=0)
            r = dot(pair_of(swap), x).astype(BF)
            for s in range(16):
                at = (16 * g + s) * CUBES + 16 * z
                keep(fine, slice(at, at + 16), r[16 * s : 16 * s + 16])


def unfold_kernel(chans, slots, rows, coarse, sel, masks, fine_h, coarse_h, fine, kept, sem):
    kept[...] = coarse[...]
    stores = [pltpu.make_async_copy(kept, coarse_h, sem.at[0])]
    stores[0].start()
    low64, low32 = masks[0] > 0.5, masks[1] > 0.5
    for g in range(slots // 8):
        for h in range(2):
            m = []
            for s in range(8):
                at = (8 * g + s) * CUBES + 32 * h
                m.append((rows[0, at : at + 32, :], rows[1, at : at + 32, :]))
            m = swap_blocks(m, low64, low32)
            x = jnp.concatenate([jnp.concatenate(p, axis=1) for p in m], axis=0)
            r = dot(x.T, jnp.concatenate([sel[0], sel[1]], axis=1)).astype(BF)
            fine[8 * g : 8 * g + 8, :, 256 * h : 256 * h + 256] = r.reshape(8, chans, 256)
        part = pl.ds(8 * g, 8)
        stores.append(pltpu.make_async_copy(fine.at[part], fine_h.at[part], sem.at[1 + g]))
        stores[-1].start()
    for c in stores:
        c.wait()


def local(
    features, coords, counts, neighbours, fine_weights, down_weight, up_weight, norm_gain,
    norm_bias, coarse_weight,
):
    slots, chans, _ = features.shape
    n_mx, n_my = lax.axis_size("mx"), lax.axis_size("my")
    cells = (RZ // 2) * (RY // 2) * (RX // 2)
    width = down_weight.shape[1]
    lanes = 8 * chans
    masks, sel, swap, same = constants(chans)
    n = n_mx * n_my
    sds = jax.ShapeDtypeStruct
    weight_t = coarse_weight.T
    ins = (
        counts[None, :], coords, neighbours, features, fine_weights, norm_gain[None, :],
        norm_bias[None, :], sel, swap, same, masks, down_weight, up_weight, weight_t,
    )
    held = [pltpu.VMEM(a.shape, a.dtype) for a in ins]
    held[3] = pltpu.VMEM((SIDE**3 // 128, slots, chans, 128), BF)
    held[11] = pltpu.VMEM((width // 128, down_weight.shape[0], 128), BF)
    held[12] = pltpu.VMEM((up_weight.shape[1] // 128, width, 128), BF)
    dma = pltpu.SemaphoreType.DMA
    total = slots * CUBES
    plane = slots * PLANE
    scratch = held + [
        pltpu.VMEM((2, total, 128), BF),
        pltpu.VMEM((2, total, 128), BF),
        pltpu.VMEM((2, total, 128), BF),
        pltpu.VMEM((2, total, 128), BF),
        pltpu.VMEM((2, total, 128), F32),
        pltpu.VMEM((3, 4, 2, lanes, 128), BF),
        pltpu.VMEM((2, plane, 128), BF),
        pltpu.VMEM((plane, lanes // 2), BF),
        pltpu.VMEM((plane, lanes // 2), BF),
        pltpu.VMEM((2, plane, 128), BF),
        pltpu.VMEM((3, 4, PLANE, FACE, lanes // 2), BF),
        pltpu.VMEM((3, 4, PLANE, FACE, lanes // 2), BF),
        pltpu.VMEM((8 * slots, lanes), F32),
        pltpu.VMEM((2, cells // 2, width), F32),
        pltpu.VMEM((2, 128), F32),
        pltpu.VMEM((n_my, 4, cells // 2, width), F32),
        pltpu.VMEM((n, 2, 128), F32),
        pltpu.VMEM((4, 4, -(-(2 * n_my + 2) // 8) * 8, width), F32),
        pltpu.VMEM((n_my, 2 * cells, coarse_weight.shape[1]), F32),
        pltpu.VMEM((n_my, 2 * cells, coarse_weight.shape[1]), F32),
        dma((64,)), dma((3, 4)), dma((3, 4)), dma((n,)), dma((n,)),
        dma((3, n_my)), dma((3, n_my)), dma((n_my,)), dma((n_my,)),
        pltpu.SemaphoreType.REGULAR((max(1, (n_mx - 1).bit_length()), 2)),
    ]
    small = (RZ // 2, RY // 2, RX // 2, width)
    held_on = pl.pallas_call(
        functools.partial(level_kernel, slots, chans, cells),
        out_shape=(
            pltpu.VMEM((2, total, 128), BF), pltpu.VMEM(small, BF),
            pltpu.VMEM(sel.shape, BF), pltpu.VMEM(masks.shape, BF),
        ),
        in_specs=[HBM] * len(ins),
        out_specs=(VM,) * 4,
        scratch_shapes=scratch,
        compiler_params=pltpu.CompilerParams(collective_id=0, has_side_effects=True),
    )(*ins)
    return pl.pallas_call(
        functools.partial(unfold_kernel, chans, slots),
        out_shape=(sds(features.shape, BF), sds(small, BF)),
        in_specs=[VM] * 4,
        out_specs=(HBM, HBM),
        scratch_shapes=[
            pltpu.VMEM(features.shape, BF), pltpu.VMEM(small, BF), dma((1 + slots // 8,)),
        ],
    )(*[pltpu.with_memory_space_constraint(a, pltpu.VMEM) for a in held_on])


def solution(mesh):
    in_specs = (
        P(("mx", "my"), None, None),
        P(None, ("mx", "my")),
        P(("mx", "my")),
        P(None, ("mx", "my")),
        P(),
        P(),
        P(),
        P(),
        P(),
        P(None, "my"),
    )
    out_specs = (P(("mx", "my"), None, None), P("mx", "my", None, None))
    return jax.shard_map(local, mesh=mesh, in_specs=in_specs, out_specs=out_specs, check_vma=False)
```

```python
import functools

import jax
import jax.numpy as jnp
import numpy as np
from jax import lax
from jax.experimental import pallas as pl
from jax.experimental.pallas import tpu as pltpu
from jax.sharding import PartitionSpec as P

GROUPS = 32
SIDE = 8
RZ = 4
RY = 4
RX = 4
HALF = SIDE // 2
CUBES = HALF**3
PLANE = HALF**2
FACE = 16
norm_eps = 1e-05
MESH = pl.DeviceIdType.MESH
BF = jnp.bfloat16
F32 = jnp.float32
I32 = jnp.int32
VM = pl.BlockSpec(memory_space=pltpu.VMEM)
HBM = pl.BlockSpec(memory_space=pl.ANY)
NN = (((1,), (0,)), ((), ()))
NT = (((1,), (1,)), ((), ()))
TN = (((0,), (0,)), ((), ()))


def constants(chans):
    lane = np.arange(4 * chans)
    masks = np.stack([lane < 2 * chans, lane // chans % 2 == 0])
    masks = np.broadcast_to(masks[:, None, :], (2, 32, 4 * chans))
    sel = np.zeros((256, 256))
    for w in range(8):
        vy, vz, vx = w >> 2, w >> 1 & 1, w & 1
        for i in range(32):
            z, y, x = i // 16 * 2 + vz, i // 4 % 4 * 2 + vy, i % 4 * 2 + vx
            sel[w * 32 + i, (z * SIDE + y) * SIDE + x] = 1
    swap = np.zeros((256, 256))
    for i in range(16):
        for s in range(16):
            swap[i * 16 + s, s * 16 + i] = 1
    wide = np.arange(8 * chans)
    same = wide[:, None] % chans == wide[None, :] % chans
    as_bf = lambda a: jnp.asarray(np.asarray(a, np.float32), BF)
    halved = lambda a: as_bf(np.stack([a[:, :128], a[:, 128:]]))
    return as_bf(masks), halved(sel), halved(swap), halved(same)


def dot(a, b, dims=NN):
    return lax.dot_general(a, b, dims, preferred_element_type=F32)


def wide_of(ref, *at):
    return jnp.concatenate([ref[at[:-1] + (t,) + at[-1:]] for t in range(2)], axis=1)


def keep(ref, span, value):
    for t in range(2):
        ref[t, span, :] = value[:, 128 * t : 128 * t + 128]


def silu(x):
    h = 0.5 * x
    return h * jnp.tanh(h) + h


def swap_blocks(parts, low64, low32):
    left, right = [p[0] for p in parts], [p[1] for p in parts]
    m = [(left[i], left[i + 4]) for i in range(4)] + [(right[i], right[i + 4]) for i in range(4)]
    for bit, low, up, down in ((2, low64, 64, 64), (1, low32, 32, 96)):
        n = list(m)
        for j in range(8):
            if j & bit:
                continue
            a, b = m[j], m[j | bit]
            n[j] = tuple(jnp.where(low, a[t], pltpu.roll(b[t], up, 1)) for t in range(2))
            n[j | bit] = tuple(jnp.where(low, pltpu.roll(a[t], down, 1), b[t]) for t in range(2))
        m = n
    return m


def level_kernel(
    slots, chans, cells,
    counts_h, coords_h, neighbours_h, feat_h, fine_w_h, gain_h, bias_h, sel_h, swap_h, same_h,
    masks_h, down_h, up_h, weight_h,
    fine, coarse_out, sel_out, masks_out,
    counts, coords, neighbours, feat, fine_w, gain, bias, sel, swap, same, masks, down, up, weight,
    blocks, base, sig, sig2, acc, wts, gx, gyp, gym, gz, faces, halo, term,
    coarse, stats, window, everyone, pad, part, result,
    load, fsend, frecv, ssend, srecv, wsend, wrecv, rsend, rrecv, ready,
):
    n_mx, n_my = lax.axis_size("mx"), lax.axis_size("my")
    mx, my = lax.axis_index("mx"), lax.axis_index("my")
    n = n_mx * n_my
    me = mx * n_my + my
    width = 8 * chans
    side = width // 2
    wide_c = gain.shape[1]

    chunks = feat.shape[0]
    order = [
        ("counts", counts_h, counts), ("coords", coords_h, coords),
        ("neighbours", neighbours_h, neighbours), ("fine_w", fine_w_h, fine_w),
    ]
    order += [
        ("feat", feat_h.at[:, :, pl.ds(128 * k, 128)], feat.at[k]) for k in range(chunks)
    ]
    order += [("sel", sel_h, sel), ("masks", masks_h, masks), ("swap", swap_h, swap)]
    late = [("same", same_h, same), ("gain", gain_h, gain), ("bias", bias_h, bias)]
    late += [("down", down_h.at[:, pl.ds(128 * k, 128)], down.at[k]) for k in range(down.shape[0])]
    late += [("weight", weight_h, weight)]
    late += [("up", up_h.at[:, pl.ds(128 * k, 128)], up.at[k]) for k in range(up.shape[0])]
    copies = [
        (name, pltpu.make_async_copy(a, b, load.at[i]))
        for i, (name, a, b) in enumerate(order + late)
    ]
    for _, c in copies[: len(order)]:
        c.start()

    def loaded(*names):
        for name, c in copies:
            if name in names:
                c.wait()

    barrier = pltpu.get_barrier_semaphore()
    low, high = mx > 0, mx < n_mx - 1

    def greet(a, b):
        pl.semaphore_signal(barrier, inc=1, device_id=(a, b), device_id_type=MESH)

    @pl.when(low)
    def _():
        greet(mx - 1, my)

    @pl.when(high)
    def _():
        greet(mx + 1, my)

    for d in range(1, n_my):
        greet(mx, lax.rem(my + d, n_my))

    def entered():
        pl.semaphore_wait(barrier, n_my - 1 + low.astype(I32) + high.astype(I32))

    rounds = max(n_mx - 1, 0).bit_length()

    def tell(k):
        @pl.when(mx + 2**k < n_mx)
        def _():
            pl.semaphore_signal(
                ready.at[k, 0], inc=1, device_id=(mx + 2**k, my), device_id_type=MESH
            )

        @pl.when(mx - 2**k >= 0)
        def _():
            pl.semaphore_signal(
                ready.at[k, 1], inc=1, device_id=(mx - 2**k, my), device_id_type=MESH
            )

    def hear(k):
        @pl.when(mx - 2**k >= 0)
        def _():
            pl.semaphore_wait(ready.at[k, 0], 1)

        @pl.when(mx + 2**k < n_mx)
        def _():
            pl.semaphore_wait(ready.at[k, 1], 1)

    loaded("counts", "coords", "neighbours")
    def one_hot(row, count):
        return (lax.broadcasted_iota(I32, (count, slots), 0) == row).astype(F32).astype(BF)

    eye = (
        lax.broadcasted_iota(I32, (slots, slots), 0) == lax.broadcasted_iota(I32, (slots, slots), 1)
    ).astype(F32).astype(BF)

    def turned(table):
        return dot(eye, table, NT).astype(BF)

    pz = coords[0:1, :] - mx * RZ
    py = coords[1:2, :] - my * RY
    px = coords[2:3, :]
    live = lax.broadcasted_iota(I32, (1, slots), 1) < counts[...]

    def link(d):
        g = neighbours[d : d + 1, :]
        here = g - me * slots
        inside = (here >= 0) & (here < slots)
        far = slots + (pz if d < 4 else py) * RX + px
        return jnp.where(g < 0, -1, jnp.where(inside, here, far))

    halo_rows = slots + FACE
    g_x = turned(jnp.concatenate([one_hot(link(d), slots) for d in (0, 1)], axis=0))
    g_yp = turned(one_hot(link(2), halo_rows))
    g_ym = turned(one_hot(link(3), halo_rows))
    g_z = turned(jnp.concatenate([one_hot(link(d), halo_rows) for d in (4, 5)], axis=0))
    edge = (
        jnp.where(live & (py == 0), pz * RX + px, -1),
        jnp.where(live & (py == RY - 1), pz * RX + px, -1),
        jnp.where(live & (pz == 0), py * RX + px, -1),
        jnp.where(live & (pz == RZ - 1), py * RX + px, -1),
    )
    g_edge = [one_hot(e, FACE) for e in edge]
    cell = (pz // 2 * 2 + px // 2) * 2 + py // 2
    place = pz % 2 * 4 + py % 2 * 2 + px % 2
    g_cell = one_hot(jnp.where(live, place * cells + cell, -1), 8 * cells)
    g_lift = turned(g_cell)
    alive = dot(
        jnp.where(live, eye.astype(F32), 0.0).astype(BF), jnp.ones((slots, width), BF)
    ) > 0.5

    lane_block = lax.broadcasted_iota(I32, (slots, width), 1) // chans
    block_f = lane_block.astype(F32).astype(BF)
    spread = (
        lax.broadcasted_iota(I32, (chans, width), 0)
        == lax.broadcasted_iota(I32, (chans, width), 1) % chans
    ).astype(F32).astype(BF)
    none = jnp.zeros((chans, width), BF)
    is_block = [block_f == float(w) for w in range(8)]

    def fit(r, k, span, v):
        for t in range(2):
            wts[r, k, t, span, :] = v[:, side * t : side * t + side]

    def fill(r):
        t = dot(fine_w[r], spread, TN).astype(BF)
        t = [t[i * chans : (i + 1) * chans] for i in range(7)]
        for w in range(8):
            span = slice(w * chans, (w + 1) * chans)
            vy, vz, vx = w >> 2, w >> 1 & 1, w & 1
            v = jnp.where(is_block[w], t[0], none)
            v = jnp.where(is_block[w ^ 1], t[1] if vx else t[2], v)
            v = jnp.where(is_block[w ^ 4], t[3] if vy else t[4], v)
            v = jnp.where(is_block[w ^ 2], t[5] if vz else t[6], v)
            fit(r, 0, span, v)
            fit(r, 1, span, jnp.where(is_block[w ^ 1], t[2] if vx else t[1], none))
            fit(r, 2, span, jnp.where(is_block[w ^ 4], t[4] if vy else t[3], none))
            fit(r, 3, span, jnp.where(is_block[w ^ 2], t[6] if vz else t[5], none))

    loaded("fine_w")
    fill(0)

    loaded("feat", "sel", "masks")
    for _, c in copies[len(order) :]:
        c.start()

    def at_cube(q):
        return slice(q * slots, (q + 1) * slots)

    def rows(ref, q):
        return wide_of(ref, at_cube(q))

    def left(ref, q):
        return ref[0, at_cube(q), :]

    def right(ref, q):
        return ref[1, at_cube(q), :]

    def pair_of(ref):
        return jnp.concatenate([ref[0], ref[1]], axis=1)

    low64, low32 = masks[0] > 0.5, masks[1] > 0.5
    zero = jnp.zeros((slots, side), BF)

    for g in range(slots // 8):
        for h in range(2):
            x = jnp.concatenate(
                [feat[2 * h + t, 8 * g : 8 * g + 8].reshape(8 * chans, 128) for t in range(2)], axis=1
            )
            r = dot(pair_of(sel), x, NT).astype(BF)
            m = [(r[32 * w : 32 * w + 32, :side], r[32 * w : 32 * w + 32, side:]) for w in range(8)]
            m = swap_blocks(m, low64, low32)
            for s in range(8):
                at = (8 * g + s) * CUBES + 32 * h
                blocks[0, at : at + 32, :] = m[s][0]
                blocks[1, at : at + 32, :] = m[s][1]
    loaded("swap")
    for z in range(HALF):
        for g in range(slots // 16):
            x = jnp.concatenate(
                [wide_of(blocks, pl.ds((16 * g + s) * CUBES + 16 * z, 16)) for s in range(16)], axis=0)
            r = dot(pair_of(swap), x)
            rb = r.astype(BF)
            rs = silu(r).astype(BF)
            for i in range(16):
                at = (16 * z + i) * slots + 16 * g
                keep(base, slice(at, at + 16), rb[16 * i : 16 * i + 16])
                keep(sig, slice(at, at + 16), rs[16 * i : 16 * i + 16])

    peers = (
        (my > 0, mx, my - 1),
        (my < n_my - 1, mx, my + 1),
        (mx > 0, mx - 1, my),
        (mx < n_mx - 1, mx + 1, my),
    )

    def face_copy(r, f):
        _, a, b = peers[f]
        return pltpu.make_async_remote_copy(
            src_ref=faces.at[r, f], dst_ref=halo.at[r, f], send_sem=fsend.at[r, f],
            recv_sem=frecv.at[r, f], device_id=(a, b), device_id_type=MESH,
        )

    low64_face = low64[:FACE]

    def send_face(r, src, f):
        for k in range(PLANE // 2):
            a, x = k // 2, k % 2 * 2
            if f < 2:
                part_of = left if f == 0 else right
                q = a * PLANE + (0 if f == 0 else HALF - 1) * HALF + x
                pair = jnp.concatenate([part_of(src, q), part_of(src, q + 1)], axis=1)
                v = dot(g_edge[f], pair).astype(BF)
                faces[r, f, 2 * k] = v[:, :side]
                faces[r, f, 2 * k + 1] = v[:, side:]
            else:
                q = (0 if f == 2 else HALF - 1) * PLANE + a * HALF + x
                va = dot(g_edge[f], rows(src, q)).astype(BF)
                vb = dot(g_edge[f], rows(src, q + 1)).astype(BF)
                for t in range(2):
                    own = va[:, t * side : (t + 1) * side]
                    other = pltpu.roll(vb[:, t * side : (t + 1) * side], 64, 1)
                    if f == 2:
                        faces[r, f, 2 * k + t] = jnp.where(low64_face, own, other)
                    else:
                        faces[r, f, 2 * k + t] = jnp.where(low64_face, other, own)

        @pl.when(peers[f][0])
        def _():
            face_copy(r, f).start()

        @pl.when(jnp.logical_not(peers[f ^ 1][0]))
        def _():
            halo[r, f] = jnp.zeros_like(halo[r, f])

    def sent_faces(r):
        for f in range(4):
            @pl.when(peers[f][0])
            def _():
                face_copy(r, f).wait_send()

    def take_face(r, f):
        @pl.when(peers[f ^ 1][0])
        def _():
            face_copy(r, f).wait_recv()

    def z_halo(r, f, y, x):
        k = 2 * (y * 2 + x // 2)
        v = [halo[r, f, k + t] for t in range(2)]
        if x % 2:
            v = [pltpu.roll(a, 64, 1) for a in v]
        none = jnp.zeros_like(v[0])
        if f == 2:
            v = [jnp.where(low64_face, a, none) for a in v]
        else:
            v = [jnp.where(low64_face, none, a) for a in v]
        return jnp.concatenate(v, axis=1)

    def both(low, a, b):
        return jnp.concatenate([jnp.where(low, a[t], b[t]) for t in range(2)], axis=1)

    def halves(ref, q):
        return left(ref, q), right(ref, q)

    def run(ref, z, y):
        at = (z * HALF + y) * HALF * slots
        return wide_of(ref, slice(at, at + HALF * slots))

    def spans(runs):
        return [
            slice((z * HALF + y) * HALF * slots, (z * HALF + y + 1) * HALF * slots)
            for z, y in runs
        ]

    def stack(parts):
        return jnp.concatenate(parts, axis=0)

    def x_taps(src, runs):
        taps = []
        for z, y in runs:
            edge_of = halves(gx, z * HALF + y)
            for x in range(HALF):
                q = (z * HALF + y) * HALF + x
                after = halves(src, q + 1) if x < HALF - 1 else edge_of
                before = halves(src, q - 1) if x > 0 else edge_of
                taps.append(both(low32, after, before))
        return stack(taps)

    def y_taps(src, runs):
        taps = []
        for z, y in runs:
            for x in range(HALF):
                q = (z * HALF + y) * HALF + x
                zx = z * HALF + x
                span = slice(zx * slots, (zx + 1) * slots)
                after = left(src, q + HALF) if y < HALF - 1 else gyp[span, :]
                before = right(src, q - HALF) if y > 0 else gym[span, :]
                taps.append(jnp.concatenate([after, before], axis=1))
        return stack(taps)

    def z_taps(src, runs):
        taps = []
        for z, y in runs:
            for x in range(HALF):
                q = (z * HALF + y) * HALF + x
                edge_of = halves(gz, y * HALF + x)
                after = halves(src, q + PLANE) if z < HALF - 1 else edge_of
                before = halves(src, q - PLANE) if z > 0 else edge_of
                taps.append(both(low64, after, before))
        return stack(taps)

    def passes(r, src, runs, kinds):
        taps = {
            0: lambda: stack([run(src, z, y) for z, y in runs]),
            1: lambda: x_taps(src, runs),
            2: lambda: y_taps(src, runs),
            3: lambda: z_taps(src, runs),
        }
        total = None
        for k in kinds:
            v = dot(taps[k](), jnp.concatenate([wts[r, k, 0], wts[r, k, 1]], axis=1))
            total = v if total is None else total + v
        return total

    def add_to(ref, runs, value):
        tall = HALF * slots
        return [
            (span, wide_of(ref, span).astype(F32) + value[i * tall : (i + 1) * tall])
            for i, span in enumerate(spans(runs))
        ]

    inner, outer = range(1, HALF - 1), (0, HALF - 1)

    def near_inner(r, src, finish):
        for zy in range(PLANE):
            first, last = halves(src, zy * HALF), halves(src, zy * HALF + HALF - 1)
            pair = jnp.concatenate(
                [both(low32, first, (zero, zero)), both(low32, (zero, zero), last)], axis=0
            )
            keep(gx, at_cube(zy), dot(g_x, pair).astype(BF))
        for z in outer:
            runs = [(z, y) for y in inner]
            for span, v in add_to(base, runs, passes(r, src, runs, (0, 1, 2))):
                keep(acc, span, v)
        for z in inner:
            runs = [(z, y) for y in inner]
            for span, v in add_to(base, runs, passes(r, src, runs, (0, 1, 2, 3))):
                finish(span, v)

    def near_outer(r, src):
        for y in outer:
            for zs, kinds in ((inner, (0, 1, 3)), (outer, (0, 1))):
                runs = [(z, y) for z in zs]
                for span, v in add_to(base, runs, passes(r, src, runs, kinds)):
                    keep(acc, span, v)

    def gather_z(r, src):
        for f in (2, 3):
            take_face(r, f)
        for y in range(HALF):
            for x in range(HALF):
                i = y * HALF + x
                first, last = halves(src, i), halves(src, (HALF - 1) * PLANE + i)
                both_z = jnp.concatenate(
                    [both(low64, first, (zero, zero)), z_halo(r, 2, y, x),
                     both(low64, (zero, zero), last), z_halo(r, 3, y, x)], axis=0,
                )
                keep(gz, at_cube(i), dot(g_z, both_z).astype(BF))

    def gather_y(r, src, f):
        part_of, table, out = ((left, g_yp, gyp), (right, g_ym, gym))[f]
        for k in range(PLANE // 2):
            z, x = k // 2, k % 2 * 2
            q = z * PLANE + (0 if f == 0 else HALF - 1) * HALF + x
            own = jnp.concatenate([part_of(src, q), part_of(src, q + 1)], axis=1)
            got = jnp.concatenate([halo[r, f, 2 * k], halo[r, f, 2 * k + 1]], axis=1)
            v = dot(table, jnp.concatenate([own, got], axis=0)).astype(BF)
            out[2 * k * slots : (2 * k + 1) * slots, :] = v[:, :side]
            out[(2 * k + 1) * slots : (2 * k + 2) * slots, :] = v[:, side:]

    def more(r, src, runs, kind, finish=None):
        for span, v in add_to(acc, runs, passes(r, src, runs, (kind,))):
            if finish is None:
                keep(acc, span, v)
            else:
                finish(span, v)

    def far_z(r, src, finish):
        gather_z(r, src)
        for z in outer:
            more(r, src, [(z, y) for y in inner], 3, finish)
        for y in outer:
            more(r, src, [(z, y) for z in outer], 3)

    def far_y(r, src, finish, f):
        take_face(r, f)
        gather_y(r, src, f)
        y = HALF - 1 if f == 0 else 0
        for zs in (range(HALF // 2), range(HALF // 2, HALF)):
            more(r, src, [(z, y) for z in zs], 2, finish)

    def first_done(span, value):
        keep(base, span, value.astype(BF))

    entered()
    for f in (0, 1, 2, 3):
        send_face(0, sig, f)
    if rounds:
        tell(0)
    near_inner(0, sig, first_done)
    if rounds > 1:
        hear(0)
        tell(1)
    near_outer(0, sig)
    for k in range(2, rounds):
        hear(k - 1)
        tell(k)
    far_z(0, sig, first_done)
    far_y(0, sig, first_done, 1)
    far_y(0, sig, first_done, 0)

    sums = []
    for o in range(8):
        total = None
        for i in range(8):
            z, y, x = (o >> 2) * 2 + (i >> 2), (o >> 1 & 1) * 2 + (i >> 1 & 1), (o & 1) * 2 + (i & 1)
            v = rows(base, (z * HALF + y) * HALF + x).astype(F32)
            total = v if i == 0 else total + v
        hi = total.astype(BF)
        sums += [hi, (total - hi.astype(F32)).astype(BF)]
    loaded("same")
    sums = dot(jnp.concatenate(sums, axis=0), pair_of(same))
    pooled = jnp.zeros((slots, width), F32)
    for o in range(8):
        v = sums[2 * o * slots : (2 * o + 1) * slots] + sums[(2 * o + 1) * slots : (2 * o + 2) * slots]
        pooled = jnp.where(lane_block == o, v, pooled)
    pooled = (pooled * (1.0 / HALF**3)).astype(BF)
    flat = dot(g_cell, pooled).astype(BF)
    loaded("down")
    ci = jnp.zeros((cells, wide_c), F32)
    for p in range(8):
        ci = ci + jnp.dot(
            flat[p * cells : (p + 1) * cells],
            jnp.concatenate([down[t, p * width : (p + 1) * width, :] for t in range(down.shape[0])], axis=1),
            preferred_element_type=F32,
        )
    layer = cells // 2
    coarse[0] = ci[:layer]
    coarse[1] = ci[layer:]
    group = wide_c // GROUPS
    lanes = stats.shape[1]

    def split(v):
        a = v.astype(BF)
        rest = v - a.astype(F32)
        b = rest.astype(BF)
        return [a, b, (rest - b.astype(F32)).astype(BF)]

    def in_three(v, table, dims):
        parts = dot(jnp.concatenate([p.astype(F32) for p in split(v)], axis=0).astype(BF), table, dims)
        tall = v.shape[0]
        return parts[:tall] + (parts[tall : 2 * tall] + parts[2 * tall :])

    grouped = (
        lax.broadcasted_iota(I32, (wide_c, lanes), 0) // group
        == lax.broadcasted_iota(I32, (wide_c, lanes), 1)
    ).astype(F32).astype(BF)
    rest = jnp.zeros((6, wide_c), F32)
    local = jnp.concatenate(
        [jnp.sum(ci, axis=0, keepdims=True), jnp.sum(ci * ci, axis=0, keepdims=True), rest], axis=0
    )
    stats[...] = in_three(local, grouped, NN)[0:2]

    offsets = sorted(range(n_mx), key=lambda i: -min(i, n_mx - i))
    others = [(i, j) for i in offsets for j in range(n_my) if i or j]

    def stat_copy(i, j):
        d = i * n_my + j
        return pltpu.make_async_remote_copy(
            src_ref=stats, dst_ref=everyone.at[me], send_sem=ssend.at[d], recv_sem=srecv.at[d],
            device_id=(lax.rem(mx + i, n_mx), lax.rem(my + j, n_my)), device_id_type=MESH,
        )

    def win_copy(kind, d):
        t = lax.rem(my + d, n_my)
        if kind == 0:
            src, dst, a = coarse, window.at[my, pl.ds(1, 2)], mx
        elif kind == 1:
            src, dst, a = coarse.at[pl.ds(0, 1)], window.at[my, pl.ds(3, 1)], mx - 1
        else:
            src, dst, a = coarse.at[pl.ds(1, 1)], window.at[my, pl.ds(0, 1)], mx + 1
        return pltpu.make_async_remote_copy(
            src_ref=src, dst_ref=dst, send_sem=wsend.at[kind, d], recv_sem=wrecv.at[kind, d],
            device_id=(a, t), device_id_type=MESH,
        )

    if rounds:
        hear(rounds - 1)
    for i, j in others:
        stat_copy(i, j).start()
    for d in range(n_my):
        if d:
            win_copy(0, d).start()

        @pl.when(low)
        def _():
            win_copy(1, d).start()

        @pl.when(high)
        def _():
            win_copy(2, d).start()
    for f in range(2):
        send_face(1, base, f)
    window[my, 1:3] = coarse[...]
    everyone[me] = stats[...]

    @pl.when(jnp.logical_not(low))
    def _():
        for j in range(n_my):
            window[j, 0] = jnp.zeros_like(window[j, 0])

    @pl.when(jnp.logical_not(high))
    def _():
        for j in range(n_my):
            window[j, 3] = jnp.zeros_like(window[j, 3])

    pad[...] = jnp.zeros_like(pad)
    sel_out[...] = sel[...]
    masks_out[...] = masks[...]
    sent_faces(0)
    for r in (1, 2):
        fill(r)
    loaded("gain", "bias", "weight", "up")
    for d in range(n_my):
        if d:
            win_copy(0, d).wait()

        @pl.when(low)
        def _():
            win_copy(1, d).wait_send()
            win_copy(2, d).wait_recv()

        @pl.when(high)
        def _():
            win_copy(2, d).wait_send()
            win_copy(1, d).wait_recv()
    for i, j in others:
        stat_copy(i, j).wait()

    total = float(cells * group) * n
    sums = jnp.sum(everyone[...], axis=0) / total
    mean = sums[0:1]
    std = jnp.sqrt(sums[1:2] - mean * mean + norm_eps)
    both_rows = jnp.concatenate([mean, std, jnp.zeros((6, lanes), F32)], axis=0)
    both_rows = in_three(both_rows, grouped, NT)
    mean, std = both_rows[0:1], both_rows[1:2]
    scale = gain[...] / std
    shift = bias[...] - mean * scale
    for zw in range(4):
        for j in range(n_my):
            value = silu(window[j, zw] * scale + shift)
            if zw == 0:
                value = jnp.where(low, value, 0.0)
            if zw == 3:
                value = jnp.where(high, value, 0.0)
            for x in range(2):
                pad[1 + x, zw, 1 + 2 * j : 3 + 2 * j, :] = value[2 * x : 2 * x + 2]
    tall = 2 * n_my
    sums = jnp.zeros((4 * tall, part.shape[2]), F32)
    t = 0
    for dz in range(3):
        for dy in range(3):
            for dx in range(3):
                lhs = jnp.concatenate(
                    [pad[x + dx, z + dz, dy : dy + tall, :] for z in range(2) for x in range(2)],
                    axis=0,
                ).astype(BF)
                sums = sums + lax.dot_general(
                    lhs, weight[:, t * wide_c : (t + 1) * wide_c], (((1,), (1,)), ((), ())),
                    preferred_element_type=F32,
                )
                t += 1
    for j in range(n_my):
        for zx in range(4):
            part[j, 2 * zx : 2 * zx + 2, :] = sums[zx * tall + 2 * j : zx * tall + 2 * j + 2, :]
            above, below = zx * tall + 2 * min(j + 1, n_my - 1), zx * tall + 2 * max(j - 1, 0) + 1
            part[j, cells + zx : cells + zx + 1, :] = sums[above : above + 1, :]
            part[j, cells + 4 + zx : cells + 5 + zx, :] = sums[below : below + 1, :]
    copies = []
    for d in range(1, n_my):
        to = lax.rem(my + d, n_my)
        copies.append(
            pltpu.make_async_remote_copy(
                src_ref=part.at[to], dst_ref=result.at[my], send_sem=rsend.at[d],
                recv_sem=rrecv.at[d], device_id=(mx, to), device_id_type=MESH,
            )
        )
    for c in copies:
        c.start()
    result[my] = part[my]
    for c in copies:
        c.wait()

    whole = jnp.concatenate([result[j] for j in range(n_my)], axis=1)
    above, below = jnp.minimum(my + 1, n_my - 1), jnp.maximum(my - 1, 0)
    beside = [window[above, 1], window[above, 2], window[below, 1], window[below, 2]]
    beside = [
        v[r : r + 1] for i, v in enumerate(beside) for r in ((0, 2) if i < 2 else (1, 3))
    ]
    co = (whole + jnp.concatenate([coarse[0], coarse[1]] + beside, axis=0)).astype(BF)
    cof = co.astype(F32)
    for z in range(2):
        for y in range(2):
            q = z * 4 + y
            pair = jnp.concatenate([cof[q : q + 1], cof[q + 2 : q + 3]], axis=0)
            coarse_out[z, y] = pair.astype(BF)
    wide = dot(co, jnp.concatenate([up[k] for k in range(up.shape[0])], axis=1))
    def in_two(v):
        hi = v.astype(BF)
        return hi, (v - hi.astype(F32)).astype(BF)

    def lifted(at):
        return jnp.concatenate(
            [wide[at : at + cells, p * width : (p + 1) * width] for p in range(8)], axis=0
        )

    picked = [dot(g_lift, v).astype(BF) for v in in_two(lifted(0))]
    spots = [jnp.where(is_block[o], v, jnp.zeros_like(v)) for o in range(8) for v in picked]

    k = lax.broadcasted_iota(I32, (2 * FACE, 8 * cells), 0)
    down_side = k // FACE
    kz, kx = k % FACE // RX, k % RX
    row = (kz % 2 * 4 + down_side * 2 + kx % 2) * cells + down_side * 4 + kz // 2 * 2 + kx // 2
    g_halo = (lax.broadcasted_iota(I32, (2 * FACE, 8 * cells), 1) == row).astype(F32).astype(BF)
    picked = [dot(g_halo, v).astype(BF) for v in in_two(lifted(cells))]
    for zx in range(4):
        for v in picked:
            for f in range(2):
                o = zx // 2 * 4 + f * 2 + zx % 2
                v_f = v[f * FACE : (f + 1) * FACE]
                spots.append(jnp.where(is_block[o][:FACE], v_f, jnp.zeros_like(v_f)))
    sums = dot(jnp.concatenate(spots, axis=0), pair_of(same))
    for o in range(8):
        v = sums[2 * o * slots : (2 * o + 1) * slots] + sums[(2 * o + 1) * slots : (2 * o + 2) * slots]
        term[o * slots : (o + 1) * slots, :] = v

    def join(z, y):
        for x in range(HALF):
            q = (z * HALF + y) * HALF + x
            o = z // 2 * 4 + y // 2 * 2 + x // 2
            span = slice(q * slots, (q + 1) * slots)
            f = (wide_of(base, span).astype(F32) + term[o * slots : (o + 1) * slots, :]).astype(BF)
            keep(base, span, f)
            keep(sig, span, silu(f.astype(F32)).astype(BF))

    for f, z in ((2, 0), (3, HALF - 1)):
        for y in range(HALF):
            join(z, y)
        send_face(1, sig, f)
    for z in inner:
        for y in range(HALF):
            join(z, y)
    for f in range(2):
        take_face(1, f)
        for zx in range(PLANE):
            at = 16 * slots + (zx // 8 * 2 + zx % 4 // 2) * 4 * FACE + f * FACE
            lift = sums[at : at + FACE, :side] + sums[at + 2 * FACE : at + 3 * FACE, :side]
            v = (halo[1, f, zx].astype(F32) + lift).astype(BF)
            halo[1, f, zx] = silu(v.astype(F32)).astype(BF)

    def second_done(span, value):
        f = value.astype(BF)
        keep(base, span, f)
        keep(sig2, span, silu(f.astype(F32)).astype(BF))

    near_inner(1, sig, second_done)
    near_outer(1, sig)
    for f, y in ((1, 0), (0, HALF - 1)):
        gather_y(1, sig, f)
        more(1, sig, [(z, y) for z in inner], 2, second_done)
        more(1, sig, [(z, y) for z in outer], 2)
    gather_z(1, sig)
    for f, y in ((0, 0), (1, HALF - 1)):
        more(1, sig, [(z, y) for z in outer], 3, second_done)
        send_face(2, sig2, f)
    for f, z in ((2, 0), (3, HALF - 1)):
        more(1, sig, [(z, y) for y in inner], 3, second_done)
        send_face(2, sig2, f)

    def last_done(span, value):
        for i in range(HALF):
            at = slice(span.start + i * slots, span.start + (i + 1) * slots)
            keep(base, at, jnp.where(alive, value[i * slots : (i + 1) * slots], 0.0).astype(BF))

    near_inner(2, sig2, last_done)
    near_outer(2, sig2)
    far_z(2, sig2, last_done)
    sent_faces(1)
    for f in (1, 0):
        far_y(2, sig2, last_done, f)

    sent_faces(2)
    for g in range(slots // 16):
        for z in range(HALF):
            x = jnp.concatenate(
                [wide_of(base, pl.ds((16 * z + i) * slots + 16 * g, 16)) for i in range(16)], axis=0)
            r = dot(pair_of(swap), x).astype(BF)
            for s in range(16):
                at = (16 * g + s) * CUBES + 16 * z
                keep(fine, slice(at, at + 16), r[16 * s : 16 * s + 16])


def unfold_kernel(chans, slots, rows, coarse, sel, masks, fine_h, coarse_h, fine, kept, sem):
    kept[...] = coarse[...]
    stores = [pltpu.make_async_copy(kept, coarse_h, sem.at[0])]
    stores[0].start()
    low64, low32 = masks[0] > 0.5, masks[1] > 0.5
    for g in range(slots // 8):
        for h in range(2):
            m = []
            for s in range(8):
                at = (8 * g + s) * CUBES + 32 * h
                m.append((rows[0, at : at + 32, :], rows[1, at : at + 32, :]))
            m = swap_blocks(m, low64, low32)
            x = jnp.concatenate([jnp.concatenate(p, axis=1) for p in m], axis=0)
            r = dot(x.T, jnp.concatenate([sel[0], sel[1]], axis=1)).astype(BF)
            fine[8 * g : 8 * g + 8, :, 256 * h : 256 * h + 256] = r.reshape(8, chans, 256)
        part = pl.ds(8 * g, 8)
        stores.append(pltpu.make_async_copy(fine.at[part], fine_h.at[part], sem.at[1 + g]))
        stores[-1].start()
    for c in stores:
        c.wait()


def local(
    features, coords, counts, neighbours, fine_weights, down_weight, up_weight, norm_gain,
    norm_bias, coarse_weight,
):
    slots, chans, _ = features.shape
    n_mx, n_my = lax.axis_size("mx"), lax.axis_size("my")
    cells = (RZ // 2) * (RY // 2) * (RX // 2)
    width = down_weight.shape[1]
    lanes = 8 * chans
    masks, sel, swap, same = constants(chans)
    n = n_mx * n_my
    sds = jax.ShapeDtypeStruct
    weight_t = coarse_weight.T
    ins = (
        counts[None, :], coords, neighbours, features, fine_weights, norm_gain[None, :],
        norm_bias[None, :], sel, swap, same, masks, down_weight, up_weight, weight_t,
    )
    held = [pltpu.VMEM(a.shape, a.dtype) for a in ins]
    held[3] = pltpu.VMEM((SIDE**3 // 128, slots, chans, 128), BF)
    held[11] = pltpu.VMEM((width // 128, down_weight.shape[0], 128), BF)
    held[12] = pltpu.VMEM((up_weight.shape[1] // 128, width, 128), BF)
    dma = pltpu.SemaphoreType.DMA
    total = slots * CUBES
    plane = slots * PLANE
    scratch = held + [
        pltpu.VMEM((2, total, 128), BF),
        pltpu.VMEM((2, total, 128), BF),
        pltpu.VMEM((2, total, 128), BF),
        pltpu.VMEM((2, total, 128), BF),
        pltpu.VMEM((2, total, 128), F32),
        pltpu.VMEM((3, 4, 2, lanes, 128), BF),
        pltpu.VMEM((2, plane, 128), BF),
        pltpu.VMEM((plane, lanes // 2), BF),
        pltpu.VMEM((plane, lanes // 2), BF),
        pltpu.VMEM((2, plane, 128), BF),
        pltpu.VMEM((3, 4, PLANE, FACE, lanes // 2), BF),
        pltpu.VMEM((3, 4, PLANE, FACE, lanes // 2), BF),
        pltpu.VMEM((8 * slots, lanes), F32),
        pltpu.VMEM((2, cells // 2, width), F32),
        pltpu.VMEM((2, 128), F32),
        pltpu.VMEM((n_my, 4, cells // 2, width), F32),
        pltpu.VMEM((n, 2, 128), F32),
        pltpu.VMEM((4, 4, -(-(2 * n_my + 2) // 8) * 8, width), F32),
        pltpu.VMEM((n_my, 2 * cells, coarse_weight.shape[1]), F32),
        pltpu.VMEM((n_my, 2 * cells, coarse_weight.shape[1]), F32),
        dma((64,)), dma((3, 4)), dma((3, 4)), dma((n,)), dma((n,)),
        dma((3, n_my)), dma((3, n_my)), dma((n_my,)), dma((n_my,)),
        pltpu.SemaphoreType.REGULAR((max(1, (n_mx - 1).bit_length()), 2)),
    ]
    small = (RZ // 2, RY // 2, RX // 2, width)
    held_on = pl.pallas_call(
        functools.partial(level_kernel, slots, chans, cells),
        out_shape=(
            pltpu.VMEM((2, total, 128), BF), pltpu.VMEM(small, BF),
            pltpu.VMEM(sel.shape, BF), pltpu.VMEM(masks.shape, BF),
        ),
        in_specs=[HBM] * len(ins),
        out_specs=(VM,) * 4,
        scratch_shapes=scratch,
        compiler_params=pltpu.CompilerParams(collective_id=0, has_side_effects=True),
    )(*ins)
    return pl.pallas_call(
        functools.partial(unfold_kernel, chans, slots),
        out_shape=(sds(features.shape, BF), sds(small, BF)),
        in_specs=[VM] * 4,
        out_specs=(HBM, HBM),
        scratch_shapes=[
            pltpu.VMEM(features.shape, BF), pltpu.VMEM(small, BF), dma((1 + slots // 8,)),
        ],
    )(*[pltpu.with_memory_space_constraint(a, pltpu.VMEM) for a in held_on])


def solution(mesh):
    in_specs = (
        P(("mx", "my"), None, None),
        P(None, ("mx", "my")),
        P(("mx", "my")),
        P(None, ("mx", "my")),
        P(),
        P(),
        P(),
        P(),
        P(),
        P(None, "my"),
    )
    out_specs = (P(("mx", "my"), None, None), P("mx", "my", None, None))
    return jax.shard_map(local, mesh=mesh, in_specs=in_specs, out_specs=out_specs, check_vma=False)
```
